32 devices in a mesh: pipe: 4 (over x, core), dp: 8 (over z, y).
Axes of the slice: x: 2, y: 2, z: 4, core: 2. Of those that a mesh axis runs over, the one named last changes fastest.
Arguments:
- section_input: bfloat16 [4, 2048, 2048], P('pipe', 'dp'), may hold values from -6 to 6
- top_grad: bfloat16 [2048, 2048], P('dp'), may hold values from -6 to 6
- w_in: bfloat16 [4, 2048, 3072], P('pipe', 'dp'), may hold values from -0.125 to 0.125
- w_out: bfloat16 [4, 1024, 2048], P('pipe', 'dp'), may hold values from -0.1875 to 0.1875
- segments: int32 [16, 128], P('dp'), may hold values from 0 to 3, never falling along the last dimension, each value on 1 to 64 neighbouring positions
Outputs:
- section_grads: bfloat16 [4, 2048, 2048], P('pipe', 'dp')
- w_in_grad: float32 [4, 2048, 3072], P('pipe', 'dp')
- w_out_grad: float32 [4, 1024, 2048], P('pipe', 'dp')
The draws below stay inside these ranges and needn't reach their ends.
Inputs may be any that keep to these rules, and one draw needn't show every extreme that they name: `segments`: in every row the history numbers run 0 to 3 without falling, each history has 1 to 64 positions, and one has exactly 64.
All inputs are finite; a program needn't handle non-finite values.
Results may differ from the reference program's by a relative error of at most 0.03.
Values may be sent and summed in bfloat16 or wider, within the bound.
A program may use at most 128 MiB of HBM per device.

```python
import math
import jax
import jax.numpy as jnp
import numpy as np
from jax import lax

D = 2048
HEADS = 16
QK_DIM = 32
V_DIM = 64
HV = 1024
F1 = 3072
TOK_MB = 128
MICRO = 2
SEGS = 4
SEG_MOST = 64
SECTIONS = 4
TOKENS = 2048
MB_ROWS = 16
N_PIPE = 4
N_DP = 8


def spiked(array, own_key, source, target, shards_of, factor):
    owner, partner = [(jnp.arange(array.shape[dim]) // (array.shape[dim] // shards_of)).reshape([-1 if axis == dim else 1 for axis in range(array.ndim)]) for dim in (source, target)]
    chosen = jax.random.permutation(own_key, shards_of)[partner]
    strong = (owner == chosen) | (owner == (partner + shards_of // 2) % shards_of)
    return jnp.where(strong, factor * array, array)


def levels(rng, dims, split, smallest, largest):
    def one(dim, shards_of):
        heights = jax.random.uniform(jax.random.fold_in(jax.random.fold_in(rng, 6), dim), (shards_of,), jnp.float32, smallest / len(split), largest / len(split))
        return jnp.repeat(jnp.exp(heights), dims[dim] // shards_of).reshape((-1,) + (1,) * (len(dims) - dim - 1))

    loudness = one(*split[0])
    for cut in split[1:]:
        loudness = loudness * one(*cut)
    return loudness


def profile(count, total, reach, skew):
    loads = [(1 << 20) // math.isqrt(standing ** skew) + 1 for standing in range(2, count + 1)]
    spare, given = total - reach - (count - 1), [1] * (count - 1)
    while spare > 0:
        free = [i for i in range(count - 1) if given[i] < reach]
        mass, left = sum([loads[i] for i in free]), spare
        for i in free:
            extra = min(reach - given[i], max(1, left * loads[i] // mass), spare)
            given[i] = given[i] + extra
            spare = spare - extra
    return np.array([reach] + given)


def ragged_sizes(stream_key, amount, total, bound, lean):
    if amount == 2:
        one = jax.random.randint(stream_key, (), max(1, total - bound), min(bound, total - 1) + 1)
        return jnp.stack([one, total - one])
    tallies = jnp.asarray(profile(amount, total, bound, lean), jnp.int32)
    twos = (amount - 1) // 2
    giver, receiver = tallies[1:1 + 2 * twos:2], tallies[2:2 + 2 * twos:2]
    room = jnp.minimum(giver - 1, bound - receiver)
    moved = jax.random.randint(jax.random.fold_in(stream_key, 1), (twos,), 0, 1 << 20) % (room + 1)
    tallies = tallies.at[1:1 + 2 * twos:2].set(giver - moved).at[2:2 + 2 * twos:2].set(receiver + moved)
    return tallies[jax.random.permutation(jax.random.fold_in(stream_key, 2), amount)]


def gaussian(rng, dims, width, most, cuts=(), kind=jnp.bfloat16):
    gain = levels(rng, dims, cuts, -0.22, 0.18) if cuts else 1.0
    array = jax.random.normal(rng, dims, jnp.float32) * width * gain
    return jnp.minimum(jnp.maximum(array, -most), most).astype(kind)


def heavy_noise(own_key, shape, spread, reach, cuts, heavy, kind=jnp.bfloat16):
    values = spread * jax.random.normal(own_key, shape, jnp.float32)
    if cuts:
        values = values * levels(own_key, shape, cuts, -0.22, 0.18)
    return jnp.clip(spiked(values, jax.random.fold_in(own_key, 3), *heavy), -reach, reach).astype(kind)


def setup_inputs(seed: int = 0) -> dict:
    seeds = jax.random.split(jax.random.key(seed), 6)
    section_input = heavy_noise(seeds[0], (SECTIONS, TOKENS, D), 1.0, 6.0, ((0, 4), (1, 8)), (1, 2, 8, 2.0))
    top_grad = gaussian(seeds[1], (TOKENS, D), 1.0, 6.0, ((0, 8),))
    w_in = gaussian(seeds[2], (SECTIONS, D, F1), D ** -0.5, 0.125, ((0, 4), (1, 8)))
    w_out = gaussian(seeds[3], (SECTIONS, HV, D), HV ** -0.5, 0.1875, ((0, 4), (1, 8)))
    segments = jax.vmap(lambda own: jnp.searchsorted(jnp.cumsum(ragged_sizes(own, SEGS, TOK_MB, SEG_MOST, 2)), jnp.arange(TOK_MB), side="right"))(jax.random.split(seeds[4], MB_ROWS)).reshape((MB_ROWS, TOK_MB)).astype(jnp.int32)
    return {"section_input": section_input, "top_grad": top_grad, "w_in": w_in, "w_out": w_out, "segments": segments}


EPSILON = 1e-05

def norm_rows(values):
    center = values - lax.optimization_barrier(jnp.mean(values, axis=-1, keepdims=True))
    return center * lax.rsqrt(lax.optimization_barrier(jnp.mean(center * center, axis=-1, keepdims=True)) + EPSILON)

def silu_slope(preact):
    squash = jax.nn.sigmoid(preact)
    return squash * (1.0 + preact * (1.0 - squash))

def contract_rows(left, right):
    return lax.dot_general(left, right, (((0,), (0,)), ((), ())), preferred_element_type=jnp.float32)

def forward_front(inputs, w_first):
    normed = norm_rows(inputs.astype(jnp.float32)).astype(jnp.bfloat16)
    preact = jnp.dot(normed, w_first, preferred_element_type=jnp.float32)
    return (normed, preact, jax.nn.silu(preact).astype(jnp.bfloat16))

def attend(activated, history):
    row_count = activated.shape[0]
    value_cols = HEADS * V_DIM
    query_cols = HEADS * QK_DIM
    active32 = activated.astype(jnp.float32)
    gating = active32[:, :value_cols]
    values = active32[:, value_cols:2 * value_cols].reshape(row_count, HEADS, V_DIM)
    queries = active32[:, 2 * value_cols:2 * value_cols + query_cols].reshape(row_count, HEADS, QK_DIM)
    key_rows = active32[:, 2 * value_cols + query_cols:].reshape(row_count, HEADS, QK_DIM)
    scores = jnp.einsum('qhd,khd->hqk', queries, key_rows) * QK_DIM ** (-0.5)
    same_doc = history[:, None] == history[None, :]
    positions = lax.broadcasted_iota(jnp.int32, (row_count, row_count), 0)
    columns = lax.broadcasted_iota(jnp.int32, (row_count, row_count), 1)
    allowed = jnp.logical_and(same_doc, columns <= positions)
    counts = lax.optimization_barrier(jnp.sum(same_doc.astype(jnp.float32), axis=1))
    weights_mask = allowed.astype(jnp.float32) / counts[:, None]
    weights = jax.nn.silu(scores) * weights_mask[None]
    mixed = jnp.einsum('hqk,khd->qhd', weights, values).reshape(row_count, value_cols)
    return norm_rows(mixed) * gating

def layer_back(inputs, normed, preact, activated, upstream, history, w_first, w_second):
    gated_full, pull = jax.vjp(lambda active_in: attend(active_in, history), activated)
    gated = gated_full.astype(jnp.bfloat16)
    grad_second = contract_rows(gated, upstream)
    grad_gated = lax.dot_general(upstream, w_second, (((1,), (1,)), ((), ())), preferred_element_type=jnp.float32)
    grad_active, = pull(grad_gated)
    grad_preact = (grad_active.astype(jnp.float32) * silu_slope(preact)).astype(jnp.bfloat16)
    grad_normed = lax.dot_general(grad_preact, w_first, (((1,), (1,)), ((), ())), preferred_element_type=jnp.float32)
    _, pull_norm = jax.vjp(norm_rows, inputs.astype(jnp.float32))
    grad_through, = pull_norm(grad_normed)
    grad_input = (upstream.astype(jnp.float32) + grad_through).astype(jnp.bfloat16)
    return (grad_input, grad_preact, grad_second)

def reference(section_input, top_grad, w_in, w_out, segments):
    upstream_all = top_grad
    section_list = []
    first_list = []
    second_list = []
    for section in range(N_PIPE - 1, -1, -1):
        inputs_all = section_input[section]
        w_first = w_in[section]
        w_second = w_out[section]
        upstream_now = upstream_all

        def device_step(carry, device):
            total_in, total_out = carry
            acc_in = jnp.zeros((D, F1), jnp.float32)
            acc_out = jnp.zeros((HV, D), jnp.float32)
            pieces = []
            for micro_index in range(MICRO):
                block = (device * MICRO + micro_index).astype(jnp.int32)
                start = (block * TOK_MB).astype(jnp.int32)
                inputs = lax.dynamic_slice_in_dim(inputs_all, start, TOK_MB, 0)
                upstream = lax.dynamic_slice_in_dim(upstream_now, start, TOK_MB, 0)
                history = lax.dynamic_index_in_dim(segments, block, 0, keepdims=False)
                normed, preact, activated = forward_front(inputs, w_first)
                grad_input, grad_preact, grad_second = layer_back(inputs, normed, preact, activated, upstream, history, w_first, w_second)
                acc_in = acc_in + contract_rows(normed, grad_preact)
                acc_out = acc_out + grad_second
                pieces.append(grad_input)
            total_in = total_in + lax.optimization_barrier(acc_in.astype(jnp.bfloat16)).astype(jnp.float32)
            total_out = total_out + lax.optimization_barrier(acc_out.astype(jnp.bfloat16)).astype(jnp.float32)
            return ((total_in, total_out), jnp.concatenate(pieces, axis=0))
        start_sums = (jnp.zeros((D, F1), jnp.float32), jnp.zeros((HV, D), jnp.float32))
        (total_in, total_out), grad_blocks = lax.scan(device_step, start_sums, jnp.arange(N_DP, dtype=jnp.int32))
        upstream_all = grad_blocks.reshape(TOKENS, D)
        section_list.insert(0, upstream_all)
        first_list.insert(0, total_in)
        second_list.insert(0, total_out)
    return (jnp.stack(section_list), jnp.stack(first_list), jnp.stack(second_list))
```

```python
import functools

import jax
import jax.numpy as jnp
from jax import lax
from jax.experimental import pallas as pl
from jax.experimental.pallas import tpu as pltpu
from jax.sharding import PartitionSpec as P

HEADS = 16
QK_DIM = 32
V_DIM = 64
LANES = 128

EPSILON = 1e-05
MESH = pl.DeviceIdType.MESH
VMEM = pl.BlockSpec(memory_space=pltpu.VMEM)

QK_HEADS = LANES // QK_DIM
V_HEADS = LANES // V_DIM
GROUPS = HEADS // QK_HEADS
V_COLS = HEADS * V_DIM
Q_COLS = HEADS * QK_DIM
GROUP_V = QK_HEADS * V_DIM
SCALE = QK_DIM ** (-0.5)


def norm_rows(values):
    center = values - jnp.mean(values, axis=-1, keepdims=True)
    return center * lax.rsqrt(jnp.mean(center * center, axis=-1, keepdims=True) + EPSILON)


def silu_slope(preact):
    squash = jax.nn.sigmoid(preact)
    return squash * (1.0 + preact * (1.0 - squash))


def dot_nt(left, right):
    return lax.dot_general(
        left, right, (((1,), (1,)), ((), ())), preferred_element_type=jnp.float32
    )


def dot_nn(left, right):
    return lax.dot_general(
        left, right, (((1,), (0,)), ((), ())), preferred_element_type=jnp.float32
    )


def contract_rows(left, right):
    return lax.dot_general(
        left, right, (((0,), (0,)), ((), ())), preferred_element_type=jnp.float32
    )


def only_head(block, lane, width, index):
    keep = jnp.logical_and(lane >= index * width, lane < (index + 1) * width)
    return jnp.where(keep, block, jnp.zeros_like(block))


def at(start, size):
    return pl.ds(pl.multiple_of(start, LANES), size)


def attend_kernel(micro, length, act_ref, mask_ref, score_ref, unit_ref, rstd_ref, gated_ref, mixed):
    lane = lax.broadcasted_iota(jnp.int32, (length, LANES), 1)

    def one(index, _):
        slot, group = index // GROUPS, index % GROUPS
        rows = at(slot * length, length)
        queries = act_ref[rows, at(2 * V_COLS + group * LANES, LANES)]
        keys = act_ref[rows, at(2 * V_COLS + Q_COLS + group * LANES, LANES)]
        mask = mask_ref[rows, :]
        for half in range(GROUP_V // LANES):
            cols = group * GROUP_V + half * LANES
            values = act_ref[rows, at(V_COLS + cols, LANES)]
            total = jnp.zeros((length, LANES), jnp.float32)
            for sub in range(V_HEADS):
                head = half * V_HEADS + sub
                score = dot_nt(only_head(queries, lane, QK_DIM, head), keys) * SCALE
                score_ref[at((index * QK_HEADS + head) * length, length), :] = score
                weight = (jax.nn.silu(score) * mask).astype(jnp.bfloat16)
                total += dot_nn(weight, only_head(values, lane, V_DIM, sub))
            mixed[rows, at(cols, LANES)] = total
        return 0

    lax.fori_loop(0, micro * GROUPS, one, 0)

    def finish(slot, _):
        rows = at(slot * length, length)
        value = mixed[rows, :]
        center = value - jnp.mean(value, axis=-1, keepdims=True)
        rstd = lax.rsqrt(jnp.mean(center * center, axis=-1, keepdims=True) + EPSILON)
        unit = center * rstd
        unit_ref[rows, :] = unit
        rstd_ref[rows, :] = jnp.broadcast_to(rstd, (length, LANES))
        gated_ref[rows, :] = (unit * act_ref[rows, :V_COLS].astype(jnp.float32)).astype(jnp.bfloat16)
        return 0

    lax.fori_loop(0, micro, finish, 0)


def attend(activated, mask, micro, length):
    tokens = micro * length
    return pl.pallas_call(
        functools.partial(attend_kernel, micro, length),
        out_shape=(
            jax.ShapeDtypeStruct((micro * HEADS * length, length), jnp.float32),
            jax.ShapeDtypeStruct((tokens, V_COLS), jnp.float32),
            jax.ShapeDtypeStruct((tokens, LANES), jnp.float32),
            jax.ShapeDtypeStruct((tokens, V_COLS), jnp.bfloat16),
        ),
        in_specs=[VMEM] * 2,
        out_specs=(VMEM,) * 4,
        scratch_shapes=[pltpu.VMEM((tokens, V_COLS), jnp.float32)],
        name="attend",
    )(activated, mask)


def chain_kernel(
    micro, length, sections,
    top_ref, input_ref, act_ref, pre_ref, score_ref, unit_ref, rstd_ref, mask_ref, first_ref, second_ref,
    up_ref, gpre_ref, gin_ref,
    landed, leaving, ggate, dmix, gnorm, send_sem, recv_sem,
):
    section = lax.axis_index("pipe")
    width = input_ref.shape[1]
    tile = 2 * LANES
    lane = lax.broadcasted_iota(jnp.int32, (length, LANES), 1)
    is_last = section == sections - 1
    is_first = section == 0

    barrier = pltpu.get_barrier_semaphore()

    @pl.when(jnp.logical_not(is_last))
    def _():
        pl.semaphore_signal(
            barrier, inc=1, device_id={"pipe": jnp.minimum(section + 1, sections - 1)}, device_id_type=MESH
        )

    @pl.when(jnp.logical_not(is_first))
    def _():
        pl.semaphore_wait(barrier, 1)

    def copy_of(slot):
        return pltpu.make_async_remote_copy(
            src_ref=leaving.at[slot],
            dst_ref=landed.at[slot],
            send_sem=send_sem.at[slot],
            recv_sem=recv_sem.at[slot],
            device_id={"pipe": jnp.maximum(section - 1, 0)},
            device_id_type=MESH,
        )

    def store_grad(rows, cols, size, value):
        rounded = value.astype(jnp.bfloat16).astype(jnp.float32)
        gpre_ref[rows, at(cols, size)] = (
            rounded * silu_slope(pre_ref[rows, at(cols, size)])
        ).astype(jnp.bfloat16)

    for slot in range(micro):
        rows = pl.ds(slot * length, length)

        @pl.when(is_last)
        def _():
            up_ref[rows, :] = top_ref[rows, :]

        @pl.when(jnp.logical_not(is_last))
        def _():
            copy_of(slot).wait_recv()
            up_ref[rows, :] = landed[slot]

        def gate_tile(index, _):
            ggate[:, at(index * tile, tile)] = dot_nt(up_ref[rows, :], second_ref[at(index * tile, tile), :])
            return 0

        lax.fori_loop(0, V_COLS // tile, gate_tile, 0)
        gating = act_ref[rows, :V_COLS].astype(jnp.float32)
        unit = unit_ref[rows, :]
        grad = ggate[...]
        store_grad(rows, 0, V_COLS, grad * unit)
        grad = grad * gating
        mean_grad = jnp.mean(grad, axis=-1, keepdims=True)
        mean_unit = jnp.mean(grad * unit, axis=-1, keepdims=True)
        dmix[...] = (rstd_ref[rows, :1] * (grad - mean_grad - unit * mean_unit)).astype(jnp.bfloat16)

        def one(group, _):
            queries = act_ref[rows, at(2 * V_COLS + group * LANES, LANES)]
            keys = act_ref[rows, at(2 * V_COLS + Q_COLS + group * LANES, LANES)]
            mask = mask_ref[rows, :]
            grad_q = jnp.zeros((length, LANES), jnp.float32)
            grad_k = jnp.zeros((length, LANES), jnp.float32)
            for half in range(GROUP_V // LANES):
                cols = group * GROUP_V + half * LANES
                values = act_ref[rows, at(V_COLS + cols, LANES)]
                grad_mix = dmix[:, at(cols, LANES)]
                grad_v = jnp.zeros((length, LANES), jnp.float32)
                for sub in range(V_HEADS):
                    head = half * V_HEADS + sub
                    mix_head = only_head(grad_mix, lane, V_DIM, sub)
                    place = (slot * HEADS + group * QK_HEADS + head) * length
                    score = score_ref[at(place, length), :]
                    squash = jax.nn.sigmoid(score)
                    weight = (score * squash * mask).astype(jnp.bfloat16)
                    slope = squash * (1.0 + score * (1.0 - squash)) * mask * SCALE
                    grad_score = (dot_nt(mix_head, values) * slope).astype(jnp.bfloat16)
                    grad_v += contract_rows(weight, mix_head)
                    grad_q += dot_nn(grad_score, only_head(keys, lane, QK_DIM, head))
                    grad_k += contract_rows(grad_score, only_head(queries, lane, QK_DIM, head))
                store_grad(rows, V_COLS + cols, LANES, grad_v)
            store_grad(rows, 2 * V_COLS + group * LANES, LANES, grad_q)
            store_grad(rows, 2 * V_COLS + Q_COLS + group * LANES, LANES, grad_k)
            return 0

        lax.fori_loop(0, GROUPS, one, 0)

        def norm_tile(index, _):
            gnorm[:, at(index * tile, tile)] = dot_nt(gpre_ref[rows, :], first_ref[at(index * tile, tile), :])
            return 0

        lax.fori_loop(0, width // tile, norm_tile, 0)
        value = input_ref[rows, :].astype(jnp.float32)
        center = value - jnp.mean(value, axis=-1, keepdims=True)
        rstd = lax.rsqrt(jnp.mean(center * center, axis=-1, keepdims=True) + EPSILON)
        unit = center * rstd
        grad = gnorm[...]
        mean_grad = jnp.mean(grad, axis=-1, keepdims=True)
        mean_unit = jnp.mean(grad * unit, axis=-1, keepdims=True)
        through = rstd * (grad - mean_grad - unit * mean_unit)
        result = (up_ref[rows, :].astype(jnp.float32) + through).astype(jnp.bfloat16)
        leaving[slot] = result
        gin_ref[rows, :] = result

        @pl.when(jnp.logical_not(is_first))
        def _():
            copy_of(slot).start()

    for slot in range(micro):

        @pl.when(jnp.logical_not(is_first))
        def _():
            copy_of(slot).wait_send()


def chain(top, inputs, activated, preact, scores, unit, rstd, mask, w_first, w_second, micro, length):
    tokens, width = inputs.shape
    return pl.pallas_call(
        functools.partial(chain_kernel, micro, length, lax.axis_size("pipe")),
        out_shape=(
            jax.ShapeDtypeStruct((tokens, width), jnp.bfloat16),
            jax.ShapeDtypeStruct(preact.shape, jnp.bfloat16),
            jax.ShapeDtypeStruct((tokens, width), jnp.bfloat16),
        ),
        in_specs=[VMEM] * 10,
        out_specs=(VMEM,) * 3,
        scratch_shapes=[
            pltpu.VMEM((micro, length, width), jnp.bfloat16),
            pltpu.VMEM((micro, length, width), jnp.bfloat16),
            pltpu.VMEM((length, V_COLS), jnp.float32),
            pltpu.VMEM((length, V_COLS), jnp.bfloat16),
            pltpu.VMEM((length, width), jnp.float32),
            pltpu.SemaphoreType.DMA((micro,)),
            pltpu.SemaphoreType.DMA((micro,)),
        ],
        compiler_params=pltpu.CompilerParams(
            collective_id=0, has_side_effects=True, vmem_limit_bytes=60 * 1024 * 1024
        ),
        name="chain",
    )(top, inputs, activated, preact, scores, unit, rstd, mask, w_first, w_second)


def add_into(target, left, right):
    step = 32

    def one(index, _):
        rows = pl.ds(pl.multiple_of(index * step, step), step)
        total = left[rows, :].astype(jnp.float32) + right[rows, :].astype(jnp.float32)
        target[rows, :] = total.astype(target.dtype)
        return 0

    lax.fori_loop(0, target.shape[0] // step, one, 0)


def scatter_kernel(line, part_a, part_b, out_a, out_b, *scratch):
    pairs = (
        (part_a, out_a) + scratch[0:4],
        (part_b, out_b) + scratch[4:8],
    )
    load_sem, pair_send, pair_recv, right_send, right_recv, left_send, left_recv = scratch[8:]
    rank = lax.axis_index("dp")
    spot, lane_of = rank // 2, rank % 2
    has_left, has_right = spot > 0, spot < line - 1
    partner = spot * 2 + 1 - lane_of
    right = jnp.minimum(spot + 1, line - 1) * 2 + lane_of
    left = jnp.maximum(spot - 1, 0) * 2 + lane_of

    barrier = pltpu.get_barrier_semaphore()
    pl.semaphore_signal(barrier, inc=1, device_id={"dp": partner}, device_id_type=MESH)

    @pl.when(has_left)
    def _():
        pl.semaphore_signal(barrier, inc=1, device_id={"dp": left}, device_id_type=MESH)

    @pl.when(has_right)
    def _():
        pl.semaphore_signal(barrier, inc=1, device_id={"dp": right}, device_id_type=MESH)

    pl.semaphore_wait(barrier, 1 + jnp.minimum(spot, 1) + jnp.minimum(line - 1 - spot, 1))

    def block_at(turn):
        near = jnp.minimum(spot, line - 1 - spot)
        ahead = line - 1 - 2 * near
        lone = jnp.where(spot <= line - 1 - spot, line - 1 - turn, turn)
        after = jnp.maximum(turn - ahead, 0)
        reach = near - after // 2
        both = jnp.where(after % 2 == 0, spot + reach, spot - reach)
        return jnp.where(turn < ahead, lone, both)

    def load_of(which, block):
        part, _, own, _, _, _ = pairs[which]
        return pltpu.make_async_copy(part.at[block, lane_of], own.at[block], load_sem.at[which, block])

    def pair_of(which, block):
        part, _, _, paired, _, _ = pairs[which]
        return pltpu.make_async_remote_copy(
            src_ref=part.at[block, 1 - lane_of], dst_ref=paired.at[block],
            send_sem=pair_send.at[which, block], recv_sem=pair_recv.at[which, block],
            device_id={"dp": partner}, device_id_type=MESH,
        )

    def flow_of(which, block, rightward, source):
        flow = pairs[which][4 if rightward else 5]
        sends, recvs = (right_send, right_recv) if rightward else (left_send, left_recv)
        return pltpu.make_async_remote_copy(
            src_ref=source.at[block], dst_ref=flow.at[block],
            send_sem=sends.at[which, block], recv_sem=recvs.at[which, block],
            device_id={"dp": right if rightward else left}, device_id_type=MESH,
        )

    def begin(turn, _):
        block = block_at(turn)
        for which in range(2):
            pair_of(which, block).start()
            load_of(which, block).start()
        return 0

    lax.fori_loop(0, line, begin, 0)

    def pass_on(turn, _):
        block = block_at(turn)
        for which in range(2):
            own, paired = pairs[which][2:4]
            load_of(which, block).wait()
            pair_of(which, block).wait_recv()
            add_into(own.at[block], own.at[block], paired.at[block])
            for rightward in (True, False):
                flow = pairs[which][4 if rightward else 5]
                fed = has_left if rightward else has_right
                wanted = block > spot if rightward else block < spot

                @pl.when(jnp.logical_and(wanted, fed))
                def _():
                    flow_of(which, block, rightward, flow).wait_recv()
                    add_into(flow.at[block], flow.at[block], own.at[block])
                    flow_of(which, block, rightward, flow).start()

                @pl.when(jnp.logical_and(wanted, jnp.logical_not(fed)))
                def _():
                    flow_of(which, block, rightward, own).start()
        return 0

    lax.fori_loop(0, line, pass_on, 0)

    for which in range(2):
        out, own = pairs[which][1:3]
        for rightward in (True, False):
            flow = pairs[which][4 if rightward else 5]

            @pl.when(has_left if rightward else has_right)
            def _():
                flow_of(which, spot, rightward, flow).wait_recv()

        @pl.when(jnp.logical_and(has_left, has_right))
        def _():
            add_into(out, own.at[spot], pairs[which][4].at[spot])
            add_into(out, out, pairs[which][5].at[spot])

        @pl.when(jnp.logical_and(has_left, jnp.logical_not(has_right)))
        def _():
            add_into(out, own.at[spot], pairs[which][4].at[spot])

        @pl.when(jnp.logical_and(has_right, jnp.logical_not(has_left)))
        def _():
            add_into(out, own.at[spot], pairs[which][5].at[spot])

    def finish(block, _):
        for which in range(2):
            pair_of(which, block).wait_send()
            for rightward in (True, False):

                @pl.when(block > spot if rightward else block < spot)
                def _():
                    flow_of(which, block, rightward, pairs[which][2]).wait_send()
        return 0

    lax.fori_loop(0, line, finish, 0)


def scatter_sums(part_a, part_b):
    devices = lax.axis_size("dp")
    line = devices // 2
    parts = [part.reshape(line, 2, part.shape[0] // devices, part.shape[1]) for part in (part_a, part_b)]
    scratch = []
    for part in parts:
        scratch += [pltpu.VMEM((line,) + part.shape[2:], part.dtype)] * 4
    scratch += [pltpu.SemaphoreType.DMA((2, line))] * 7
    return pl.pallas_call(
        functools.partial(scatter_kernel, line),
        out_shape=tuple(jax.ShapeDtypeStruct(part.shape[2:], jnp.float32) for part in parts),
        in_specs=[pl.BlockSpec(memory_space=pl.ANY)] * 2,
        out_specs=(VMEM,) * 2,
        scratch_shapes=scratch,
        compiler_params=pltpu.CompilerParams(
            collective_id=1, has_side_effects=True, vmem_limit_bytes=60 * 1024 * 1024
        ),
        name="scatter_sums",
    )(*parts)


def mask_of(segments):
    length = segments.shape[1]
    same = segments[:, :, None] == segments[:, None, :]
    positions = lax.broadcasted_iota(jnp.int32, (length, length), 0)
    columns = lax.broadcasted_iota(jnp.int32, (length, length), 1)
    counts = jnp.sum(same.astype(jnp.float32), axis=2, keepdims=True)
    allowed = jnp.logical_and(same, (columns <= positions)[None])
    return (allowed.astype(jnp.float32) / counts).reshape(-1, length)


def body(section_input, top_grad, w_in, w_out, segments):
    micro, length = segments.shape
    inputs = section_input[0]
    w_first = lax.all_gather(w_in[0], "dp", axis=0, tiled=True)
    w_mine, w_first = lax.optimization_barrier((w_out[0], w_first))
    w_second = lax.all_gather(w_mine, "dp", axis=0, tiled=True)
    mask = mask_of(segments)
    normed = norm_rows(inputs.astype(jnp.float32)).astype(jnp.bfloat16)
    preact = jnp.dot(normed, w_first, preferred_element_type=jnp.float32)
    activated = jax.nn.silu(preact).astype(jnp.bfloat16)
    scores, unit, rstd, gated = attend(activated, mask, micro, length)
    upstream, grad_preact, grads = chain(
        top_grad, inputs, activated, preact, scores, unit, rstd, mask, w_first, w_second, micro, length
    )
    part_out = contract_rows(gated, upstream).astype(jnp.bfloat16)
    part_in = contract_rows(normed, grad_preact).astype(jnp.bfloat16)
    grad_first, grad_out = scatter_sums(part_in, part_out)
    return (grads[None], grad_first[None], grad_out[None])


CORES = 2


class Place:
    def __init__(self):
        self.pipe, self.dp = lax.axis_index("pipe"), lax.axis_index("dp")
        self.x, self.core = self.pipe // CORES, self.pipe % CORES
        self.z, self.y = self.dp // CORES, self.dp % CORES

    def device(self, x=None, core=None, z=None, y=None, pipe=None):
        x = self.x if x is None else x
        core = self.core if core is None else core
        z = self.z if z is None else z
        y = self.y if y is None else y
        return {"pipe": x * CORES + core if pipe is None else pipe, "dp": z * CORES + y}


def signal(sem, device):
    pl.semaphore_signal(sem, inc=1, device_id=device, device_id_type=MESH)


def remote(src, dst, send, recv, device):
    return pltpu.make_async_remote_copy(
        src_ref=src, dst_ref=dst, send_sem=send, recv_sem=recv, device_id=device, device_id_type=MESH
    )


def either(local_if, local, far):
    pl.when(local_if)(local)
    pl.when(jnp.logical_not(local_if))(far)


def layer_order(step, z, layers):
    return jnp.where(2 * z < layers, (z + step) % layers, (z + layers - step) % layers)


def work_kernel(
    micro, length, layers,
    input_ref, top_ref, w_in_ref, w_out_ref, home_mask_ref,
    grads_ref, up_ref, gpre_ref, normed_ref, gated_ref,
    first, second, stage_first, stage_second, work_in, top, mask,
    pre, act, score, unit, rstd, mixed, landed, leaving, ggate, dmix, gnorm,
    swap_send, swap_recv, top_send, top_recv, pre_send, pre_recv, own_send, hop_send, to_core, to_x, to_y, came,
    chain_send, chain_recv, back_send, back_recv,
):
    me = Place()
    width = work_in.shape[1]
    tokens = micro * length
    section = me.z
    other_x, other_core, other_y = 1 - me.x, 1 - me.core, 1 - me.y
    at_home = me.pipe == me.z
    is_last, is_first = section == layers - 1, section == 0
    weights = (
        (w_in_ref, first, stage_first),
        (w_out_ref, second, stage_second),
    )
    sizes = [ref.shape[0] // 4 for ref, _, _ in weights]

    def quarter(which, block, half, core):
        size = sizes[which]
        start = pl.multiple_of(((block * 2 + half) * CORES + core) * size, size)
        return weights[which][1].at[pl.ds(start, size), :]

    def shard(which, half, core):
        size = sizes[which]
        start = pl.multiple_of((half * CORES + core) * size, size)
        return weights[which][0].at[pl.ds(start, size), :]

    def came_at(which, block, half, core):
        return came.at[which, (block * 2 + half) * CORES + core]

    barrier = pltpu.get_barrier_semaphore()
    for layer in range(layers):
        for core in range(CORES):

            @pl.when(jnp.logical_not(jnp.logical_and(layer == me.z, core == me.core)))
            def _():
                signal(barrier, me.device(core=core, z=layer))

    for core in range(CORES):
        signal(barrier, me.device(x=other_x, core=core))
    signal(barrier, me.device(y=other_y))

    @pl.when(jnp.logical_not(at_home))
    def _():
        signal(barrier, {"pipe": me.z, "dp": me.pipe * CORES + me.y})

    pl.semaphore_wait(barrier, layers * CORES + 2 + jnp.where(at_home, 0, 1))

    swap = {"pipe": me.z, "dp": me.pipe * CORES + me.y}
    swaps = ((input_ref, work_in), (home_mask_ref, mask))

    def swap_far(index):
        src, dst = swaps[index]
        return remote(src, dst, swap_send.at[index], swap_recv.at[index], swap)

    def swap_near(index):
        src, dst = swaps[index]
        return pltpu.make_async_copy(src, dst, swap_recv.at[index])

    for index in range(2):
        either(at_home, lambda: swap_near(index).start(), lambda: swap_far(index).start())

    def before(which, core):
        return remote(
            shard(which, other_x, core), weights[which][2].at[me.core],
            pre_send.at[which, core], pre_recv.at[which, me.core], me.device(x=other_x, core=core),
        )

    def own(which, core):
        return remote(
            shard(which, me.x, core), quarter(which, me.dp, me.x, core),
            own_send.at[which, core], came_at(which, me.dp, me.x, core), me.device(core=core, z=me.pipe),
        )

    def own_near(which, core):
        return pltpu.make_async_copy(
            shard(which, me.x, core), quarter(which, me.dp, me.x, core), came_at(which, me.dp, me.x, core)
        )

    def hop(which, source):
        return remote(
            weights[which][2].at[source], quarter(which, me.dp, me.x, me.core),
            hop_send.at[which, source], came_at(which, me.dp, me.x, me.core),
            me.device(z=other_x * CORES + source),
        )

    def hop_near(which, source):
        return pltpu.make_async_copy(
            weights[which][2].at[source], quarter(which, me.dp, me.x, me.core),
            came_at(which, me.dp, me.x, me.core),
        )

    def before_came(which, source):
        return remote(
            shard(which, other_x, me.core), weights[which][2].at[source],
            pre_send.at[which, source], pre_recv.at[which, source], me.device(x=other_x),
        )

    for which in range(2):
        for core in range(CORES):
            before(which, core).start()
        for core in range(CORES):
            near = jnp.logical_and(at_home, core == me.core)
            either(near, lambda: own_near(which, core).start(), lambda: own(which, core).start())

    for which in range(2):
        for source in range(CORES):
            before_came(which, source).wait_recv()
            either(
                other_x * CORES + source == me.z,
                lambda: hop_near(which, source).start(),
                lambda: hop(which, source).start(),
            )

    top_far = remote(top_ref, top, top_send, top_recv, me.device(z=layers - 1))
    top_near = pltpu.make_async_copy(top_ref, top, top_recv)
    gives_top = jnp.logical_and(at_home, me.pipe < layers - 1)
    keeps_top = jnp.logical_and(at_home, me.pipe == layers - 1)

    @pl.when(gives_top)
    def _():
        top_far.start()

    @pl.when(keeps_top)
    def _():
        top_near.start()

    def send(which, block, half, core, sem, index, device):
        place = quarter(which, block, half, core)
        return remote(place, place, sem.at[which, index], came_at(which, block, half, core), device)

    def direct_block(step):
        return layer_order(step, me.z, layers) * CORES + me.y

    def core_copy(which, kind, step):
        block = direct_block(step)
        lane = kind // 2
        block = block if lane == 0 else block - me.y + other_y
        half = me.x if kind % 2 == 0 else other_x
        return send(which, block, half, me.core, to_core, kind * layers + step, me.device(core=other_core))

    def x_copy(which, step):
        return send(which, direct_block(step), me.x, me.core, to_x, step, me.device(x=other_x))

    def y_copy(which, kind, step):
        half = me.x if kind == 0 else other_x
        return send(which, direct_block(step), half, me.core, to_y, kind * layers + step, me.device(y=other_y))

    def arrived(which, block, half, core):
        place = quarter(which, block, half, core)
        return remote(
            place, place, to_core.at[which, 0], came_at(which, block, half, core), me.device(core=other_core)
        )

    def direct_near(which, step):
        block = direct_block(step)
        own_half = me.pipe // CORES == me.z // CORES
        return own_half, block

    for which in range(2):
        for step in range(layers + 2):
            if step < layers:
                block = direct_block(step)
                if step == 0:
                    far = jnp.logical_and(me.x == me.z // CORES, me.core != me.z % CORES)
                    place = quarter(which, block, me.x, me.core)
                    either(
                        jnp.logical_not(far),
                        lambda: pltpu.make_async_copy(
                            shard(which, 0, 0), place, came_at(which, block, me.x, me.core)
                        ).wait(),
                        lambda: arrived(which, block, me.x, me.core).wait_recv(),
                    )
                else:
                    arrived(which, block, me.x, me.core).wait_recv()
                x_copy(which, step).start()
                y_copy(which, 0, step).start()
                core_copy(which, 0, step).start()
            if 1 <= step <= layers:
                block = direct_block(step - 1)
                arrived(which, block, other_x, me.core).wait_recv()
                y_copy(which, 1, step - 1).start()
                core_copy(which, 1, step - 1).start()
                arrived(which, block - me.y + other_y, me.x, me.core).wait_recv()
                core_copy(which, 2, step - 1).start()
            if step >= 2:
                block = direct_block(step - 2)
                arrived(which, block - me.y + other_y, other_x, me.core).wait_recv()
                core_copy(which, 3, step - 2).start()

    for index in range(2):
        either(at_home, lambda: swap_near(index).wait(), lambda: swap_far(index).wait_recv())

    for which in range(2):
        def landed_all(index, _):
            block, half = index // 2, index % 2
            arrived(which, block, half, other_core).wait_recv()
            return 0

        lax.fori_loop(0, 2 * layers * CORES, landed_all, 0)

    normed_ref[...] = norm_rows(work_in[...].astype(jnp.float32)).astype(jnp.bfloat16)
    tile = 2 * LANES

    def front(index, _):
        cols = at(index * tile, tile)
        value = dot_nn(normed_ref[...], first[:, cols])
        pre[:, cols] = value
        act[:, cols] = jax.nn.silu(value).astype(jnp.bfloat16)
        return 0

    lax.fori_loop(0, pre.shape[1] // tile, front, 0)

    attend_kernel(micro, length, act, mask, score, unit, rstd, gated_ref, mixed)

    def copy_of(slot):
        return remote(
            leaving.at[slot], landed.at[slot], chain_send.at[slot], chain_recv.at[slot],
            me.device(z=jnp.maximum(me.z - 1, 0)),
        )

    def back_rows(ref, slot):
        return ref.at[pl.ds(slot * length, length), :]

    def back_far(slot):
        return remote(leaving.at[slot], back_rows(grads_ref, slot), back_send.at[slot], back_recv.at[slot], swap)

    def back_near(slot):
        return pltpu.make_async_copy(leaving.at[slot], back_rows(grads_ref, slot), back_recv.at[slot])

    @pl.when(jnp.logical_and(is_last, jnp.logical_not(at_home)))
    def _():
        top_far.wait_recv()

    @pl.when(keeps_top)
    def _():
        top_near.wait()

    chain_steps(
        micro, length, is_first, is_last, copy_of, back_far, back_near, at_home,
        top, work_in, act, pre, score, unit, rstd, mask, first, second,
        up_ref, gpre_ref, landed, leaving, ggate, dmix, gnorm,
    )

    for slot in range(micro):

        @pl.when(jnp.logical_not(is_first))
        def _():
            copy_of(slot).wait_send()

        either(at_home, lambda: back_near(slot).wait(), lambda: back_far(slot).wait())

    for index in range(2):
        pl.when(jnp.logical_not(at_home))(lambda: swap_far(index).wait_send())
    pl.when(gives_top)(lambda: top_far.wait_send())
    for which in range(2):
        for core in range(CORES):
            before(which, core).wait_send()
            near = jnp.logical_and(at_home, core == me.core)
            pl.when(jnp.logical_not(near))(lambda: own(which, core).wait_send())
        for source in range(CORES):
            near = other_x * CORES + source == me.z
            pl.when(jnp.logical_not(near))(lambda: hop(which, source).wait_send())

        def sent(step, _):
            x_copy(which, step).wait_send()
            for kind in range(2):
                y_copy(which, kind, step).wait_send()
            for kind in range(4):
                core_copy(which, kind, step).wait_send()
            return 0

        lax.fori_loop(0, layers, sent, 0)


def chain_steps(
    micro, length, is_first, is_last, copy_of, back_far, back_near, at_home,
    top_ref, input_ref, act_ref, pre_ref, score_ref, unit_ref, rstd_ref, mask_ref, first_ref, second_ref,
    up_ref, gpre_ref, landed, leaving, ggate, dmix, gnorm,
):
    width = input_ref.shape[1]
    tile = 2 * LANES
    lane = lax.broadcasted_iota(jnp.int32, (length, LANES), 1)

    def store_grad(rows, cols, size, value):
        rounded = value.astype(jnp.bfloat16).astype(jnp.float32)
        gpre_ref[rows, at(cols, size)] = (
            rounded * silu_slope(pre_ref[rows, at(cols, size)])
        ).astype(jnp.bfloat16)

    for slot in range(micro):
        rows = pl.ds(slot * length, length)

        @pl.when(is_last)
        def _():
            up_ref[rows, :] = top_ref[rows, :]

        @pl.when(jnp.logical_not(is_last))
        def _():
            copy_of(slot).wait_recv()
            up_ref[rows, :] = landed[slot]

        def gate_tile(index, _):
            ggate[:, at(index * tile, tile)] = dot_nt(up_ref[rows, :], second_ref[at(index * tile, tile), :])
            return 0

        lax.fori_loop(0, V_COLS // tile, gate_tile, 0)
        gating = act_ref[rows, :V_COLS].astype(jnp.float32)
        unit = unit_ref[rows, :]
        grad = ggate[...]
        store_grad(rows, 0, V_COLS, grad * unit)
        grad = grad * gating
        mean_grad = jnp.mean(grad, axis=-1, keepdims=True)
        mean_unit = jnp.mean(grad * unit, axis=-1, keepdims=True)
        dmix[...] = (rstd_ref[rows, :1] * (grad - mean_grad - unit * mean_unit)).astype(jnp.bfloat16)

        def one(group, _):
            queries = act_ref[rows, at(2 * V_COLS + group * LANES, LANES)]
            keys = act_ref[rows, at(2 * V_COLS + Q_COLS + group * LANES, LANES)]
            mask = mask_ref[rows, :]
            grad_q = jnp.zeros((length, LANES), jnp.float32)
            grad_k = jnp.zeros((length, LANES), jnp.float32)
            for half in range(GROUP_V // LANES):
                cols = group * GROUP_V + half * LANES
                values = act_ref[rows, at(V_COLS + cols, LANES)]
                grad_mix = dmix[:, at(cols, LANES)]
                grad_v = jnp.zeros((length, LANES), jnp.float32)
                for sub in range(V_HEADS):
                    head = half * V_HEADS + sub
                    mix_head = only_head(grad_mix, lane, V_DIM, sub)
                    place = (slot * HEADS + group * QK_HEADS + head) * length
                    score = score_ref[at(place, length), :]
                    squash = jax.nn.sigmoid(score)
                    weight = (score * squash * mask).astype(jnp.bfloat16)
                    slope = squash * (1.0 + score * (1.0 - squash)) * mask * SCALE
                    grad_score = (dot_nt(mix_head, values) * slope).astype(jnp.bfloat16)
                    grad_v += contract_rows(weight, mix_head)
                    grad_q += dot_nn(grad_score, only_head(keys, lane, QK_DIM, head))
                    grad_k += contract_rows(grad_score, only_head(queries, lane, QK_DIM, head))
                store_grad(rows, V_COLS + cols, LANES, grad_v)
            store_grad(rows, 2 * V_COLS + group * LANES, LANES, grad_q)
            store_grad(rows, 2 * V_COLS + Q_COLS + group * LANES, LANES, grad_k)
            return 0

        lax.fori_loop(0, GROUPS, one, 0)

        def norm_tile(index, _):
            gnorm[:, at(index * tile, tile)] = dot_nt(gpre_ref[rows, :], first_ref[at(index * tile, tile), :])
            return 0

        lax.fori_loop(0, width // tile, norm_tile, 0)
        value = input_ref[rows, :].astype(jnp.float32)
        center = value - jnp.mean(value, axis=-1, keepdims=True)
        rstd = lax.rsqrt(jnp.mean(center * center, axis=-1, keepdims=True) + EPSILON)
        unit = center * rstd
        grad = gnorm[...]
        mean_grad = jnp.mean(grad, axis=-1, keepdims=True)
        mean_unit = jnp.mean(grad * unit, axis=-1, keepdims=True)
        through = rstd * (grad - mean_grad - unit * mean_unit)
        leaving[slot] = (up_ref[rows, :].astype(jnp.float32) + through).astype(jnp.bfloat16)

        @pl.when(jnp.logical_not(is_first))
        def _():
            copy_of(slot).start()

        either(at_home, lambda: back_near(slot).start(), lambda: back_far(slot).start())


ANY = pl.BlockSpec(memory_space=pl.ANY)
LIMIT = 60 * 1024 * 1024


def work(inputs, top_grad, w_in, w_out, mask, micro, length):
    tokens, width = inputs.shape
    layers, blocks = lax.axis_size("pipe"), lax.axis_size("dp")
    columns = w_in.shape[1]
    quarters = [w.shape[0] // 4 for w in (w_in, w_out)]
    dma = pltpu.SemaphoreType.DMA
    return pl.pallas_call(
        functools.partial(work_kernel, micro, length, layers),
        out_shape=(
            jax.ShapeDtypeStruct((tokens, width), jnp.bfloat16),
            jax.ShapeDtypeStruct((tokens, width), jnp.bfloat16),
            jax.ShapeDtypeStruct((tokens, columns), jnp.bfloat16),
            jax.ShapeDtypeStruct((tokens, width), jnp.bfloat16),
            jax.ShapeDtypeStruct((tokens, V_COLS), jnp.bfloat16),
        ),
        in_specs=[ANY] * 5,
        out_specs=(ANY,) + (VMEM,) * 4,
        scratch_shapes=[
            pltpu.VMEM((blocks * w_in.shape[0], columns), jnp.bfloat16),
            pltpu.VMEM((blocks * w_out.shape[0], width), jnp.bfloat16),
            pltpu.VMEM((CORES, quarters[0], columns), jnp.bfloat16),
            pltpu.VMEM((CORES, quarters[1], width), jnp.bfloat16),
            pltpu.VMEM((tokens, width), jnp.bfloat16),
            pltpu.VMEM((tokens, width), jnp.bfloat16),
            pltpu.VMEM((tokens, length), jnp.float32),
            pltpu.VMEM((tokens, columns), jnp.float32),
            pltpu.VMEM((tokens, columns), jnp.bfloat16),
            pltpu.VMEM((micro * HEADS * length, length), jnp.float32),
            pltpu.VMEM((tokens, V_COLS), jnp.float32),
            pltpu.VMEM((tokens, LANES), jnp.float32),
            pltpu.VMEM((tokens, V_COLS), jnp.float32),
            pltpu.VMEM((micro, length, width), jnp.bfloat16),
            pltpu.VMEM((micro, length, width), jnp.bfloat16),
            pltpu.VMEM((length, V_COLS), jnp.float32),
            pltpu.VMEM((length, V_COLS), jnp.bfloat16),
            pltpu.VMEM((length, width), jnp.float32),
            dma((2,)), dma((2,)), dma, dma,
            dma((2, CORES)), dma((2, CORES)), dma((2, CORES)), dma((2, CORES)),
            dma((2, 4 * layers)), dma((2, layers)), dma((2, 2 * layers)), dma((2, 4 * blocks)),
            dma((micro,)), dma((micro,)), dma((micro,)), dma((micro,)),
        ],
        compiler_params=pltpu.CompilerParams(collective_id=2, has_side_effects=True, vmem_limit_bytes=LIMIT),
        name="work",
    )(inputs, top_grad, w_in, w_out, mask)


def add_rows(target, other):
    step = 16

    def one(index, _):
        rows = pl.ds(pl.multiple_of(index * step, step), step)
        total = target[rows, :].astype(jnp.float32) + other[rows, :].astype(jnp.float32)
        target[rows, :] = total.astype(target.dtype)
        return 0

    lax.fori_loop(0, target.shape[0] // step, one, 0)


def weight_kernel(
    layers,
    normed_ref, gpre_ref, gated_ref, up_ref,
    out_first, out_second,
    first, second, core_first, core_second, y_first, y_second, x_first, x_second,
    core_send, core_recv, y_send, y_recv, x_send, x_recv, home_send, home_recv,
):
    me = Place()
    other_x, other_core, other_y = 1 - me.x, 1 - me.core, 1 - me.y
    at_home = me.pipe == me.z
    sets = (
        (normed_ref, gpre_ref, out_first, first, core_first, y_first, x_first),
        (gated_ref, up_ref, out_second, second, core_second, y_second, x_second),
    )
    sizes = [s[2].shape[0] // 4 for s in sets]

    barrier = pltpu.get_barrier_semaphore()
    signal(barrier, me.device(core=other_core))
    signal(barrier, me.device(x=other_x))
    signal(barrier, me.device(y=other_y))
    for pipe in range(layers):

        @pl.when(jnp.logical_not(jnp.logical_and(at_home, pipe == me.pipe)))
        def _():
            signal(barrier, {"pipe": pipe, "dp": me.pipe * CORES + me.y})

    pl.semaphore_wait(barrier, 3 + layers - jnp.where(at_home, 1, 0))

    def quarter(which, block, half, core):
        size = sizes[which]
        start = pl.multiple_of(((block * 2 + half) * CORES + core) * size, size)
        return sets[which][3].at[pl.ds(start, size), :]

    def core_copy(which, block, half, mine):
        core = me.core if mine else other_core
        index = block * 2 + half
        return remote(
            quarter(which, block, half, core), sets[which][4].at[index],
            core_send.at[which, index], core_recv.at[which, index], me.device(core=other_core),
        )

    def y_copy(which, row, half, mine):
        block = row * CORES + (me.y if mine else other_y)
        index = row * 2 + half
        return remote(
            quarter(which, block, half, me.core), sets[which][5].at[index],
            y_send.at[which, index], y_recv.at[which, index], me.device(y=other_y),
        )

    def x_copy(which, row, mine):
        block = row * CORES + me.y
        return remote(
            quarter(which, block, me.x if mine else other_x, me.core), sets[which][6].at[row],
            x_send.at[which, row], x_recv.at[which, row], me.device(x=other_x),
        )

    def home_rows(which, half, core):
        size = sizes[which]
        return sets[which][2].at[pl.ds(pl.multiple_of((half * CORES + core) * size, size), size), :]

    def home_copy(which, row):
        return remote(
            quarter(which, row * CORES + me.y, me.x, me.core), home_rows(which, me.x, me.core),
            home_send.at[which, row], home_recv.at[which, me.x * CORES + me.core],
            {"pipe": me.z, "dp": row * CORES + me.y},
        )

    def home_near(which):
        return pltpu.make_async_copy(
            quarter(which, me.dp, me.x, me.core), home_rows(which, me.x, me.core),
            home_recv.at[which, me.x * CORES + me.core],
        )

    def row_at(step):
        return layer_order(layers - 1 - step, me.z, layers)

    def product(which, row):
        left, right, _, whole = sets[which][:4]
        size = 4 * sizes[which]
        tile = 2 * LANES
        for lane_of in (other_y, me.y):
            block = row * CORES + lane_of
            place = pl.ds(pl.multiple_of(block * size, size), size)

            def one(index, _):
                cols = at(index * tile, tile)
                whole[place, cols] = contract_rows(left[:, place], right[:, cols]).astype(whole.dtype)
                return 0

            lax.fori_loop(0, right.shape[1] // tile, one, 0)
            for half in range(2):
                core_copy(which, block, half, False).start()

    def fold_y(which, row):
        for half in range(2):
            block = row * CORES + other_y
            core_copy(which, block, half, True).wait_recv()
            add_rows(quarter(which, block, half, me.core), sets[which][4].at[block * 2 + half])
            y_copy(which, row, half, False).start()

    def fold_x(which, row):
        for half in (other_x, me.x):
            block = row * CORES + me.y
            core_copy(which, block, half, True).wait_recv()
            place = quarter(which, block, half, me.core)
            add_rows(place, sets[which][4].at[block * 2 + half])
            y_copy(which, row, half, True).wait_recv()
            add_rows(place, sets[which][5].at[row * 2 + half])

            @pl.when(half == other_x)
            def _():
                x_copy(which, row, False).start()

    def fold_home(which, row):
        x_copy(which, row, True).wait_recv()
        add_rows(quarter(which, row * CORES + me.y, me.x, me.core), sets[which][6].at[row])
        near = jnp.logical_and(at_home, row == me.z)
        either(near, lambda: home_near(which).start(), lambda: home_copy(which, row).start())

    def run(step, _):
        for which in range(2):

            @pl.when(step < layers)
            def _():
                product(which, row_at(step))

            @pl.when(jnp.logical_and(step >= 1, step < layers + 1))
            def _():
                fold_y(which, row_at(step - 1))

            @pl.when(jnp.logical_and(step >= 2, step < layers + 2))
            def _():
                fold_x(which, row_at(step - 2))

            @pl.when(step >= 3)
            def _():
                fold_home(which, row_at(step - 3))

        return 0

    lax.fori_loop(0, layers + 3, run, 0)

    for which in range(2):
        for pipe in range(layers):
            place = home_rows(which, pipe // CORES, pipe % CORES)
            near = jnp.logical_and(at_home, pipe == me.pipe)
            either(
                near,
                lambda: home_near(which).wait(),
                lambda: remote(
                    place, place, home_send.at[which, 0], home_recv.at[which, pipe], me.device(core=other_core)
                ).wait_recv(),
            )

        def sent(row, _):
            for half in range(2):
                for lane_of in range(2):
                    core_copy(which, row * CORES + lane_of, half, False).wait_send()
                y_copy(which, row, half, False).wait_send()
            x_copy(which, row, False).wait_send()
            near = jnp.logical_and(at_home, row == me.z)
            pl.when(jnp.logical_not(near))(lambda: home_copy(which, row).wait_send())
            return 0

        lax.fori_loop(0, layers, sent, 0)


def weight_sums(normed, grad_preact, gated, upstream):
    layers, blocks = lax.axis_size("pipe"), lax.axis_size("dp")
    dma = pltpu.SemaphoreType.DMA
    pairs = ((normed, grad_preact), (gated, upstream))
    shapes = [(left.shape[1], right.shape[1]) for left, right in pairs]
    scratch = [pltpu.VMEM(shape, jnp.bfloat16) for shape in shapes]
    for count in (2 * blocks, 2 * layers, layers):
        for rows, cols in shapes:
            scratch.append(pltpu.VMEM((count, rows // (4 * blocks), cols), jnp.bfloat16))
    for count in (2 * blocks, 2 * layers, layers, layers):
        scratch += [dma((2, count))] * 2
    return pl.pallas_call(
        functools.partial(weight_kernel, layers),
        out_shape=tuple(jax.ShapeDtypeStruct((rows // blocks, cols), jnp.bfloat16) for rows, cols in shapes),
        in_specs=[VMEM] * 4,
        out_specs=(ANY,) * 2,
        scratch_shapes=scratch,
        compiler_params=pltpu.CompilerParams(collective_id=3, has_side_effects=True, vmem_limit_bytes=LIMIT),
        name="weight_sums",
    )(normed, grad_preact, gated, upstream)


def layered_body(section_input, top_grad, w_in, w_out, segments):
    micro, length = segments.shape
    mask = mask_of(segments)
    grads, upstream, grad_preact, normed, gated = work(
        section_input[0], top_grad, w_in[0], w_out[0], mask, micro, length
    )
    grad_first, grad_out = weight_sums(normed, grad_preact, gated, upstream)
    return (grads[None], grad_first.astype(jnp.float32)[None], grad_out.astype(jnp.float32)[None])


def solution(mesh):
    layered = mesh.shape["pipe"] == CORES * 2 and mesh.shape["dp"] == CORES * mesh.shape["pipe"]
    return jax.shard_map(
        layered_body if layered else body,
        mesh=mesh,
        in_specs=(
            P("pipe", "dp", None),
            P("dp", None),
            P("pipe", "dp", None),
            P("pipe", "dp", None),
            P("dp", None),
        ),
        out_specs=(P("pipe", "dp", None), P("pipe", "dp", None), P("pipe", "dp", None)),
        check_vma=False,
    )
```

```python
import functools

import jax
import jax.numpy as jnp
from jax import lax
from jax.experimental import pallas as pl
from jax.experimental.pallas import tpu as pltpu
from jax.sharding import PartitionSpec as P

HEADS = 16
QK_DIM = 32
V_DIM = 64
LANES = 128

EPSILON = 1e-05
MESH = pl.DeviceIdType.MESH
VMEM = pl.BlockSpec(memory_space=pltpu.VMEM)

QK_HEADS = LANES // QK_DIM
V_HEADS = LANES // V_DIM
GROUPS = HEADS // QK_HEADS
V_COLS = HEADS * V_DIM
Q_COLS = HEADS * QK_DIM
GROUP_V = QK_HEADS * V_DIM
SCALE = QK_DIM ** (-0.5)


def norm_rows(values):
    center = values - jnp.mean(values, axis=-1, keepdims=True)
    return center * lax.rsqrt(jnp.mean(center * center, axis=-1, keepdims=True) + EPSILON)


def silu_slope(preact):
    squash = jax.nn.sigmoid(preact)
    return squash * (1.0 + preact * (1.0 - squash))


def dot_nt(left, right):
    return lax.dot_general(
        left, right, (((1,), (1,)), ((), ())), preferred_element_type=jnp.float32
    )


def dot_nn(left, right):
    return lax.dot_general(
        left, right, (((1,), (0,)), ((), ())), preferred_element_type=jnp.float32
    )


def contract_rows(left, right):
    return lax.dot_general(
        left, right, (((0,), (0,)), ((), ())), preferred_element_type=jnp.float32
    )


def only_head(block, lane, width, index):
    keep = jnp.logical_and(lane >= index * width, lane < (index + 1) * width)
    return jnp.where(keep, block, jnp.zeros_like(block))


def at(start, size):
    return pl.ds(pl.multiple_of(start, LANES), size)


def attend_kernel(micro, length, act_ref, mask_ref, score_ref, unit_ref, rstd_ref, gated_ref, mixed):
    lane = lax.broadcasted_iota(jnp.int32, (length, LANES), 1)

    def one(index, _):
        slot, group = index // GROUPS, index % GROUPS
        rows = at(slot * length, length)
        queries = act_ref[rows, at(2 * V_COLS + group * LANES, LANES)]
        keys = act_ref[rows, at(2 * V_COLS + Q_COLS + group * LANES, LANES)]
        mask = mask_ref[rows, :]
        for half in range(GROUP_V // LANES):
            cols = group * GROUP_V + half * LANES
            values = act_ref[rows, at(V_COLS + cols, LANES)]
            total = jnp.zeros((length, LANES), jnp.float32)
            for sub in range(V_HEADS):
                head = half * V_HEADS + sub
                score = dot_nt(only_head(queries, lane, QK_DIM, head), keys) * SCALE
                score_ref[at((index * QK_HEADS + head) * length, length), :] = score
                weight = (jax.nn.silu(score) * mask).astype(jnp.bfloat16)
                total += dot_nn(weight, only_head(values, lane, V_DIM, sub))
            mixed[rows, at(cols, LANES)] = total
        return 0

    lax.fori_loop(0, micro * GROUPS, one, 0)

    def finish(slot, _):
        rows = at(slot * length, length)
        value = mixed[rows, :]
        center = value - jnp.mean(value, axis=-1, keepdims=True)
        rstd = lax.rsqrt(jnp.mean(center * center, axis=-1, keepdims=True) + EPSILON)
        unit = center * rstd
        unit_ref[rows, :] = unit
        rstd_ref[rows, :] = jnp.broadcast_to(rstd, (length, LANES))
        gated_ref[rows, :] = (unit * act_ref[rows, :V_COLS].astype(jnp.float32)).astype(jnp.bfloat16)
        return 0

    lax.fori_loop(0, micro, finish, 0)


def attend(activated, mask, micro, length):
    tokens = micro * length
    return pl.pallas_call(
        functools.partial(attend_kernel, micro, length),
        out_shape=(
            jax.ShapeDtypeStruct((micro * HEADS * length, length), jnp.float32),
            jax.ShapeDtypeStruct((tokens, V_COLS), jnp.float32),
            jax.ShapeDtypeStruct((tokens, LANES), jnp.float32),
            jax.ShapeDtypeStruct((tokens, V_COLS), jnp.bfloat16),
        ),
        in_specs=[VMEM] * 2,
        out_specs=(VMEM,) * 4,
        scratch_shapes=[pltpu.VMEM((tokens, V_COLS), jnp.float32)],
        name="attend",
    )(activated, mask)


def chain_kernel(
    micro, length, sections,
    top_ref, input_ref, act_ref, pre_ref, score_ref, unit_ref, rstd_ref, mask_ref, first_ref, second_ref,
    up_ref, gpre_ref, gin_ref,
    landed, leaving, ggate, dmix, gnorm, send_sem, recv_sem,
):
    section = lax.axis_index("pipe")
    width = input_ref.shape[1]
    tile = 2 * LANES
    lane = lax.broadcasted_iota(jnp.int32, (length, LANES), 1)
    is_last = section == sections - 1
    is_first = section == 0

    barrier = pltpu.get_barrier_semaphore()

    @pl.when(jnp.logical_not(is_last))
    def _():
        pl.semaphore_signal(
            barrier, inc=1, device_id={"pipe": jnp.minimum(section + 1, sections - 1)}, device_id_type=MESH
        )

    @pl.when(jnp.logical_not(is_first))
    def _():
        pl.semaphore_wait(barrier, 1)

    def copy_of(slot):
        return pltpu.make_async_remote_copy(
            src_ref=leaving.at[slot],
            dst_ref=landed.at[slot],
            send_sem=send_sem.at[slot],
            recv_sem=recv_sem.at[slot],
            device_id={"pipe": jnp.maximum(section - 1, 0)},
            device_id_type=MESH,
        )

    def store_grad(rows, cols, size, value):
        rounded = value.astype(jnp.bfloat16).astype(jnp.float32)
        gpre_ref[rows, at(cols, size)] = (
            rounded * silu_slope(pre_ref[rows, at(cols, size)])
        ).astype(jnp.bfloat16)

    for slot in range(micro):
        rows = pl.ds(slot * length, length)

        @pl.when(is_last)
        def _():
            up_ref[rows, :] = top_ref[rows, :]

        @pl.when(jnp.logical_not(is_last))
        def _():
            copy_of(slot).wait_recv()
            up_ref[rows, :] = landed[slot]

        def gate_tile(index, _):
            ggate[:, at(index * tile, tile)] = dot_nt(up_ref[rows, :], second_ref[at(index * tile, tile), :])
            return 0

        lax.fori_loop(0, V_COLS // tile, gate_tile, 0)
        gating = act_ref[rows, :V_COLS].astype(jnp.float32)
        unit = unit_ref[rows, :]
        grad = ggate[...]
        store_grad(rows, 0, V_COLS, grad * unit)
        grad = grad * gating
        mean_grad = jnp.mean(grad, axis=-1, keepdims=True)
        mean_unit = jnp.mean(grad * unit, axis=-1, keepdims=True)
        dmix[...] = (rstd_ref[rows, :1] * (grad - mean_grad - unit * mean_unit)).astype(jnp.bfloat16)

        def one(group, _):
            queries = act_ref[rows, at(2 * V_COLS + group * LANES, LANES)]
            keys = act_ref[rows, at(2 * V_COLS + Q_COLS + group * LANES, LANES)]
            mask = mask_ref[rows, :]
            grad_q = jnp.zeros((length, LANES), jnp.float32)
            grad_k = jnp.zeros((length, LANES), jnp.float32)
            for half in range(GROUP_V // LANES):
                cols = group * GROUP_V + half * LANES
                values = act_ref[rows, at(V_COLS + cols, LANES)]
                grad_mix = dmix[:, at(cols, LANES)]
                grad_v = jnp.zeros((length, LANES), jnp.float32)
                for sub in range(V_HEADS):
                    head = half * V_HEADS + sub
                    mix_head = only_head(grad_mix, lane, V_DIM, sub)
                    place = (slot * HEADS + group * QK_HEADS + head) * length
                    score = score_ref[at(place, length), :]
                    squash = jax.nn.sigmoid(score)
                    weight = (score * squash * mask).astype(jnp.bfloat16)
                    slope = squash * (1.0 + score * (1.0 - squash)) * mask * SCALE
                    grad_score = (dot_nt(mix_head, values) * slope).astype(jnp.bfloat16)
                    grad_v += contract_rows(weight, mix_head)
                    grad_q += dot_nn(grad_score, only_head(keys, lane, QK_DIM, head))
                    grad_k += contract_rows(grad_score, only_head(queries, lane, QK_DIM, head))
                store_grad(rows, V_COLS + cols, LANES, grad_v)
            store_grad(rows, 2 * V_COLS + group * LANES, LANES, grad_q)
            store_grad(rows, 2 * V_COLS + Q_COLS + group * LANES, LANES, grad_k)
            return 0

        lax.fori_loop(0, GROUPS, one, 0)

        def norm_tile(index, _):
            gnorm[:, at(index * tile, tile)] = dot_nt(gpre_ref[rows, :], first_ref[at(index * tile, tile), :])
            return 0

        lax.fori_loop(0, width // tile, norm_tile, 0)
        value = input_ref[rows, :].astype(jnp.float32)
        center = value - jnp.mean(value, axis=-1, keepdims=True)
        rstd = lax.rsqrt(jnp.mean(center * center, axis=-1, keepdims=True) + EPSILON)
        unit = center * rstd
        grad = gnorm[...]
        mean_grad = jnp.mean(grad, axis=-1, keepdims=True)
        mean_unit = jnp.mean(grad * unit, axis=-1, keepdims=True)
        through = rstd * (grad - mean_grad - unit * mean_unit)
        result = (up_ref[rows, :].astype(jnp.float32) + through).astype(jnp.bfloat16)
        leaving[slot] = result
        gin_ref[rows, :] = result

        @pl.when(jnp.logical_not(is_first))
        def _():
            copy_of(slot).start()

    for slot in range(micro):

        @pl.when(jnp.logical_not(is_first))
        def _():
            copy_of(slot).wait_send()


def chain(top, inputs, activated, preact, scores, unit, rstd, mask, w_first, w_second, micro, length):
    tokens, width = inputs.shape
    return pl.pallas_call(
        functools.partial(chain_kernel, micro, length, lax.axis_size("pipe")),
        out_shape=(
            jax.ShapeDtypeStruct((tokens, width), jnp.bfloat16),
            jax.ShapeDtypeStruct(preact.shape, jnp.bfloat16),
            jax.ShapeDtypeStruct((tokens, width), jnp.bfloat16),
        ),
        in_specs=[VMEM] * 10,
        out_specs=(VMEM,) * 3,
        scratch_shapes=[
            pltpu.VMEM((micro, length, width), jnp.bfloat16),
            pltpu.VMEM((micro, length, width), jnp.bfloat16),
            pltpu.VMEM((length, V_COLS), jnp.float32),
            pltpu.VMEM((length, V_COLS), jnp.bfloat16),
            pltpu.VMEM((length, width), jnp.float32),
            pltpu.SemaphoreType.DMA((micro,)),
            pltpu.SemaphoreType.DMA((micro,)),
        ],
        compiler_params=pltpu.CompilerParams(
            collective_id=0, has_side_effects=True, vmem_limit_bytes=60 * 1024 * 1024
        ),
        name="chain",
    )(top, inputs, activated, preact, scores, unit, rstd, mask, w_first, w_second)


def add_into(target, left, right):
    step = 32

    def one(index, _):
        rows = pl.ds(pl.multiple_of(index * step, step), step)
        total = left[rows, :].astype(jnp.float32) + right[rows, :].astype(jnp.float32)
        target[rows, :] = total.astype(target.dtype)
        return 0

    lax.fori_loop(0, target.shape[0] // step, one, 0)


def scatter_kernel(line, part_a, part_b, out_a, out_b, *scratch):
    pairs = (
        (part_a, out_a) + scratch[0:4],
        (part_b, out_b) + scratch[4:8],
    )
    load_sem, pair_send, pair_recv, right_send, right_recv, left_send, left_recv = scratch[8:]
    rank = lax.axis_index("dp")
    spot, lane_of = rank // 2, rank % 2
    has_left, has_right = spot > 0, spot < line - 1
    partner = spot * 2 + 1 - lane_of
    right = jnp.minimum(spot + 1, line - 1) * 2 + lane_of
    left = jnp.maximum(spot - 1, 0) * 2 + lane_of

    barrier = pltpu.get_barrier_semaphore()
    pl.semaphore_signal(barrier, inc=1, device_id={"dp": partner}, device_id_type=MESH)

    @pl.when(has_left)
    def _():
        pl.semaphore_signal(barrier, inc=1, device_id={"dp": left}, device_id_type=MESH)

    @pl.when(has_right)
    def _():
        pl.semaphore_signal(barrier, inc=1, device_id={"dp": right}, device_id_type=MESH)

    pl.semaphore_wait(barrier, 1 + jnp.minimum(spot, 1) + jnp.minimum(line - 1 - spot, 1))

    def block_at(turn):
        near = jnp.minimum(spot, line - 1 - spot)
        ahead = line - 1 - 2 * near
        lone = jnp.where(spot <= line - 1 - spot, line - 1 - turn, turn)
        after = jnp.maximum(turn - ahead, 0)
        reach = near - after // 2
        both = jnp.where(after % 2 == 0, spot + reach, spot - reach)
        return jnp.where(turn < ahead, lone, both)

    def load_of(which, block):
        part, _, own, _, _, _ = pairs[which]
        return pltpu.make_async_copy(part.at[block, lane_of], own.at[block], load_sem.at[which, block])

    def pair_of(which, block):
        part, _, _, paired, _, _ = pairs[which]
        return pltpu.make_async_remote_copy(
            src_ref=part.at[block, 1 - lane_of], dst_ref=paired.at[block],
            send_sem=pair_send.at[which, block], recv_sem=pair_recv.at[which, block],
            device_id={"dp": partner}, device_id_type=MESH,
        )

    def flow_of(which, block, rightward, source):
        flow = pairs[which][4 if rightward else 5]
        sends, recvs = (right_send, right_recv) if rightward else (left_send, left_recv)
        return pltpu.make_async_remote_copy(
            src_ref=source.at[block], dst_ref=flow.at[block],
            send_sem=sends.at[which, block], recv_sem=recvs.at[which, block],
            device_id={"dp": right if rightward else left}, device_id_type=MESH,
        )

    def begin(turn, _):
        block = block_at(turn)
        for which in range(2):
            pair_of(which, block).start()
            load_of(which, block).start()
        return 0

    lax.fori_loop(0, line, begin, 0)

    def pass_on(turn, _):
        block = block_at(turn)
        for which in range(2):
            own, paired = pairs[which][2:4]
            load_of(which, block).wait()
            pair_of(which, block).wait_recv()
            add_into(own.at[block], own.at[block], paired.at[block])
            for rightward in (True, False):
                flow = pairs[which][4 if rightward else 5]
                fed = has_left if rightward else has_right
                wanted = block > spot if rightward else block < spot

                @pl.when(jnp.logical_and(wanted, fed))
                def _():
                    flow_of(which, block, rightward, flow).wait_recv()
                    add_into(flow.at[block], flow.at[block], own.at[block])
                    flow_of(which, block, rightward, flow).start()

                @pl.when(jnp.logical_and(wanted, jnp.logical_not(fed)))
                def _():
                    flow_of(which, block, rightward, own).start()
        return 0

    lax.fori_loop(0, line, pass_on, 0)

    for which in range(2):
        out, own = pairs[which][1:3]
        for rightward in (True, False):
            flow = pairs[which][4 if rightward else 5]

            @pl.when(has_left if rightward else has_right)
            def _():
                flow_of(which, spot, rightward, flow).wait_recv()

        @pl.when(jnp.logical_and(has_left, has_right))
        def _():
            add_into(out, own.at[spot], pairs[which][4].at[spot])
            add_into(out, out, pairs[which][5].at[spot])

        @pl.when(jnp.logical_and(has_left, jnp.logical_not(has_right)))
        def _():
            add_into(out, own.at[spot], pairs[which][4].at[spot])

        @pl.when(jnp.logical_and(has_right, jnp.logical_not(has_left)))
        def _():
            add_into(out, own.at[spot], pairs[which][5].at[spot])

    def finish(block, _):
        for which in range(2):
            pair_of(which, block).wait_send()
            for rightward in (True, False):

                @pl.when(block > spot if rightward else block < spot)
                def _():
                    flow_of(which, block, rightward, pairs[which][2]).wait_send()
        return 0

    lax.fori_loop(0, line, finish, 0)


def scatter_sums(part_a, part_b):
    devices = lax.axis_size("dp")
    line = devices // 2
    parts = [part.reshape(line, 2, part.shape[0] // devices, part.shape[1]) for part in (part_a, part_b)]
    scratch = []
    for part in parts:
        scratch += [pltpu.VMEM((line,) + part.shape[2:], part.dtype)] * 4
    scratch += [pltpu.SemaphoreType.DMA((2, line))] * 7
    return pl.pallas_call(
        functools.partial(scatter_kernel, line),
        out_shape=tuple(jax.ShapeDtypeStruct(part.shape[2:], jnp.float32) for part in parts),
        in_specs=[pl.BlockSpec(memory_space=pl.ANY)] * 2,
        out_specs=(VMEM,) * 2,
        scratch_shapes=scratch,
        compiler_params=pltpu.CompilerParams(
            collective_id=1, has_side_effects=True, vmem_limit_bytes=60 * 1024 * 1024
        ),
        name="scatter_sums",
    )(*parts)


def mask_of(segments):
    length = segments.shape[1]
    same = segments[:, :, None] == segments[:, None, :]
    positions = lax.broadcasted_iota(jnp.int32, (length, length), 0)
    columns = lax.broadcasted_iota(jnp.int32, (length, length), 1)
    counts = jnp.sum(same.astype(jnp.float32), axis=2, keepdims=True)
    allowed = jnp.logical_and(same, (columns <= positions)[None])
    return (allowed.astype(jnp.float32) / counts).reshape(-1, length)


def body(section_input, top_grad, w_in, w_out, segments):
    micro, length = segments.shape
    inputs = section_input[0]
    w_first = lax.all_gather(w_in[0], "dp", axis=0, tiled=True)
    w_mine, w_first = lax.optimization_barrier((w_out[0], w_first))
    w_second = lax.all_gather(w_mine, "dp", axis=0, tiled=True)
    mask = mask_of(segments)
    normed = norm_rows(inputs.astype(jnp.float32)).astype(jnp.bfloat16)
    preact = jnp.dot(normed, w_first, preferred_element_type=jnp.float32)
    activated = jax.nn.silu(preact).astype(jnp.bfloat16)
    scores, unit, rstd, gated = attend(activated, mask, micro, length)
    upstream, grad_preact, grads = chain(
        top_grad, inputs, activated, preact, scores, unit, rstd, mask, w_first, w_second, micro, length
    )
    part_out = contract_rows(gated, upstream).astype(jnp.bfloat16)
    part_in = contract_rows(normed, grad_preact).astype(jnp.bfloat16)
    grad_first, grad_out = scatter_sums(part_in, part_out)
    return (grads[None], grad_first[None], grad_out[None])


CORES = 2


class Place:
    def __init__(self):
        self.pipe, self.dp = lax.axis_index("pipe"), lax.axis_index("dp")
        self.x, self.core = self.pipe // CORES, self.pipe % CORES
        self.z, self.y = self.dp // CORES, self.dp % CORES

    def device(self, x=None, core=None, z=None, y=None, pipe=None):
        x = self.x if x is None else x
        core = self.core if core is None else core
        z = self.z if z is None else z
        y = self.y if y is None else y
        return {"pipe": x * CORES + core if pipe is None else pipe, "dp": z * CORES + y}


def signal(sem, device):
    pl.semaphore_signal(sem, inc=1, device_id=device, device_id_type=MESH)


def remote(src, dst, send, recv, device):
    return pltpu.make_async_remote_copy(
        src_ref=src, dst_ref=dst, send_sem=send, recv_sem=recv, device_id=device, device_id_type=MESH
    )


def either(local_if, local, far):
    pl.when(local_if)(local)
    pl.when(jnp.logical_not(local_if))(far)


def layer_order(step, z, layers):
    return jnp.where(2 * z < layers, (z + step) % layers, (z + layers - step) % layers)


def work_kernel(
    micro, length, layers,
    input_ref, top_ref, w_in_ref, w_out_ref, home_mask_ref,
    grads_ref, up_ref, gpre_ref, normed_ref, gated_ref,
    first, second, stage_first, stage_second, work_in, top, mask,
    unit_in, rstd_in, slope, act, weight, weight_slope, unit, rstd, mixed, landed, ggate, gnorm,
    swap_send, swap_recv, top_send, top_recv, pre_send, pre_recv, own_send, hop_send, to_core, to_x, to_y, came,
    chain_send, chain_recv,
):
    me = Place()
    width = work_in.shape[1]
    tokens = micro * length
    section = me.z
    other_x, other_core, other_y = 1 - me.x, 1 - me.core, 1 - me.y
    at_home = me.pipe == me.z
    is_last, is_first = section == layers - 1, section == 0
    weights = (
        (w_in_ref, first, stage_first),
        (w_out_ref, second, stage_second),
    )
    sizes = [ref.shape[0] // 4 for ref, _, _ in weights]

    def quarter(which, block, half, core):
        size = sizes[which]
        start = pl.multiple_of(((block * 2 + half) * CORES + core) * size, size)
        return weights[which][1].at[pl.ds(start, size), :]

    def shard(which, half, core):
        size = sizes[which]
        start = pl.multiple_of((half * CORES + core) * size, size)
        return weights[which][0].at[pl.ds(start, size), :]

    def came_at(which, block, half, core):
        return came.at[which, (block * 2 + half) * CORES + core]

    barrier = pltpu.get_barrier_semaphore()
    for layer in range(layers):
        for core in range(CORES):

            @pl.when(jnp.logical_not(jnp.logical_and(layer == me.z, core == me.core)))
            def _():
                signal(barrier, me.device(core=core, z=layer))

    for core in range(CORES):
        signal(barrier, me.device(x=other_x, core=core))
    signal(barrier, me.device(y=other_y))

    @pl.when(jnp.logical_not(at_home))
    def _():
        signal(barrier, {"pipe": me.z, "dp": me.pipe * CORES + me.y})

    pl.semaphore_wait(barrier, layers * CORES + 2 + jnp.where(at_home, 0, 1))

    swap = {"pipe": me.z, "dp": me.pipe * CORES + me.y}
    swaps = ((input_ref, work_in), (home_mask_ref, mask))

    def swap_far(index):
        src, dst = swaps[index]
        return remote(src, dst, swap_send.at[index], swap_recv.at[index], swap)

    def swap_near(index):
        src, dst = swaps[index]
        return pltpu.make_async_copy(src, dst, swap_recv.at[index])

    def swap_start():
        for index in range(2):
            either(at_home, lambda: swap_near(index).start(), lambda: swap_far(index).start())

    def before(which, core):
        return remote(
            shard(which, other_x, core), weights[which][2].at[me.core],
            pre_send.at[which, core], pre_recv.at[which, me.core], me.device(x=other_x, core=core),
        )

    def own(which, core):
        return remote(
            shard(which, me.x, core), quarter(which, me.dp, me.x, core),
            own_send.at[which, core], came_at(which, me.dp, me.x, core), me.device(core=core, z=me.pipe),
        )

    def own_near(which, core):
        return pltpu.make_async_copy(
            shard(which, me.x, core), quarter(which, me.dp, me.x, core), came_at(which, me.dp, me.x, core)
        )

    def hop(which, source):
        return remote(
            weights[which][2].at[source], quarter(which, me.dp, me.x, me.core),
            hop_send.at[which, source], came_at(which, me.dp, me.x, me.core),
            me.device(z=other_x * CORES + source),
        )

    def hop_near(which, source):
        return pltpu.make_async_copy(
            weights[which][2].at[source], quarter(which, me.dp, me.x, me.core),
            came_at(which, me.dp, me.x, me.core),
        )

    def before_came(which, source):
        return remote(
            shard(which, other_x, me.core), weights[which][2].at[source],
            pre_send.at[which, source], pre_recv.at[which, source], me.device(x=other_x),
        )

    for which in range(2):
        for core in range(CORES):
            before(which, core).start()
        for core in range(CORES):
            near = jnp.logical_and(at_home, core == me.core)
            either(near, lambda: own_near(which, core).start(), lambda: own(which, core).start())

    for which in range(2):
        for source in range(CORES):
            before_came(which, source).wait_recv()
            either(
                other_x * CORES + source == me.z,
                lambda: hop_near(which, source).start(),
                lambda: hop(which, source).start(),
            )

    top_far = remote(top_ref, top, top_send, top_recv, me.device(z=layers - 1))
    top_near = pltpu.make_async_copy(top_ref, top, top_recv)
    gives_top = jnp.logical_and(at_home, me.pipe < layers - 1)
    keeps_top = jnp.logical_and(at_home, me.pipe == layers - 1)

    def top_start():
        pl.when(gives_top)(lambda: top_far.start())
        pl.when(keeps_top)(lambda: top_near.start())

    def send(which, block, half, core, sem, index, device):
        place = quarter(which, block, half, core)
        return remote(place, place, sem.at[which, index], came_at(which, block, half, core), device)

    def direct_block(step):
        return layer_order(step, me.z, layers) * CORES + me.y

    def core_copy(which, kind, step):
        block = direct_block(step)
        lane = kind // 2
        block = block if lane == 0 else block - me.y + other_y
        half = me.x if kind % 2 == 0 else other_x
        return send(which, block, half, me.core, to_core, kind * layers + step, me.device(core=other_core))

    def x_copy(which, step):
        return send(which, direct_block(step), me.x, me.core, to_x, step, me.device(x=other_x))

    def y_copy(which, kind, step):
        half = me.x if kind == 0 else other_x
        return send(which, direct_block(step), half, me.core, to_y, kind * layers + step, me.device(y=other_y))

    def arrived(which, block, half, core):
        place = quarter(which, block, half, core)
        return remote(
            place, place, to_core.at[which, 0], came_at(which, block, half, core), me.device(core=other_core)
        )

    def settled(which):
        for core in range(CORES):
            near = jnp.logical_and(at_home, core == me.core)
            pl.when(jnp.logical_not(near))(lambda: own(which, core).wait_send())
        for source in range(CORES):
            near = other_x * CORES + source == me.z
            pl.when(jnp.logical_not(near))(lambda: hop(which, source).wait_send())

    for step in range(layers + 2):
        if step == 2:
            for which in range(2):
                settled(which)
            swap_start()
            top_start()
        for which in range(2):
            if step < layers:
                block = direct_block(step)
                if step == 0:
                    far = jnp.logical_and(me.x == me.z // CORES, me.core != me.z % CORES)
                    place = quarter(which, block, me.x, me.core)
                    either(
                        jnp.logical_not(far),
                        lambda: pltpu.make_async_copy(
                            shard(which, 0, 0), place, came_at(which, block, me.x, me.core)
                        ).wait(),
                        lambda: arrived(which, block, me.x, me.core).wait_recv(),
                    )
                else:
                    arrived(which, block, me.x, me.core).wait_recv()
                x_copy(which, step).start()
                y_copy(which, 0, step).start()
                core_copy(which, 0, step).start()
        for which in range(2):
            if 1 <= step <= layers:
                block = direct_block(step - 1)
                arrived(which, block, other_x, me.core).wait_recv()
                y_copy(which, 1, step - 1).start()
                core_copy(which, 1, step - 1).start()
                arrived(which, block - me.y + other_y, me.x, me.core).wait_recv()
                core_copy(which, 2, step - 1).start()
        for which in range(2):
            if step >= 2:
                block = direct_block(step - 2)
                arrived(which, block - me.y + other_y, other_x, me.core).wait_recv()
                core_copy(which, 3, step - 2).start()

    for index in range(2):
        either(at_home, lambda: swap_near(index).wait(), lambda: swap_far(index).wait_recv())

    for which in range(2):
        def landed_all(index, _):
            block, half = index // 2, index % 2
            arrived(which, block, half, other_core).wait_recv()
            return 0

        lax.fori_loop(0, 2 * layers * CORES, landed_all, 0)

    norm_input(work_in, normed_ref, unit_in, rstd_in)
    tile = 2 * LANES

    def front(index, _):
        cols = at(index * tile, tile)
        value = dot_nn(normed_ref[...], first[:, cols])
        squash = jax.nn.sigmoid(value)
        act[:, cols] = (value * squash).astype(jnp.bfloat16)
        slope[:, cols] = squash * (1.0 + value * (1.0 - squash))
        return 0

    lax.fori_loop(0, slope.shape[1] // tile, front, 0)
    attend_front(micro, length, act, mask, weight, weight_slope, unit, rstd, gated_ref, mixed)

    def copy_of(slot):
        return remote(
            grads_ref.at[pl.ds(slot * length, length), :], landed.at[slot], chain_send.at[slot], chain_recv.at[slot],
            me.device(z=jnp.maximum(me.z - 1, 0)),
        )

    @pl.when(jnp.logical_and(is_last, jnp.logical_not(at_home)))
    def _():
        top_far.wait_recv()

    @pl.when(keeps_top)
    def _():
        top_near.wait()

    chain_steps(
        micro, length, is_first, is_last, copy_of,
        top, unit_in, rstd_in, act, slope, weight, weight_slope, unit, rstd, first, second,
        grads_ref, up_ref, gpre_ref, landed, ggate, gnorm,
    )

    for slot in range(micro):

        @pl.when(jnp.logical_not(is_first))
        def _():
            copy_of(slot).wait_send()

    for index in range(2):
        pl.when(jnp.logical_not(at_home))(lambda: swap_far(index).wait_send())
    pl.when(gives_top)(lambda: top_far.wait_send())
    for which in range(2):
        for core in range(CORES):
            before(which, core).wait_send()

        def sent(step, _):
            x_copy(which, step).wait_send()
            for kind in range(2):
                y_copy(which, kind, step).wait_send()
            for kind in range(4):
                core_copy(which, kind, step).wait_send()
            return 0

        lax.fori_loop(0, layers, sent, 0)


def folded(value):
    total = value[:, :LANES]
    for start in range(LANES, value.shape[1], LANES):
        total = total + value[:, start : start + LANES]
    return total


def norm_input(work_in, normed_ref, unit_in, rstd_in):
    step = 64
    width = work_in.shape[1]

    def one(index, _):
        rows = pl.ds(pl.multiple_of(index * step, step), step)
        value = work_in[rows, :].astype(jnp.float32)
        center = value - jnp.mean(value, axis=-1, keepdims=True)
        rstd = lax.rsqrt(jnp.mean(center * center, axis=-1, keepdims=True) + EPSILON)
        unit = center * rstd
        unit_in[rows, :] = unit
        normed_ref[rows, :] = unit.astype(jnp.bfloat16)
        rstd_in[rows, :] = jnp.broadcast_to(rstd, (step, LANES))
        return 0

    lax.fori_loop(0, work_in.shape[0] // step, one, 0)


def attend_front(micro, length, act_ref, mask_ref, weight_ref, slope_ref, unit_ref, rstd_ref, gated_ref, mixed):
    lane = lax.broadcasted_iota(jnp.int32, (length, LANES), 1)

    def one(index, _):
        slot, group = index // GROUPS, index % GROUPS
        rows = at(slot * length, length)
        queries = act_ref[rows, at(2 * V_COLS + group * LANES, LANES)]
        keys = act_ref[rows, at(2 * V_COLS + Q_COLS + group * LANES, LANES)]
        mask = mask_ref[rows, :]
        for half in range(GROUP_V // LANES):
            cols = group * GROUP_V + half * LANES
            values = act_ref[rows, at(V_COLS + cols, LANES)]
            total = jnp.zeros((length, LANES), jnp.float32)
            for sub in range(V_HEADS):
                head = half * V_HEADS + sub
                score = dot_nt(only_head(queries, lane, QK_DIM, head), keys) * SCALE
                squash = jax.nn.sigmoid(score)
                place = at((index * QK_HEADS + head) * length, length)
                slope_ref[place, :] = squash * (1.0 + score * (1.0 - squash)) * (mask * SCALE)
                weight = (score * squash * mask).astype(jnp.bfloat16)
                weight_ref[place, :] = weight
                total += dot_nn(weight, only_head(values, lane, V_DIM, sub))
            mixed[rows, at(cols, LANES)] = total
        return 0

    lax.fori_loop(0, micro * GROUPS, one, 0)
    step = 64

    def finish(index, _):
        rows = pl.ds(pl.multiple_of(index * step, step), step)
        value = mixed[rows, :]
        center = value - jnp.mean(value, axis=-1, keepdims=True)
        rstd = lax.rsqrt(jnp.mean(center * center, axis=-1, keepdims=True) + EPSILON)
        unit = center * rstd
        unit_ref[rows, :] = unit
        rstd_ref[rows, :] = jnp.broadcast_to(rstd, (step, LANES))
        gated_ref[rows, :] = (unit * act_ref[rows, :V_COLS].astype(jnp.float32)).astype(jnp.bfloat16)
        return 0

    lax.fori_loop(0, micro * length // step, finish, 0)


def chain_steps(
    micro, length, is_first, is_last, copy_of,
    top_ref, unit_in, rstd_in, act_ref, slope_ref, weight_ref, weight_slope, unit_ref, rstd_ref, first_ref, second_ref,
    grads_ref, up_ref, gpre_ref, landed, ggate, gnorm,
):
    width = unit_in.shape[1]
    tile = 2 * LANES
    lane = lax.broadcasted_iota(jnp.int32, (length, LANES), 1)
    nothing = jnp.zeros((length, LANES), jnp.float32)

    def store_grad(rows, cols, size, value):
        rounded = value.astype(jnp.bfloat16).astype(jnp.float32)
        gpre_ref[rows, at(cols, size)] = (rounded * slope_ref[rows, at(cols, size)]).astype(jnp.bfloat16)

    for slot in range(micro):
        rows = pl.ds(slot * length, length)

        @pl.when(is_last)
        def _():
            up_ref[rows, :] = top_ref[rows, :]

        @pl.when(jnp.logical_not(is_last))
        def _():
            copy_of(slot).wait_recv()
            up_ref[rows, :] = landed[slot]

        def gate_tile(index, sums):
            cols = at(index * tile, tile)
            grad = dot_nt(up_ref[rows, :], second_ref[cols, :])
            unit = unit_ref[rows, cols]
            store_grad(rows, index * tile, tile, grad * unit)
            grad = grad * act_ref[rows, cols].astype(jnp.float32)
            ggate[:, cols] = grad
            return sums[0] + folded(grad), sums[1] + folded(grad * unit)

        sums = lax.fori_loop(0, V_COLS // tile, gate_tile, (nothing, nothing))
        mean_grad, mean_unit = [jnp.sum(part, axis=-1, keepdims=True) * (1.0 / V_COLS) for part in sums]
        rstd = rstd_ref[rows, :1]

        def one(group, _):
            queries = act_ref[rows, at(2 * V_COLS + group * LANES, LANES)]
            keys = act_ref[rows, at(2 * V_COLS + Q_COLS + group * LANES, LANES)]
            grad_q = jnp.zeros((length, LANES), jnp.float32)
            grad_k = jnp.zeros((length, LANES), jnp.float32)
            for half in range(GROUP_V // LANES):
                cols = group * GROUP_V + half * LANES
                values = act_ref[rows, at(V_COLS + cols, LANES)]
                spread = ggate[:, at(cols, LANES)] - mean_grad - unit_ref[rows, at(cols, LANES)] * mean_unit
                grad_mix = (rstd * spread).astype(jnp.bfloat16)
                grad_v = jnp.zeros((length, LANES), jnp.float32)
                for sub in range(V_HEADS):
                    head = half * V_HEADS + sub
                    mix_head = only_head(grad_mix, lane, V_DIM, sub)
                    place = at((slot * HEADS + group * QK_HEADS + head) * length, length)
                    grad_score = (dot_nt(mix_head, values) * weight_slope[place, :]).astype(jnp.bfloat16)
                    grad_v += contract_rows(weight_ref[place, :], mix_head)
                    grad_q += dot_nn(grad_score, only_head(keys, lane, QK_DIM, head))
                    grad_k += contract_rows(grad_score, only_head(queries, lane, QK_DIM, head))
                store_grad(rows, V_COLS + cols, LANES, grad_v)
            store_grad(rows, 2 * V_COLS + group * LANES, LANES, grad_q)
            store_grad(rows, 2 * V_COLS + Q_COLS + group * LANES, LANES, grad_k)
            return 0

        lax.fori_loop(0, GROUPS, one, 0)

        def norm_tile(index, sums):
            cols = at(index * tile, tile)
            grad = dot_nt(gpre_ref[rows, :], first_ref[cols, :])
            gnorm[:, cols] = grad
            return sums[0] + folded(grad), sums[1] + folded(grad * unit_in[rows, cols])

        sums = lax.fori_loop(0, width // tile, norm_tile, (nothing, nothing))
        mean_grad, mean_unit = [jnp.sum(part, axis=-1, keepdims=True) * (1.0 / width) for part in sums]
        rstd = rstd_in[rows, :1]

        def pass_tile(index, _):
            cols = at(index * tile, tile)
            through = rstd * (gnorm[:, cols] - mean_grad - unit_in[rows, cols] * mean_unit)
            grads_ref[rows, cols] = (up_ref[rows, cols].astype(jnp.float32) + through).astype(jnp.bfloat16)
            return 0

        lax.fori_loop(0, width // tile, pass_tile, 0)

        @pl.when(jnp.logical_not(is_first))
        def _():
            copy_of(slot).start()


ANY = pl.BlockSpec(memory_space=pl.ANY)
LIMIT = 60 * 1024 * 1024


def work(inputs, top_grad, w_in, w_out, mask, micro, length):
    tokens, width = inputs.shape
    layers, blocks = lax.axis_size("pipe"), lax.axis_size("dp")
    columns = w_in.shape[1]
    quarters = [w.shape[0] // 4 for w in (w_in, w_out)]
    dma = pltpu.SemaphoreType.DMA
    return pl.pallas_call(
        functools.partial(work_kernel, micro, length, layers),
        out_shape=(
            jax.ShapeDtypeStruct((tokens, width), jnp.bfloat16),
            jax.ShapeDtypeStruct((tokens, width), jnp.bfloat16),
            jax.ShapeDtypeStruct((tokens, columns), jnp.bfloat16),
            jax.ShapeDtypeStruct((tokens, width), jnp.bfloat16),
            jax.ShapeDtypeStruct((tokens, V_COLS), jnp.bfloat16),
        ),
        in_specs=[ANY] * 5,
        out_specs=(VMEM,) * 5,
        scratch_shapes=[
            pltpu.VMEM((blocks * w_in.shape[0], columns), jnp.bfloat16),
            pltpu.VMEM((blocks * w_out.shape[0], width), jnp.bfloat16),
            pltpu.VMEM((CORES, quarters[0], columns), jnp.bfloat16),
            pltpu.VMEM((CORES, quarters[1], width), jnp.bfloat16),
            pltpu.VMEM((tokens, width), jnp.bfloat16),
            pltpu.VMEM((tokens, width), jnp.bfloat16),
            pltpu.VMEM((tokens, length), jnp.float32),
            pltpu.VMEM((tokens, width), jnp.float32),
            pltpu.VMEM((tokens, LANES), jnp.float32),
            pltpu.VMEM((tokens, columns), jnp.float32),
            pltpu.VMEM((tokens, columns), jnp.bfloat16),
            pltpu.VMEM((micro * HEADS * length, length), jnp.bfloat16),
            pltpu.VMEM((micro * HEADS * length, length), jnp.float32),
            pltpu.VMEM((tokens, V_COLS), jnp.float32),
            pltpu.VMEM((tokens, LANES), jnp.float32),
            pltpu.VMEM((tokens, V_COLS), jnp.float32),
            pltpu.VMEM((micro, length, width), jnp.bfloat16),
            pltpu.VMEM((length, V_COLS), jnp.float32),
            pltpu.VMEM((length, width), jnp.float32),
            dma((2,)), dma((2,)), dma, dma,
            dma((2, CORES)), dma((2, CORES)), dma((2, CORES)), dma((2, CORES)),
            dma((2, 4 * layers)), dma((2, layers)), dma((2, 2 * layers)), dma((2, 4 * blocks)),
            dma((micro,)), dma((micro,)),
        ],
        compiler_params=pltpu.CompilerParams(collective_id=2, has_side_effects=True, vmem_limit_bytes=LIMIT),
        name="work",
    )(inputs, top_grad, w_in, w_out, mask)


def add_rows(target, other):
    step = 16

    def one(index, _):
        rows = pl.ds(pl.multiple_of(index * step, step), step)
        total = target[rows, :].astype(jnp.float32) + other[rows, :].astype(jnp.float32)
        target[rows, :] = total.astype(target.dtype)
        return 0

    lax.fori_loop(0, target.shape[0] // step, one, 0)


def weight_kernel(
    layers,
    normed_ref, gpre_ref, gated_ref, up_ref, done_ref,
    out_first, out_second, grads_ref,
    first, second, core_first, core_second, y_first, y_second, x_first, x_second,
    core_send, core_recv, y_send, y_recv, x_send, x_recv, home_send, home_recv,
    back_send, back_recv,
):
    me = Place()
    other_x, other_core, other_y = 1 - me.x, 1 - me.core, 1 - me.y
    at_home = me.pipe == me.z
    sets = (
        (normed_ref, gpre_ref, out_first, first, core_first, y_first, x_first),
        (gated_ref, up_ref, out_second, second, core_second, y_second, x_second),
    )
    sizes = [s[2].shape[0] // 4 for s in sets]

    barrier = pltpu.get_barrier_semaphore()
    signal(barrier, me.device(core=other_core))
    signal(barrier, me.device(x=other_x))
    signal(barrier, me.device(y=other_y))
    for pipe in range(layers):

        @pl.when(jnp.logical_not(jnp.logical_and(at_home, pipe == me.pipe)))
        def _():
            signal(barrier, {"pipe": pipe, "dp": me.pipe * CORES + me.y})

    pl.semaphore_wait(barrier, 3 + layers - jnp.where(at_home, 1, 0))

    back_far = remote(done_ref, grads_ref, back_send, back_recv, {"pipe": me.z, "dp": me.pipe * CORES + me.y})
    back_near = pltpu.make_async_copy(done_ref, grads_ref, back_recv)
    either(at_home, lambda: back_near.start(), lambda: back_far.start())

    def quarter(which, block, half, core):
        size = sizes[which]
        start = pl.multiple_of(((block * 2 + half) * CORES + core) * size, size)
        return sets[which][3].at[pl.ds(start, size), :]

    def core_copy(which, block, half, mine):
        core = me.core if mine else other_core
        index = block * 2 + half
        return remote(
            quarter(which, block, half, core), sets[which][4].at[index],
            core_send.at[which, index], core_recv.at[which, index], me.device(core=other_core),
        )

    def y_copy(which, row, half, mine):
        block = row * CORES + (me.y if mine else other_y)
        index = row * 2 + half
        return remote(
            quarter(which, block, half, me.core), sets[which][5].at[index],
            y_send.at[which, index], y_recv.at[which, index], me.device(y=other_y),
        )

    def x_copy(which, row, mine):
        block = row * CORES + me.y
        return remote(
            quarter(which, block, me.x if mine else other_x, me.core), sets[which][6].at[row],
            x_send.at[which, row], x_recv.at[which, row], me.device(x=other_x),
        )

    def home_rows(which, half, core):
        size = sizes[which]
        return sets[which][2].at[pl.ds(pl.multiple_of((half * CORES + core) * size, size), size), :]

    def home_copy(which, row):
        return remote(
            quarter(which, row * CORES + me.y, me.x, me.core), home_rows(which, me.x, me.core),
            home_send.at[which, row], home_recv.at[which, me.x * CORES + me.core],
            {"pipe": me.z, "dp": row * CORES + me.y},
        )

    def home_near(which):
        return pltpu.make_async_copy(
            quarter(which, me.dp, me.x, me.core), home_rows(which, me.x, me.core),
            home_recv.at[which, me.x * CORES + me.core],
        )

    def row_at(step):
        return layer_order(layers - 1 - step, me.z, layers)

    def product(which, row):
        left, right, _, whole = sets[which][:4]
        size = 4 * sizes[which]
        tile = 2 * LANES
        for lane_of in (other_y, me.y):
            block = row * CORES + lane_of
            place = pl.ds(pl.multiple_of(block * size, size), size)

            def one(index, _):
                cols = at(index * tile, tile)
                whole[place, cols] = contract_rows(left[:, place], right[:, cols]).astype(whole.dtype)
                return 0

            lax.fori_loop(0, right.shape[1] // tile, one, 0)
            for half in range(2):
                core_copy(which, block, half, False).start()

    def fold_y(which, row):
        for half in range(2):
            block = row * CORES + other_y
            core_copy(which, block, half, True).wait_recv()
            add_rows(quarter(which, block, half, me.core), sets[which][4].at[block * 2 + half])
            y_copy(which, row, half, False).start()

    def fold_x(which, row):
        for half in (other_x, me.x):
            block = row * CORES + me.y
            core_copy(which, block, half, True).wait_recv()
            place = quarter(which, block, half, me.core)
            add_rows(place, sets[which][4].at[block * 2 + half])
            y_copy(which, row, half, True).wait_recv()
            add_rows(place, sets[which][5].at[row * 2 + half])

            @pl.when(half == other_x)
            def _():
                x_copy(which, row, False).start()

    def fold_home(which, row):
        x_copy(which, row, True).wait_recv()
        add_rows(quarter(which, row * CORES + me.y, me.x, me.core), sets[which][6].at[row])
        near = jnp.logical_and(at_home, row == me.z)
        either(near, lambda: home_near(which).start(), lambda: home_copy(which, row).start())

    def run(step, _):
        for which in range(2):

            @pl.when(step < layers)
            def _():
                product(which, row_at(step))

            @pl.when(jnp.logical_and(step >= 1, step < layers + 1))
            def _():
                fold_y(which, row_at(step - 1))

            @pl.when(jnp.logical_and(step >= 2, step < layers + 2))
            def _():
                fold_x(which, row_at(step - 2))

            @pl.when(step >= 3)
            def _():
                fold_home(which, row_at(step - 3))

        return 0

    lax.fori_loop(0, layers + 3, run, 0)
    either(at_home, lambda: back_near.wait(), lambda: back_far.wait())

    for which in range(2):
        for pipe in range(layers):
            place = home_rows(which, pipe // CORES, pipe % CORES)
            near = jnp.logical_and(at_home, pipe == me.pipe)
            either(
                near,
                lambda: home_near(which).wait(),
                lambda: remote(
                    place, place, home_send.at[which, 0], home_recv.at[which, pipe], me.device(core=other_core)
                ).wait_recv(),
            )

        def sent(row, _):
            for half in range(2):
                for lane_of in range(2):
                    core_copy(which, row * CORES + lane_of, half, False).wait_send()
                y_copy(which, row, half, False).wait_send()
            x_copy(which, row, False).wait_send()
            near = jnp.logical_and(at_home, row == me.z)
            pl.when(jnp.logical_not(near))(lambda: home_copy(which, row).wait_send())
            return 0

        lax.fori_loop(0, layers, sent, 0)


def weight_sums(normed, grad_preact, gated, upstream, grads):
    layers, blocks = lax.axis_size("pipe"), lax.axis_size("dp")
    dma = pltpu.SemaphoreType.DMA
    pairs = ((normed, grad_preact), (gated, upstream))
    shapes = [(left.shape[1], right.shape[1]) for left, right in pairs]
    scratch = [pltpu.VMEM(shape, jnp.bfloat16) for shape in shapes]
    for count in (2 * blocks, 2 * layers, layers):
        for rows, cols in shapes:
            scratch.append(pltpu.VMEM((count, rows // (4 * blocks), cols), jnp.bfloat16))
    for count in (2 * blocks, 2 * layers, layers, layers):
        scratch += [dma((2, count))] * 2
    scratch += [dma, dma]
    return pl.pallas_call(
        functools.partial(weight_kernel, layers),
        out_shape=tuple(jax.ShapeDtypeStruct((rows // blocks, cols), jnp.bfloat16) for rows, cols in shapes)
        + (jax.ShapeDtypeStruct(grads.shape, grads.dtype),),
        in_specs=[VMEM] * 4 + [ANY],
        out_specs=(ANY,) * 3,
        scratch_shapes=scratch,
        compiler_params=pltpu.CompilerParams(collective_id=3, has_side_effects=True, vmem_limit_bytes=LIMIT),
        name="weight_sums",
    )(normed, grad_preact, gated, upstream, grads)


def layered_body(section_input, top_grad, w_in, w_out, segments):
    micro, length = segments.shape
    mask = mask_of(segments)
    grads, upstream, grad_preact, normed, gated = work(
        section_input[0], top_grad, w_in[0], w_out[0], mask, micro, length
    )
    grad_first, grad_out, grads = weight_sums(normed, grad_preact, gated, upstream, grads)
    return (grads[None], grad_first.astype(jnp.float32)[None], grad_out.astype(jnp.float32)[None])


def solution(mesh):
    layered = mesh.shape["pipe"] == CORES * 2 and mesh.shape["dp"] == CORES * mesh.shape["pipe"]
    return jax.shard_map(
        layered_body if layered else body,
        mesh=mesh,
        in_specs=(
            P("pipe", "dp", None),
            P("dp", None),
            P("pipe", "dp", None),
            P("pipe", "dp", None),
            P("dp", None),
        ),
        out_specs=(P("pipe", "dp", None), P("pipe", "dp", None), P("pipe", "dp", None)),
        check_vma=False,
    )
```

```python
import functools

import jax
import jax.numpy as jnp
from jax import lax
from jax.experimental import pallas as pl
from jax.experimental.pallas import tpu as pltpu
from jax.sharding import PartitionSpec as P

HEADS = 16
QK_DIM = 32
V_DIM = 64
LANES = 128

EPSILON = 1e-05
MESH = pl.DeviceIdType.MESH
VMEM = pl.BlockSpec(memory_space=pltpu.VMEM)

QK_HEADS = LANES // QK_DIM
V_HEADS = LANES // V_DIM
GROUPS = HEADS // QK_HEADS
V_COLS = HEADS * V_DIM
Q_COLS = HEADS * QK_DIM
GROUP_V = QK_HEADS * V_DIM
SCALE = QK_DIM ** (-0.5)


def norm_rows(values):
    center = values - jnp.mean(values, axis=-1, keepdims=True)
    return center * lax.rsqrt(jnp.mean(center * center, axis=-1, keepdims=True) + EPSILON)


def silu_slope(preact):
    squash = jax.nn.sigmoid(preact)
    return squash * (1.0 + preact * (1.0 - squash))


def dot_nt(left, right):
    return lax.dot_general(
        left, right, (((1,), (1,)), ((), ())), preferred_element_type=jnp.float32
    )


def dot_nn(left, right):
    return lax.dot_general(
        left, right, (((1,), (0,)), ((), ())), preferred_element_type=jnp.float32
    )


def contract_rows(left, right):
    return lax.dot_general(
        left, right, (((0,), (0,)), ((), ())), preferred_element_type=jnp.float32
    )


def only_head(block, lane, width, index):
    keep = jnp.logical_and(lane >= index * width, lane < (index + 1) * width)
    return jnp.where(keep, block, jnp.zeros_like(block))


def at(start, size):
    return pl.ds(pl.multiple_of(start, LANES), size)


def attend_kernel(micro, length, act_ref, mask_ref, score_ref, unit_ref, rstd_ref, gated_ref, mixed):
    lane = lax.broadcasted_iota(jnp.int32, (length, LANES), 1)

    def one(index, _):
        slot, group = index // GROUPS, index % GROUPS
        rows = at(slot * length, length)
        queries = act_ref[rows, at(2 * V_COLS + group * LANES, LANES)]
        keys = act_ref[rows, at(2 * V_COLS + Q_COLS + group * LANES, LANES)]
        mask = mask_ref[rows, :]
        for half in range(GROUP_V // LANES):
            cols = group * GROUP_V + half * LANES
            values = act_ref[rows, at(V_COLS + cols, LANES)]
            total = jnp.zeros((length, LANES), jnp.float32)
            for sub in range(V_HEADS):
                head = half * V_HEADS + sub
                score = dot_nt(only_head(queries, lane, QK_DIM, head), keys) * SCALE
                score_ref[at((index * QK_HEADS + head) * length, length), :] = score
                weight = (jax.nn.silu(score) * mask).astype(jnp.bfloat16)
                total += dot_nn(weight, only_head(values, lane, V_DIM, sub))
            mixed[rows, at(cols, LANES)] = total
        return 0

    lax.fori_loop(0, micro * GROUPS, one, 0)

    def finish(slot, _):
        rows = at(slot * length, length)
        value = mixed[rows, :]
        center = value - jnp.mean(value, axis=-1, keepdims=True)
        rstd = lax.rsqrt(jnp.mean(center * center, axis=-1, keepdims=True) + EPSILON)
        unit = center * rstd
        unit_ref[rows, :] = unit
        rstd_ref[rows, :] = jnp.broadcast_to(rstd, (length, LANES))
        gated_ref[rows, :] = (unit * act_ref[rows, :V_COLS].astype(jnp.float32)).astype(jnp.bfloat16)
        return 0

    lax.fori_loop(0, micro, finish, 0)


def attend(activated, mask, micro, length):
    tokens = micro * length
    return pl.pallas_call(
        functools.partial(attend_kernel, micro, length),
        out_shape=(
            jax.ShapeDtypeStruct((micro * HEADS * length, length), jnp.float32),
            jax.ShapeDtypeStruct((tokens, V_COLS), jnp.float32),
            jax.ShapeDtypeStruct((tokens, LANES), jnp.float32),
            jax.ShapeDtypeStruct((tokens, V_COLS), jnp.bfloat16),
        ),
        in_specs=[VMEM] * 2,
        out_specs=(VMEM,) * 4,
        scratch_shapes=[pltpu.VMEM((tokens, V_COLS), jnp.float32)],
        name="attend",
    )(activated, mask)


def chain_kernel(
    micro, length, sections,
    top_ref, input_ref, act_ref, pre_ref, score_ref, unit_ref, rstd_ref, mask_ref, first_ref, second_ref,
    up_ref, gpre_ref, gin_ref,
    landed, leaving, ggate, dmix, gnorm, send_sem, recv_sem,
):
    section = lax.axis_index("pipe")
    width = input_ref.shape[1]
    tile = 2 * LANES
    lane = lax.broadcasted_iota(jnp.int32, (length, LANES), 1)
    is_last = section == sections - 1
    is_first = section == 0

    barrier = pltpu.get_barrier_semaphore()

    @pl.when(jnp.logical_not(is_last))
    def _():
        pl.semaphore_signal(
            barrier, inc=1, device_id={"pipe": jnp.minimum(section + 1, sections - 1)}, device_id_type=MESH
        )

    @pl.when(jnp.logical_not(is_first))
    def _():
        pl.semaphore_wait(barrier, 1)

    def copy_of(slot):
        return pltpu.make_async_remote_copy(
            src_ref=leaving.at[slot],
            dst_ref=landed.at[slot],
            send_sem=send_sem.at[slot],
            recv_sem=recv_sem.at[slot],
            device_id={"pipe": jnp.maximum(section - 1, 0)},
            device_id_type=MESH,
        )

    def store_grad(rows, cols, size, value):
        rounded = value.astype(jnp.bfloat16).astype(jnp.float32)
        gpre_ref[rows, at(cols, size)] = (
            rounded * silu_slope(pre_ref[rows, at(cols, size)])
        ).astype(jnp.bfloat16)

    for slot in range(micro):
        rows = pl.ds(slot * length, length)

        @pl.when(is_last)
        def _():
            up_ref[rows, :] = top_ref[rows, :]

        @pl.when(jnp.logical_not(is_last))
        def _():
            copy_of(slot).wait_recv()
            up_ref[rows, :] = landed[slot]

        def gate_tile(index, _):
            ggate[:, at(index * tile, tile)] = dot_nt(up_ref[rows, :], second_ref[at(index * tile, tile), :])
            return 0

        lax.fori_loop(0, V_COLS // tile, gate_tile, 0)
        gating = act_ref[rows, :V_COLS].astype(jnp.float32)
        unit = unit_ref[rows, :]
        grad = ggate[...]
        store_grad(rows, 0, V_COLS, grad * unit)
        grad = grad * gating
        mean_grad = jnp.mean(grad, axis=-1, keepdims=True)
        mean_unit = jnp.mean(grad * unit, axis=-1, keepdims=True)
        dmix[...] = (rstd_ref[rows, :1] * (grad - mean_grad - unit * mean_unit)).astype(jnp.bfloat16)

        def one(group, _):
            queries = act_ref[rows, at(2 * V_COLS + group * LANES, LANES)]
            keys = act_ref[rows, at(2 * V_COLS + Q_COLS + group * LANES, LANES)]
            mask = mask_ref[rows, :]
            grad_q = jnp.zeros((length, LANES), jnp.float32)
            grad_k = jnp.zeros((length, LANES), jnp.float32)
            for half in range(GROUP_V // LANES):
                cols = group * GROUP_V + half * LANES
                values = act_ref[rows, at(V_COLS + cols, LANES)]
                grad_mix = dmix[:, at(cols, LANES)]
                grad_v = jnp.zeros((length, LANES), jnp.float32)
                for sub in range(V_HEADS):
                    head = half * V_HEADS + sub
                    mix_head = only_head(grad_mix, lane, V_DIM, sub)
                    place = (slot * HEADS + group * QK_HEADS + head) * length
                    score = score_ref[at(place, length), :]
                    squash = jax.nn.sigmoid(score)
                    weight = (score * squash * mask).astype(jnp.bfloat16)
                    slope = squash * (1.0 + score * (1.0 - squash)) * mask * SCALE
                    grad_score = (dot_nt(mix_head, values) * slope).astype(jnp.bfloat16)
                    grad_v += contract_rows(weight, mix_head)
                    grad_q += dot_nn(grad_score, only_head(keys, lane, QK_DIM, head))
                    grad_k += contract_rows(grad_score, only_head(queries, lane, QK_DIM, head))
                store_grad(rows, V_COLS + cols, LANES, grad_v)
            store_grad(rows, 2 * V_COLS + group * LANES, LANES, grad_q)
            store_grad(rows, 2 * V_COLS + Q_COLS + group * LANES, LANES, grad_k)
            return 0

        lax.fori_loop(0, GROUPS, one, 0)

        def norm_tile(index, _):
            gnorm[:, at(index * tile, tile)] = dot_nt(gpre_ref[rows, :], first_ref[at(index * tile, tile), :])
            return 0

        lax.fori_loop(0, width // tile, norm_tile, 0)
        value = input_ref[rows, :].astype(jnp.float32)
        center = value - jnp.mean(value, axis=-1, keepdims=True)
        rstd = lax.rsqrt(jnp.mean(center * center, axis=-1, keepdims=True) + EPSILON)
        unit = center * rstd
        grad = gnorm[...]
        mean_grad = jnp.mean(grad, axis=-1, keepdims=True)
        mean_unit = jnp.mean(grad * unit, axis=-1, keepdims=True)
        through = rstd * (grad - mean_grad - unit * mean_unit)
        result = (up_ref[rows, :].astype(jnp.float32) + through).astype(jnp.bfloat16)
        leaving[slot] = result
        gin_ref[rows, :] = result

        @pl.when(jnp.logical_not(is_first))
        def _():
            copy_of(slot).start()

    for slot in range(micro):

        @pl.when(jnp.logical_not(is_first))
        def _():
            copy_of(slot).wait_send()


def chain(top, inputs, activated, preact, scores, unit, rstd, mask, w_first, w_second, micro, length):
    tokens, width = inputs.shape
    return pl.pallas_call(
        functools.partial(chain_kernel, micro, length, lax.axis_size("pipe")),
        out_shape=(
            jax.ShapeDtypeStruct((tokens, width), jnp.bfloat16),
            jax.ShapeDtypeStruct(preact.shape, jnp.bfloat16),
            jax.ShapeDtypeStruct((tokens, width), jnp.bfloat16),
        ),
        in_specs=[VMEM] * 10,
        out_specs=(VMEM,) * 3,
        scratch_shapes=[
            pltpu.VMEM((micro, length, width), jnp.bfloat16),
            pltpu.VMEM((micro, length, width), jnp.bfloat16),
            pltpu.VMEM((length, V_COLS), jnp.float32),
            pltpu.VMEM((length, V_COLS), jnp.bfloat16),
            pltpu.VMEM((length, width), jnp.float32),
            pltpu.SemaphoreType.DMA((micro,)),
            pltpu.SemaphoreType.DMA((micro,)),
        ],
        compiler_params=pltpu.CompilerParams(
            collective_id=0, has_side_effects=True, vmem_limit_bytes=60 * 1024 * 1024
        ),
        name="chain",
    )(top, inputs, activated, preact, scores, unit, rstd, mask, w_first, w_second)


def add_into(target, left, right):
    step = 32

    def one(index, _):
        rows = pl.ds(pl.multiple_of(index * step, step), step)
        total = left[rows, :].astype(jnp.float32) + right[rows, :].astype(jnp.float32)
        target[rows, :] = total.astype(target.dtype)
        return 0

    lax.fori_loop(0, target.shape[0] // step, one, 0)


def scatter_kernel(line, part_a, part_b, out_a, out_b, *scratch):
    pairs = (
        (part_a, out_a) + scratch[0:4],
        (part_b, out_b) + scratch[4:8],
    )
    load_sem, pair_send, pair_recv, right_send, right_recv, left_send, left_recv = scratch[8:]
    rank = lax.axis_index("dp")
    spot, lane_of = rank // 2, rank % 2
    has_left, has_right = spot > 0, spot < line - 1
    partner = spot * 2 + 1 - lane_of
    right = jnp.minimum(spot + 1, line - 1) * 2 + lane_of
    left = jnp.maximum(spot - 1, 0) * 2 + lane_of

    barrier = pltpu.get_barrier_semaphore()
    pl.semaphore_signal(barrier, inc=1, device_id={"dp": partner}, device_id_type=MESH)

    @pl.when(has_left)
    def _():
        pl.semaphore_signal(barrier, inc=1, device_id={"dp": left}, device_id_type=MESH)

    @pl.when(has_right)
    def _():
        pl.semaphore_signal(barrier, inc=1, device_id={"dp": right}, device_id_type=MESH)

    pl.semaphore_wait(barrier, 1 + jnp.minimum(spot, 1) + jnp.minimum(line - 1 - spot, 1))

    def block_at(turn):
        near = jnp.minimum(spot, line - 1 - spot)
        ahead = line - 1 - 2 * near
        lone = jnp.where(spot <= line - 1 - spot, line - 1 - turn, turn)
        after = jnp.maximum(turn - ahead, 0)
        reach = near - after // 2
        both = jnp.where(after % 2 == 0, spot + reach, spot - reach)
        return jnp.where(turn < ahead, lone, both)

    def load_of(which, block):
        part, _, own, _, _, _ = pairs[which]
        return pltpu.make_async_copy(part.at[block, lane_of], own.at[block], load_sem.at[which, block])

    def pair_of(which, block):
        part, _, _, paired, _, _ = pairs[which]
        return pltpu.make_async_remote_copy(
            src_ref=part.at[block, 1 - lane_of], dst_ref=paired.at[block],
            send_sem=pair_send.at[which, block], recv_sem=pair_recv.at[which, block],
            device_id={"dp": partner}, device_id_type=MESH,
        )

    def flow_of(which, block, rightward, source):
        flow = pairs[which][4 if rightward else 5]
        sends, recvs = (right_send, right_recv) if rightward else (left_send, left_recv)
        return pltpu.make_async_remote_copy(
            src_ref=source.at[block], dst_ref=flow.at[block],
            send_sem=sends.at[which, block], recv_sem=recvs.at[which, block],
            device_id={"dp": right if rightward else left}, device_id_type=MESH,
        )

    def begin(turn, _):
        block = block_at(turn)
        for which in range(2):
            pair_of(which, block).start()
            load_of(which, block).start()
        return 0

    lax.fori_loop(0, line, begin, 0)

    def pass_on(turn, _):
        block = block_at(turn)
        for which in range(2):
            own, paired = pairs[which][2:4]
            load_of(which, block).wait()
            pair_of(which, block).wait_recv()
            add_into(own.at[block], own.at[block], paired.at[block])
            for rightward in (True, False):
                flow = pairs[which][4 if rightward else 5]
                fed = has_left if rightward else has_right
                wanted = block > spot if rightward else block < spot

                @pl.when(jnp.logical_and(wanted, fed))
                def _():
                    flow_of(which, block, rightward, flow).wait_recv()
                    add_into(flow.at[block], flow.at[block], own.at[block])
                    flow_of(which, block, rightward, flow).start()

                @pl.when(jnp.logical_and(wanted, jnp.logical_not(fed)))
                def _():
                    flow_of(which, block, rightward, own).start()
        return 0

    lax.fori_loop(0, line, pass_on, 0)

    for which in range(2):
        out, own = pairs[which][1:3]
        for rightward in (True, False):
            flow = pairs[which][4 if rightward else 5]

            @pl.when(has_left if rightward else has_right)
            def _():
                flow_of(which, spot, rightward, flow).wait_recv()

        @pl.when(jnp.logical_and(has_left, has_right))
        def _():
            add_into(out, own.at[spot], pairs[which][4].at[spot])
            add_into(out, out, pairs[which][5].at[spot])

        @pl.when(jnp.logical_and(has_left, jnp.logical_not(has_right)))
        def _():
            add_into(out, own.at[spot], pairs[which][4].at[spot])

        @pl.when(jnp.logical_and(has_right, jnp.logical_not(has_left)))
        def _():
            add_into(out, own.at[spot], pairs[which][5].at[spot])

    def finish(block, _):
        for which in range(2):
            pair_of(which, block).wait_send()
            for rightward in (True, False):

                @pl.when(block > spot if rightward else block < spot)
                def _():
                    flow_of(which, block, rightward, pairs[which][2]).wait_send()
        return 0

    lax.fori_loop(0, line, finish, 0)


def scatter_sums(part_a, part_b):
    devices = lax.axis_size("dp")
    line = devices // 2
    parts = [part.reshape(line, 2, part.shape[0] // devices, part.shape[1]) for part in (part_a, part_b)]
    scratch = []
    for part in parts:
        scratch += [pltpu.VMEM((line,) + part.shape[2:], part.dtype)] * 4
    scratch += [pltpu.SemaphoreType.DMA((2, line))] * 7
    return pl.pallas_call(
        functools.partial(scatter_kernel, line),
        out_shape=tuple(jax.ShapeDtypeStruct(part.shape[2:], jnp.float32) for part in parts),
        in_specs=[pl.BlockSpec(memory_space=pl.ANY)] * 2,
        out_specs=(VMEM,) * 2,
        scratch_shapes=scratch,
        compiler_params=pltpu.CompilerParams(
            collective_id=1, has_side_effects=True, vmem_limit_bytes=60 * 1024 * 1024
        ),
        name="scatter_sums",
    )(*parts)


def mask_of(segments):
    length = segments.shape[1]
    same = segments[:, :, None] == segments[:, None, :]
    positions = lax.broadcasted_iota(jnp.int32, (length, length), 0)
    columns = lax.broadcasted_iota(jnp.int32, (length, length), 1)
    counts = jnp.sum(same.astype(jnp.float32), axis=2, keepdims=True)
    allowed = jnp.logical_and(same, (columns <= positions)[None])
    return (allowed.astype(jnp.float32) / counts).reshape(-1, length)


def body(section_input, top_grad, w_in, w_out, segments):
    micro, length = segments.shape
    inputs = section_input[0]
    w_first = lax.all_gather(w_in[0], "dp", axis=0, tiled=True)
    w_mine, w_first = lax.optimization_barrier((w_out[0], w_first))
    w_second = lax.all_gather(w_mine, "dp", axis=0, tiled=True)
    mask = mask_of(segments)
    normed = norm_rows(inputs.astype(jnp.float32)).astype(jnp.bfloat16)
    preact = jnp.dot(normed, w_first, preferred_element_type=jnp.float32)
    activated = jax.nn.silu(preact).astype(jnp.bfloat16)
    scores, unit, rstd, gated = attend(activated, mask, micro, length)
    upstream, grad_preact, grads = chain(
        top_grad, inputs, activated, preact, scores, unit, rstd, mask, w_first, w_second, micro, length
    )
    part_out = contract_rows(gated, upstream).astype(jnp.bfloat16)
    part_in = contract_rows(normed, grad_preact).astype(jnp.bfloat16)
    grad_first, grad_out = scatter_sums(part_in, part_out)
    return (grads[None], grad_first[None], grad_out[None])


CORES = 2


class Place:
    def __init__(self):
        self.pipe, self.dp = lax.axis_index("pipe"), lax.axis_index("dp")
        self.x, self.core = self.pipe // CORES, self.pipe % CORES
        self.z, self.y = self.dp // CORES, self.dp % CORES

    def device(self, x=None, core=None, z=None, y=None, pipe=None):
        x = self.x if x is None else x
        core = self.core if core is None else core
        z = self.z if z is None else z
        y = self.y if y is None else y
        return {"pipe": x * CORES + core if pipe is None else pipe, "dp": z * CORES + y}


def signal(sem, device):
    pl.semaphore_signal(sem, inc=1, device_id=device, device_id_type=MESH)


def remote(src, dst, send, recv, device):
    return pltpu.make_async_remote_copy(
        src_ref=src, dst_ref=dst, send_sem=send, recv_sem=recv, device_id=device, device_id_type=MESH
    )


def either(local_if, local, far):
    pl.when(local_if)(local)
    pl.when(jnp.logical_not(local_if))(far)


def turned(index):
    return index % CORES * CORES + index // CORES


def layer_order(step, z, layers):
    return jnp.where(2 * z < layers, (z + step) % layers, (z + layers - step) % layers)


def work_kernel(
    micro, length, layers,
    input_ref, top_ref, w_in_ref, w_out_ref, home_mask_ref,
    out_first, out_second, out_grads,
    grads_ref, up_ref, gpre_ref, normed_ref, gated_ref,
    first, second, stage_first, stage_second, work_in, top, mask,
    unit_in, rstd_in, slope, act, weight, weight_slope, unit, rstd, mixed, landed, ggate, gnorm,
    swap_send, swap_recv, top_send, top_recv, pre_send, pre_recv, own_send, hop_send, to_core, to_x, to_y, came,
    chain_send, chain_recv, back_send, back_recv,
    *sums,
):
    me = Place()
    width = work_in.shape[1]
    tokens = micro * length
    section = me.z
    other_x, other_core, other_y = 1 - me.x, 1 - me.core, 1 - me.y
    at_home = me.pipe == me.z
    is_last, is_first = section == layers - 1, section == 0
    weights = (
        (w_in_ref, first, stage_first),
        (w_out_ref, second, stage_second),
    )
    sizes = [ref.shape[0] // 4 for ref, _, _ in weights]

    def quarter(which, block, half, core):
        size = sizes[which]
        start = pl.multiple_of(((block * 2 + half) * CORES + core) * size, size)
        return weights[which][1].at[pl.ds(start, size), :]

    def shard(which, half, core):
        size = sizes[which]
        start = pl.multiple_of((half * CORES + core) * size, size)
        return weights[which][0].at[pl.ds(start, size), :]

    def came_at(which, block, half, core):
        return came.at[which, (block * 2 + half) * CORES + core]

    barrier = pltpu.get_barrier_semaphore()
    def greet(index, _):
        pipe, layer = index // layers, index % layers

        @pl.when(jnp.logical_not(jnp.logical_and(pipe == me.pipe, layer == me.z)))
        def _():
            signal(barrier, {"pipe": pipe, "dp": layer * CORES + me.y})

        return 0

    lax.fori_loop(0, layers * layers, greet, 0)
    signal(barrier, me.device(y=other_y))
    pl.semaphore_wait(barrier, layers * layers)

    away = {"pipe": turned(me.z), "dp": me.pipe * CORES + me.y}
    back = {"pipe": me.z, "dp": turned(me.pipe) * CORES + me.y}
    stays = jnp.logical_and(at_home, turned(me.pipe) == me.pipe)
    swaps = ((input_ref, work_in), (home_mask_ref, mask))

    def swap_far(index):
        src, dst = swaps[index]
        return remote(src, dst, swap_send.at[index], swap_recv.at[index], away)

    def swap_near(index):
        src, dst = swaps[index]
        return pltpu.make_async_copy(src, dst, swap_recv.at[index])

    def swap_start():
        for index in range(2):
            either(stays, lambda: swap_near(index).start(), lambda: swap_far(index).start())

    def before(which, core):
        return remote(
            shard(which, other_x, core), weights[which][2].at[me.core],
            pre_send.at[which, core], pre_recv.at[which, me.core], me.device(x=other_x, core=core),
        )

    def own(which, core):
        return remote(
            shard(which, me.x, core), quarter(which, me.dp, me.x, core),
            own_send.at[which, core], came_at(which, me.dp, me.x, core), me.device(core=core, z=me.pipe),
        )

    def own_near(which, core):
        return pltpu.make_async_copy(
            shard(which, me.x, core), quarter(which, me.dp, me.x, core), came_at(which, me.dp, me.x, core)
        )

    def hop(which, source):
        return remote(
            weights[which][2].at[source], quarter(which, me.dp, me.x, me.core),
            hop_send.at[which, source], came_at(which, me.dp, me.x, me.core),
            me.device(z=other_x * CORES + source),
        )

    def hop_near(which, source):
        return pltpu.make_async_copy(
            weights[which][2].at[source], quarter(which, me.dp, me.x, me.core),
            came_at(which, me.dp, me.x, me.core),
        )

    def before_came(which, source):
        return remote(
            shard(which, other_x, me.core), weights[which][2].at[source],
            pre_send.at[which, source], pre_recv.at[which, source], me.device(x=other_x),
        )

    for which in range(2):
        for core in range(CORES):
            before(which, core).start()
        for core in range(CORES):
            near = jnp.logical_and(at_home, core == me.core)
            either(near, lambda: own_near(which, core).start(), lambda: own(which, core).start())

    for which in range(2):
        for source in range(CORES):
            before_came(which, source).wait_recv()
            either(
                other_x * CORES + source == me.z,
                lambda: hop_near(which, source).start(),
                lambda: hop(which, source).start(),
            )

    top_far = remote(top_ref, top, top_send, top_recv, me.device(z=layers - 1))
    top_near = pltpu.make_async_copy(top_ref, top, top_recv)
    has_top = me.z == turned(me.pipe)
    gives_top = jnp.logical_and(has_top, jnp.logical_not(is_last))
    keeps_top = jnp.logical_and(has_top, is_last)

    def top_start():
        pl.when(gives_top)(lambda: top_far.start())
        pl.when(keeps_top)(lambda: top_near.start())

    def send(which, block, half, core, sem, index, device):
        place = quarter(which, block, half, core)
        return remote(place, place, sem.at[which, index], came_at(which, block, half, core), device)

    def direct_block(step):
        return layer_order(step, me.z, layers) * CORES + me.y

    def core_copy(which, kind, step):
        block = direct_block(step)
        lane = kind // 2
        block = block if lane == 0 else block - me.y + other_y
        half = me.x if kind % 2 == 0 else other_x
        return send(which, block, half, me.core, to_core, kind * layers + step, me.device(core=other_core))

    def x_copy(which, step):
        return send(which, direct_block(step), me.x, me.core, to_x, step, me.device(x=other_x))

    def y_copy(which, kind, step):
        half = me.x if kind == 0 else other_x
        return send(which, direct_block(step), half, me.core, to_y, kind * layers + step, me.device(y=other_y))

    def arrived(which, block, half, core):
        place = quarter(which, block, half, core)
        return remote(
            place, place, to_core.at[which, 0], came_at(which, block, half, core), me.device(core=other_core)
        )

    def settled(which):
        for core in range(CORES):
            near = jnp.logical_and(at_home, core == me.core)
            pl.when(jnp.logical_not(near))(lambda: own(which, core).wait_send())
        for source in range(CORES):
            near = other_x * CORES + source == me.z
            pl.when(jnp.logical_not(near))(lambda: hop(which, source).wait_send())

    def direct_ready(which, step):
        block = direct_block(step)
        if step == 0:
            far = jnp.logical_and(me.x == me.z // CORES, me.core != me.z % CORES)
            place = quarter(which, block, me.x, me.core)
            either(
                jnp.logical_not(far),
                lambda: pltpu.make_async_copy(shard(which, 0, 0), place, came_at(which, block, me.x, me.core)).wait(),
                lambda: arrived(which, block, me.x, me.core).wait_recv(),
            )
        else:
            arrived(which, block, me.x, me.core).wait_recv()
        x_copy(which, step).start()
        y_copy(which, 0, step).start()
        core_copy(which, 0, step).start()

    def from_x(which, step):
        arrived(which, direct_block(step), other_x, me.core).wait_recv()
        y_copy(which, 1, step).start()
        core_copy(which, 1, step).start()

    def from_y(which, kind, step):
        block = direct_block(step) - me.y + other_y
        arrived(which, block, me.x if kind == 0 else other_x, me.core).wait_recv()
        core_copy(which, 2 + kind, step).start()

    def whole(which):
        def one(index, _):
            arrived(which, index // 2, index % 2, other_core).wait_recv()
            return 0

        lax.fori_loop(0, 2 * layers * CORES, one, 0)

    for step in range(layers + 1):
        if step == 2:
            for which in range(2):
                settled(which)
            swap_start()
            top_start()
        if step < layers:
            direct_ready(0, step)
        if step >= 1:
            from_x(0, step - 1)
            from_y(0, 0, step - 1)
        if step >= 2:
            from_y(0, 1, step - 2)
    for step in range(layers):
        direct_ready(1, step)
    for index in range(2):
        either(stays, lambda: swap_near(index).wait(), lambda: swap_far(index).wait_recv())
    norm_input(work_in, normed_ref, unit_in, rstd_in)
    from_y(0, 1, layers - 1)
    for step in range(layers):
        from_x(1, step)
    whole(0)
    tile = 2 * LANES

    def front(index, _):
        cols = at(index * tile, tile)
        value = dot_nn(normed_ref[...], first[:, cols])
        squash = jax.nn.sigmoid(value)
        act[:, cols] = (value * squash).astype(jnp.bfloat16)
        slope[:, cols] = squash * (1.0 + value * (1.0 - squash))
        return 0

    lax.fori_loop(0, slope.shape[1] // tile, front, 0)
    for step in range(layers):
        from_y(1, 0, step)
    attend_front(micro, length, act, mask, weight, weight_slope, unit, rstd, gated_ref, mixed)
    for step in range(layers):
        from_y(1, 1, step)
    whole(1)

    def copy_of(slot):
        return remote(
            grads_ref.at[pl.ds(slot * length, length), :], landed.at[slot], chain_send.at[slot], chain_recv.at[slot],
            me.device(z=jnp.maximum(me.z - 1, 0)),
        )

    def back_far(slot):
        rows = pl.ds(slot * length, length)
        return remote(grads_ref.at[rows, :], out_grads.at[rows, :], back_send.at[slot], back_recv.at[slot], back)

    def back_near(slot):
        rows = pl.ds(slot * length, length)
        return pltpu.make_async_copy(grads_ref.at[rows, :], out_grads.at[rows, :], back_recv.at[slot])

    def back_one(slot):
        either(stays, lambda: back_near(slot).start(), lambda: back_far(slot).start())

    def back_start():
        for slot in range(micro):
            back_one(slot)

    @pl.when(jnp.logical_and(is_last, jnp.logical_not(has_top)))
    def _():
        top_far.wait_recv()

    @pl.when(keeps_top)
    def _():
        top_near.wait()

    chain_steps(
        micro, length, is_first, is_last, copy_of, back_one,
        top, unit_in, rstd_in, act, slope, weight, weight_slope, unit, rstd, first, second,
        grads_ref, up_ref, gpre_ref, landed, ggate, gnorm,
    )

    for slot in range(micro):

        @pl.when(jnp.logical_not(is_first))
        def _():
            copy_of(slot).wait_send()

    for index in range(2):
        pl.when(jnp.logical_not(stays))(lambda: swap_far(index).wait_send())
    pl.when(gives_top)(lambda: top_far.wait_send())
    for which in range(2):
        for core in range(CORES):
            before(which, core).wait_send()

        def sent(step, _):
            x_copy(which, step).wait_send()
            for kind in range(2):
                y_copy(which, kind, step).wait_send()
            for kind in range(4):
                core_copy(which, kind, step).wait_send()
            return 0

        lax.fori_loop(0, layers, sent, 0)

    sum_weights(
        me, layers, normed_ref, gpre_ref, gated_ref, up_ref, out_first, out_second, first, second, *sums,
        lambda: pl.when(jnp.logical_not(is_first))(back_start),
    )
    for slot in range(micro):
        either(stays, lambda: back_near(slot).wait(), lambda: back_far(slot).wait())


def folded(value):
    total = value[:, :LANES]
    for start in range(LANES, value.shape[1], LANES):
        total = total + value[:, start : start + LANES]
    return total


def norm_input(work_in, normed_ref, unit_in, rstd_in):
    step = 64
    width = work_in.shape[1]

    def one(index, _):
        rows = pl.ds(pl.multiple_of(index * step, step), step)
        value = work_in[rows, :].astype(jnp.float32)
        center = value - jnp.mean(value, axis=-1, keepdims=True)
        rstd = lax.rsqrt(jnp.mean(center * center, axis=-1, keepdims=True) + EPSILON)
        unit = center * rstd
        unit_in[rows, :] = unit
        normed_ref[rows, :] = unit.astype(jnp.bfloat16)
        rstd_in[rows, :] = jnp.broadcast_to(rstd, (step, LANES))
        return 0

    lax.fori_loop(0, work_in.shape[0] // step, one, 0)


def attend_front(micro, length, act_ref, mask_ref, weight_ref, slope_ref, unit_ref, rstd_ref, gated_ref, mixed):
    lane = lax.broadcasted_iota(jnp.int32, (length, LANES), 1)

    def one(index, _):
        slot, group = index // GROUPS, index % GROUPS
        rows = at(slot * length, length)
        queries = act_ref[rows, at(2 * V_COLS + group * LANES, LANES)]
        keys = act_ref[rows, at(2 * V_COLS + Q_COLS + group * LANES, LANES)]
        mask = mask_ref[rows, :]
        for half in range(GROUP_V // LANES):
            cols = group * GROUP_V + half * LANES
            values = act_ref[rows, at(V_COLS + cols, LANES)]
            total = jnp.zeros((length, LANES), jnp.float32)
            for sub in range(V_HEADS):
                head = half * V_HEADS + sub
                score = dot_nt(only_head(queries, lane, QK_DIM, head), keys) * SCALE
                squash = jax.nn.sigmoid(score)
                place = at((index * QK_HEADS + head) * length, length)
                slope_ref[place, :] = squash * (1.0 + score * (1.0 - squash)) * (mask * SCALE)
                weight = (score * squash * mask).astype(jnp.bfloat16)
                weight_ref[place, :] = weight
                total += dot_nn(weight, only_head(values, lane, V_DIM, sub))
            mixed[rows, at(cols, LANES)] = total
        return 0

    lax.fori_loop(0, micro * GROUPS, one, 0)
    step = 64

    def finish(index, _):
        rows = pl.ds(pl.multiple_of(index * step, step), step)
        value = mixed[rows, :]
        center = value - jnp.mean(value, axis=-1, keepdims=True)
        rstd = lax.rsqrt(jnp.mean(center * center, axis=-1, keepdims=True) + EPSILON)
        unit = center * rstd
        unit_ref[rows, :] = unit
        rstd_ref[rows, :] = jnp.broadcast_to(rstd, (step, LANES))
        gated_ref[rows, :] = (unit * act_ref[rows, :V_COLS].astype(jnp.float32)).astype(jnp.bfloat16)
        return 0

    lax.fori_loop(0, micro * length // step, finish, 0)


def chain_steps(
    micro, length, is_first, is_last, copy_of, back_one,
    top_ref, unit_in, rstd_in, act_ref, slope_ref, weight_ref, weight_slope, unit_ref, rstd_ref, first_ref, second_ref,
    grads_ref, up_ref, gpre_ref, landed, ggate, gnorm,
):
    width = unit_in.shape[1]
    tile = 2 * LANES
    lane = lax.broadcasted_iota(jnp.int32, (length, LANES), 1)
    nothing = jnp.zeros((length, LANES), jnp.float32)

    def store_grad(rows, cols, size, value):
        rounded = value.astype(jnp.bfloat16).astype(jnp.float32)
        gpre_ref[rows, at(cols, size)] = (rounded * slope_ref[rows, at(cols, size)]).astype(jnp.bfloat16)

    for slot in range(micro):
        rows = pl.ds(slot * length, length)

        @pl.when(is_last)
        def _():
            up_ref[rows, :] = top_ref[rows, :]

        @pl.when(jnp.logical_not(is_last))
        def _():
            copy_of(slot).wait_recv()
            up_ref[rows, :] = landed[slot]

        def gate_tile(index, sums):
            cols = at(index * tile, tile)
            grad = dot_nt(up_ref[rows, :], second_ref[cols, :])
            unit = unit_ref[rows, cols]
            store_grad(rows, index * tile, tile, grad * unit)
            grad = grad * act_ref[rows, cols].astype(jnp.float32)
            ggate[:, cols] = grad
            return sums[0] + folded(grad), sums[1] + folded(grad * unit)

        sums = lax.fori_loop(0, V_COLS // tile, gate_tile, (nothing, nothing))
        mean_grad, mean_unit = [jnp.sum(part, axis=-1, keepdims=True) * (1.0 / V_COLS) for part in sums]
        rstd = rstd_ref[rows, :1]

        def one(group, _):
            queries = act_ref[rows, at(2 * V_COLS + group * LANES, LANES)]
            keys = act_ref[rows, at(2 * V_COLS + Q_COLS + group * LANES, LANES)]
            grad_q = jnp.zeros((length, LANES), jnp.float32)
            grad_k = jnp.zeros((length, LANES), jnp.float32)
            for half in range(GROUP_V // LANES):
                cols = group * GROUP_V + half * LANES
                values = act_ref[rows, at(V_COLS + cols, LANES)]
                spread = ggate[:, at(cols, LANES)] - mean_grad - unit_ref[rows, at(cols, LANES)] * mean_unit
                grad_mix = (rstd * spread).astype(jnp.bfloat16)
                grad_v = jnp.zeros((length, LANES), jnp.float32)
                for sub in range(V_HEADS):
                    head = half * V_HEADS + sub
                    mix_head = only_head(grad_mix, lane, V_DIM, sub)
                    place = at((slot * HEADS + group * QK_HEADS + head) * length, length)
                    grad_score = (dot_nt(mix_head, values) * weight_slope[place, :]).astype(jnp.bfloat16)
                    grad_v += contract_rows(weight_ref[place, :], mix_head)
                    grad_q += dot_nn(grad_score, only_head(keys, lane, QK_DIM, head))
                    grad_k += contract_rows(grad_score, only_head(queries, lane, QK_DIM, head))
                store_grad(rows, V_COLS + cols, LANES, grad_v)
            store_grad(rows, 2 * V_COLS + group * LANES, LANES, grad_q)
            store_grad(rows, 2 * V_COLS + Q_COLS + group * LANES, LANES, grad_k)
            return 0

        lax.fori_loop(0, GROUPS, one, 0)

        def norm_tile(index, sums):
            cols = at(index * tile, tile)
            grad = dot_nt(gpre_ref[rows, :], first_ref[cols, :])
            gnorm[:, cols] = grad
            return sums[0] + folded(grad), sums[1] + folded(grad * unit_in[rows, cols])

        sums = lax.fori_loop(0, width // tile, norm_tile, (nothing, nothing))
        mean_grad, mean_unit = [jnp.sum(part, axis=-1, keepdims=True) * (1.0 / width) for part in sums]
        rstd = rstd_in[rows, :1]

        def pass_tile(index, _):
            cols = at(index * tile, tile)
            through = rstd * (gnorm[:, cols] - mean_grad - unit_in[rows, cols] * mean_unit)
            grads_ref[rows, cols] = (up_ref[rows, cols].astype(jnp.float32) + through).astype(jnp.bfloat16)
            return 0

        lax.fori_loop(0, width // tile, pass_tile, 0)

        @pl.when(jnp.logical_not(is_first))
        def _():
            copy_of(slot).start()

        back_one(slot)


ANY = pl.BlockSpec(memory_space=pl.ANY)
LIMIT = 60 * 1024 * 1024


def work(inputs, top_grad, w_in, w_out, mask, micro, length):
    tokens, width = inputs.shape
    layers, blocks = lax.axis_size("pipe"), lax.axis_size("dp")
    columns = w_in.shape[1]
    quarters = [w.shape[0] // 4 for w in (w_in, w_out)]
    dma = pltpu.SemaphoreType.DMA
    return pl.pallas_call(
        functools.partial(work_kernel, micro, length, layers),
        out_shape=tuple(jax.ShapeDtypeStruct(a.shape, a.dtype) for a in (w_in, w_out, inputs)),
        in_specs=[ANY] * 5,
        out_specs=(ANY,) * 3,
        scratch_shapes=[
            pltpu.VMEM((tokens, width), jnp.bfloat16),
            pltpu.VMEM((tokens, width), jnp.bfloat16),
            pltpu.VMEM((tokens, columns), jnp.bfloat16),
            pltpu.VMEM((tokens, width), jnp.bfloat16),
            pltpu.VMEM((tokens, V_COLS), jnp.bfloat16),
            pltpu.VMEM((blocks * w_in.shape[0], columns), jnp.bfloat16),
            pltpu.VMEM((blocks * w_out.shape[0], width), jnp.bfloat16),
            pltpu.VMEM((CORES, quarters[0], columns), jnp.bfloat16),
            pltpu.VMEM((CORES, quarters[1], width), jnp.bfloat16),
            pltpu.VMEM((tokens, width), jnp.bfloat16),
            pltpu.VMEM((tokens, width), jnp.bfloat16),
            pltpu.VMEM((tokens, length), jnp.float32),
            pltpu.VMEM((tokens, width), jnp.float32),
            pltpu.VMEM((tokens, LANES), jnp.float32),
            pltpu.VMEM((tokens, columns), jnp.float32),
            pltpu.VMEM((tokens, columns), jnp.bfloat16),
            pltpu.VMEM((micro * HEADS * length, length), jnp.bfloat16),
            pltpu.VMEM((micro * HEADS * length, length), jnp.float32),
            pltpu.VMEM((tokens, V_COLS), jnp.float32),
            pltpu.VMEM((tokens, LANES), jnp.float32),
            pltpu.VMEM((tokens, V_COLS), jnp.float32),
            pltpu.VMEM((micro, length, width), jnp.bfloat16),
            pltpu.VMEM((length, V_COLS), jnp.float32),
            pltpu.VMEM((length, width), jnp.float32),
            dma((2,)), dma((2,)), dma, dma,
            dma((2, CORES)), dma((2, CORES)), dma((2, CORES)), dma((2, CORES)),
            dma((2, 4 * layers)), dma((2, layers)), dma((2, 2 * layers)), dma((2, 4 * blocks)),
            dma((micro,)), dma((micro,)), dma((micro,)), dma((micro,)),
        ]
        + [
            pltpu.VMEM((count, size, cols), jnp.bfloat16)
            for count in (2 * blocks, 2 * layers, layers)
            for size, cols in zip(quarters, (columns, width))
        ]
        + [dma((2, count)) for count in (2 * blocks, 2 * layers, layers, layers) for _ in range(2)],
        compiler_params=pltpu.CompilerParams(collective_id=2, has_side_effects=True, vmem_limit_bytes=LIMIT),
        name="work",
    )(inputs, top_grad, w_in, w_out, mask)


def add_rows(target, other):
    step = 16

    def one(index, _):
        rows = pl.ds(pl.multiple_of(index * step, step), step)
        total = target[rows, :].astype(jnp.float32) + other[rows, :].astype(jnp.float32)
        target[rows, :] = total.astype(target.dtype)
        return 0

    lax.fori_loop(0, target.shape[0] // step, one, 0)


def sum_weights(
    me, layers, normed_ref, gpre_ref, gated_ref, up_ref, out_first, out_second, first, second,
    core_first, core_second, early_first, early_second, late_first, late_second,
    core_send, core_recv, y_send, y_recv, x_send, x_recv, home_send, home_recv,
    between,
):
    other_x, other_core, other_y = 1 - me.x, 1 - me.core, 1 - me.y
    at_home = me.pipe == me.z
    sets = (
        (normed_ref, gpre_ref, out_first, first, core_first, early_first, late_first),
        (gated_ref, up_ref, out_second, second, core_second, early_second, late_second),
    )
    sizes = [s[2].shape[0] // 4 for s in sets]

    def quarter(which, block, half, core):
        size = sizes[which]
        start = pl.multiple_of(((block * 2 + half) * CORES + core) * size, size)
        return sets[which][3].at[pl.ds(start, size), :]

    def core_copy(which, block, half, mine):
        core = me.core if mine else other_core
        index = block * 2 + half
        return remote(
            quarter(which, block, half, core), sets[which][4].at[index],
            core_send.at[which, index], core_recv.at[which, index], me.device(core=other_core),
        )

    along_y = me.core == 0
    early_to = {
        "pipe": jnp.where(along_y, me.x, other_x) * CORES + me.core,
        "dp": me.z * CORES + jnp.where(along_y, other_y, me.y),
    }
    late_to = {
        "pipe": jnp.where(along_y, other_x, me.x) * CORES + me.core,
        "dp": me.z * CORES + jnp.where(along_y, me.y, other_y),
    }

    def near_unit(row, index, far):
        lane_of = jnp.where(along_y, other_y if far else me.y, index)
        half = jnp.where(along_y, index, other_x if far else me.x)
        return row * CORES + lane_of, half

    def early_copy(which, row, index):
        block, half = near_unit(row, index, True)
        slot = row * 2 + index
        return remote(
            quarter(which, block, half, me.core), sets[which][5].at[slot],
            y_send.at[which, slot], y_recv.at[which, slot], early_to,
        )

    def late_copy(which, row):
        block, half = near_unit(row, jnp.where(along_y, other_x, other_y), False)
        return remote(
            quarter(which, block, half, me.core), sets[which][6].at[row],
            x_send.at[which, row], x_recv.at[which, row], late_to,
        )

    def home_rows(which, half, core):
        size = sizes[which]
        return sets[which][2].at[pl.ds(pl.multiple_of((half * CORES + core) * size, size), size), :]

    def home_copy(which, row):
        return remote(
            quarter(which, row * CORES + me.y, me.x, me.core), home_rows(which, me.x, me.core),
            home_send.at[which, row], home_recv.at[which, me.x * CORES + me.core],
            {"pipe": me.z, "dp": row * CORES + me.y},
        )

    def home_near(which):
        return pltpu.make_async_copy(
            quarter(which, me.dp, me.x, me.core), home_rows(which, me.x, me.core),
            home_recv.at[which, me.x * CORES + me.core],
        )

    def row_at(step):
        return layer_order(layers - 1 - step, me.z, layers)

    def product(row):
        for which in (1, 0):
            left, right, _, whole = sets[which][:4]
            size = 8 * sizes[which]
            tile = 2 * LANES
            place = pl.ds(pl.multiple_of(row * size, size), size)

            def one(index, _):
                cols = at(index * tile, tile)
                whole[place, cols] = contract_rows(left[:, place], right[:, cols]).astype(whole.dtype)
                return 0

            lax.fori_loop(0, right.shape[1] // tile, one, 0)
            for lane_of in range(CORES):
                for half in range(2):
                    core_copy(which, row * CORES + lane_of, half, False).start()

    def fold_core(row, far):
        for which in (1, 0):

            def one(index, _):
                block, half = near_unit(row, index, far)
                core_copy(which, block, half, True).wait_recv()
                add_rows(quarter(which, block, half, me.core), sets[which][4].at[block * 2 + half])
                return 0

            lax.fori_loop(0, 2, one, 0)

    def start_early(row):
        for which in (1, 0):
            for index in range(2):
                early_copy(which, row, index).start()

    def fold_early(row):
        for which in (1, 0):

            def one(turn, _):
                mine = jnp.where(along_y, me.x, me.y)
                index = jnp.where(turn == 0, 1 - mine, mine)
                block, half = near_unit(row, index, False)
                early_copy(which, row, index).wait_recv()
                add_rows(quarter(which, block, half, me.core), sets[which][5].at[row * 2 + index])
                pl.when(turn == 0)(lambda: late_copy(which, row).start())
                return 0

            lax.fori_loop(0, 2, one, 0)

    def fold_late(row):
        for which in (1, 0):
            late_copy(which, row).wait_recv()
            add_rows(quarter(which, row * CORES + me.y, me.x, me.core), sets[which][6].at[row])
            near = jnp.logical_and(at_home, row == me.z)
            either(near, lambda: home_near(which).start(), lambda: home_copy(which, row).start())

    steps = [row_at(step) for step in range(layers)]
    ahead = 1
    for step in range(layers + 1):
        if step < layers:
            product(steps[step])
        if step >= 1:
            fold_core(steps[step - 1], True)
            if step <= ahead:
                start_early(steps[step - 1])
            fold_core(steps[step - 1], False)
    for step in range(layers + 1):
        if step < layers:
            if step + ahead < layers:
                for which in (1, 0):
                    early_copy(which, steps[step], 0).wait_send()
                    early_copy(which, steps[step], 1).wait_send()
                start_early(steps[step + ahead])
            fold_early(steps[step])
        if step >= 1:
            fold_late(steps[step - 1])
    for which in range(2):
        for pipe in range(layers):
            place = home_rows(which, pipe // CORES, pipe % CORES)
            near = jnp.logical_and(at_home, pipe == me.pipe)
            either(
                near,
                lambda: home_near(which).wait(),
                lambda: remote(
                    place, place, home_send.at[which, 0], home_recv.at[which, pipe], me.device(core=other_core)
                ).wait_recv(),
            )

        def sent(row, _):
            for half in range(2):
                for lane_of in range(2):
                    core_copy(which, row * CORES + lane_of, half, False).wait_send()
            near = jnp.logical_and(at_home, row == me.z)
            pl.when(jnp.logical_not(near))(lambda: home_copy(which, row).wait_send())
            return 0

        lax.fori_loop(0, layers, sent, 0)
        for step in range(layers):
            if step + ahead >= layers:
                early_copy(which, steps[step], 0).wait_send()
                early_copy(which, steps[step], 1).wait_send()
            late_copy(which, steps[step]).wait_send()


def layered_body(section_input, top_grad, w_in, w_out, segments):
    micro, length = segments.shape
    mask = mask_of(segments)
    grad_first, grad_out, grads = work(section_input[0], top_grad, w_in[0], w_out[0], mask, micro, length)
    return (grads[None], grad_first.astype(jnp.float32)[None], grad_out.astype(jnp.float32)[None])


def solution(mesh):
    layered = mesh.shape["pipe"] == CORES * 2 and mesh.shape["dp"] == CORES * mesh.shape["pipe"]
    return jax.shard_map(
        layered_body if layered else body,
        mesh=mesh,
        in_specs=(
            P("pipe", "dp", None),
            P("dp", None),
            P("pipe", "dp", None),
            P("pipe", "dp", None),
            P("dp", None),
        ),
        out_specs=(P("pipe", "dp", None), P("pipe", "dp", None), P("pipe", "dp", None)),
        check_vma=False,
    )
```

```python
import functools

import jax
import jax.numpy as jnp
from jax import lax
from jax.experimental import pallas as pl
from jax.experimental.pallas import tpu as pltpu
from jax.sharding import PartitionSpec as P

HEADS = 16
QK_DIM = 32
V_DIM = 64
LANES = 128

EPSILON = 1e-05
MESH = pl.DeviceIdType.MESH
VMEM = pl.BlockSpec(memory_space=pltpu.VMEM)

QK_HEADS = LANES // QK_DIM
V_HEADS = LANES // V_DIM
GROUPS = HEADS // QK_HEADS
V_COLS = HEADS * V_DIM
Q_COLS = HEADS * QK_DIM
GROUP_V = QK_HEADS * V_DIM
SCALE = QK_DIM ** (-0.5)


def norm_rows(values):
    center = values - jnp.mean(values, axis=-1, keepdims=True)
    return center * lax.rsqrt(jnp.mean(center * center, axis=-1, keepdims=True) + EPSILON)


def silu_slope(preact):
    squash = jax.nn.sigmoid(preact)
    return squash * (1.0 + preact * (1.0 - squash))


def dot_nt(left, right):
    return lax.dot_general(
        left, right, (((1,), (1,)), ((), ())), preferred_element_type=jnp.float32
    )


def dot_nn(left, right):
    return lax.dot_general(
        left, right, (((1,), (0,)), ((), ())), preferred_element_type=jnp.float32
    )


def contract_rows(left, right):
    return lax.dot_general(
        left, right, (((0,), (0,)), ((), ())), preferred_element_type=jnp.float32
    )


def only_head(block, lane, width, index):
    keep = jnp.logical_and(lane >= index * width, lane < (index + 1) * width)
    return jnp.where(keep, block, jnp.zeros_like(block))


def at(start, size):
    return pl.ds(pl.multiple_of(start, LANES), size)


def attend_kernel(micro, length, act_ref, mask_ref, score_ref, unit_ref, rstd_ref, gated_ref, mixed):
    lane = lax.broadcasted_iota(jnp.int32, (length, LANES), 1)

    def one(index, _):
        slot, group = index // GROUPS, index % GROUPS
        rows = at(slot * length, length)
        queries = act_ref[rows, at(2 * V_COLS + group * LANES, LANES)]
        keys = act_ref[rows, at(2 * V_COLS + Q_COLS + group * LANES, LANES)]
        mask = mask_ref[rows, :]
        for half in range(GROUP_V // LANES):
            cols = group * GROUP_V + half * LANES
            values = act_ref[rows, at(V_COLS + cols, LANES)]
            total = jnp.zeros((length, LANES), jnp.float32)
            for sub in range(V_HEADS):
                head = half * V_HEADS + sub
                score = dot_nt(only_head(queries, lane, QK_DIM, head), keys) * SCALE
                score_ref[at((index * QK_HEADS + head) * length, length), :] = score
                weight = (jax.nn.silu(score) * mask).astype(jnp.bfloat16)
                total += dot_nn(weight, only_head(values, lane, V_DIM, sub))
            mixed[rows, at(cols, LANES)] = total
        return 0

    lax.fori_loop(0, micro * GROUPS, one, 0)

    def finish(slot, _):
        rows = at(slot * length, length)
        value = mixed[rows, :]
        center = value - jnp.mean(value, axis=-1, keepdims=True)
        rstd = lax.rsqrt(jnp.mean(center * center, axis=-1, keepdims=True) + EPSILON)
        unit = center * rstd
        unit_ref[rows, :] = unit
        rstd_ref[rows, :] = jnp.broadcast_to(rstd, (length, LANES))
        gated_ref[rows, :] = (unit * act_ref[rows, :V_COLS].astype(jnp.float32)).astype(jnp.bfloat16)
        return 0

    lax.fori_loop(0, micro, finish, 0)


def attend(activated, mask, micro, length):
    tokens = micro * length
    return pl.pallas_call(
        functools.partial(attend_kernel, micro, length),
        out_shape=(
            jax.ShapeDtypeStruct((micro * HEADS * length, length), jnp.float32),
            jax.ShapeDtypeStruct((tokens, V_COLS), jnp.float32),
            jax.ShapeDtypeStruct((tokens, LANES), jnp.float32),
            jax.ShapeDtypeStruct((tokens, V_COLS), jnp.bfloat16),
        ),
        in_specs=[VMEM] * 2,
        out_specs=(VMEM,) * 4,
        scratch_shapes=[pltpu.VMEM((tokens, V_COLS), jnp.float32)],
        name="attend",
    )(activated, mask)


def chain_kernel(
    micro, length, sections,
    top_ref, input_ref, act_ref, pre_ref, score_ref, unit_ref, rstd_ref, mask_ref, first_ref, second_ref,
    up_ref, gpre_ref, gin_ref,
    landed, leaving, ggate, dmix, gnorm, send_sem, recv_sem,
):
    section = lax.axis_index("pipe")
    width = input_ref.shape[1]
    tile = 2 * LANES
    lane = lax.broadcasted_iota(jnp.int32, (length, LANES), 1)
    is_last = section == sections - 1
    is_first = section == 0

    barrier = pltpu.get_barrier_semaphore()

    @pl.when(jnp.logical_not(is_last))
    def _():
        pl.semaphore_signal(
            barrier, inc=1, device_id={"pipe": jnp.minimum(section + 1, sections - 1)}, device_id_type=MESH
        )

    @pl.when(jnp.logical_not(is_first))
    def _():
        pl.semaphore_wait(barrier, 1)

    def copy_of(slot):
        return pltpu.make_async_remote_copy(
            src_ref=leaving.at[slot],
            dst_ref=landed.at[slot],
            send_sem=send_sem.at[slot],
            recv_sem=recv_sem.at[slot],
            device_id={"pipe": jnp.maximum(section - 1, 0)},
            device_id_type=MESH,
        )

    def store_grad(rows, cols, size, value):
        rounded = value.astype(jnp.bfloat16).astype(jnp.float32)
        gpre_ref[rows, at(cols, size)] = (
            rounded * silu_slope(pre_ref[rows, at(cols, size)])
        ).astype(jnp.bfloat16)

    for slot in range(micro):
        rows = pl.ds(slot * length, length)

        @pl.when(is_last)
        def _():
            up_ref[rows, :] = top_ref[rows, :]

        @pl.when(jnp.logical_not(is_last))
        def _():
            copy_of(slot).wait_recv()
            up_ref[rows, :] = landed[slot]

        def gate_tile(index, _):
            ggate[:, at(index * tile, tile)] = dot_nt(up_ref[rows, :], second_ref[at(index * tile, tile), :])
            return 0

        lax.fori_loop(0, V_COLS // tile, gate_tile, 0)
        gating = act_ref[rows, :V_COLS].astype(jnp.float32)
        unit = unit_ref[rows, :]
        grad = ggate[...]
        store_grad(rows, 0, V_COLS, grad * unit)
        grad = grad * gating
        mean_grad = jnp.mean(grad, axis=-1, keepdims=True)
        mean_unit = jnp.mean(grad * unit, axis=-1, keepdims=True)
        dmix[...] = (rstd_ref[rows, :1] * (grad - mean_grad - unit * mean_unit)).astype(jnp.bfloat16)

        def one(group, _):
            queries = act_ref[rows, at(2 * V_COLS + group * LANES, LANES)]
            keys = act_ref[rows, at(2 * V_COLS + Q_COLS + group * LANES, LANES)]
            mask = mask_ref[rows, :]
            grad_q = jnp.zeros((length, LANES), jnp.float32)
            grad_k = jnp.zeros((length, LANES), jnp.float32)
            for half in range(GROUP_V // LANES):
                cols = group * GROUP_V + half * LANES
                values = act_ref[rows, at(V_COLS + cols, LANES)]
                grad_mix = dmix[:, at(cols, LANES)]
                grad_v = jnp.zeros((length, LANES), jnp.float32)
                for sub in range(V_HEADS):
                    head = half * V_HEADS + sub
                    mix_head = only_head(grad_mix, lane, V_DIM, sub)
                    place = (slot * HEADS + group * QK_HEADS + head) * length
                    score = score_ref[at(place, length), :]
                    squash = jax.nn.sigmoid(score)
                    weight = (score * squash * mask).astype(jnp.bfloat16)
                    slope = squash * (1.0 + score * (1.0 - squash)) * mask * SCALE
                    grad_score = (dot_nt(mix_head, values) * slope).astype(jnp.bfloat16)
                    grad_v += contract_rows(weight, mix_head)
                    grad_q += dot_nn(grad_score, only_head(keys, lane, QK_DIM, head))
                    grad_k += contract_rows(grad_score, only_head(queries, lane, QK_DIM, head))
                store_grad(rows, V_COLS + cols, LANES, grad_v)
            store_grad(rows, 2 * V_COLS + group * LANES, LANES, grad_q)
            store_grad(rows, 2 * V_COLS + Q_COLS + group * LANES, LANES, grad_k)
            return 0

        lax.fori_loop(0, GROUPS, one, 0)

        def norm_tile(index, _):
            gnorm[:, at(index * tile, tile)] = dot_nt(gpre_ref[rows, :], first_ref[at(index * tile, tile), :])
            return 0

        lax.fori_loop(0, width // tile, norm_tile, 0)
        value = input_ref[rows, :].astype(jnp.float32)
        center = value - jnp.mean(value, axis=-1, keepdims=True)
        rstd = lax.rsqrt(jnp.mean(center * center, axis=-1, keepdims=True) + EPSILON)
        unit = center * rstd
        grad = gnorm[...]
        mean_grad = jnp.mean(grad, axis=-1, keepdims=True)
        mean_unit = jnp.mean(grad * unit, axis=-1, keepdims=True)
        through = rstd * (grad - mean_grad - unit * mean_unit)
        result = (up_ref[rows, :].astype(jnp.float32) + through).astype(jnp.bfloat16)
        leaving[slot] = result
        gin_ref[rows, :] = result

        @pl.when(jnp.logical_not(is_first))
        def _():
            copy_of(slot).start()

    for slot in range(micro):

        @pl.when(jnp.logical_not(is_first))
        def _():
            copy_of(slot).wait_send()


def chain(top, inputs, activated, preact, scores, unit, rstd, mask, w_first, w_second, micro, length):
    tokens, width = inputs.shape
    return pl.pallas_call(
        functools.partial(chain_kernel, micro, length, lax.axis_size("pipe")),
        out_shape=(
            jax.ShapeDtypeStruct((tokens, width), jnp.bfloat16),
            jax.ShapeDtypeStruct(preact.shape, jnp.bfloat16),
            jax.ShapeDtypeStruct((tokens, width), jnp.bfloat16),
        ),
        in_specs=[VMEM] * 10,
        out_specs=(VMEM,) * 3,
        scratch_shapes=[
            pltpu.VMEM((micro, length, width), jnp.bfloat16),
            pltpu.VMEM((micro, length, width), jnp.bfloat16),
            pltpu.VMEM((length, V_COLS), jnp.float32),
            pltpu.VMEM((length, V_COLS), jnp.bfloat16),
            pltpu.VMEM((length, width), jnp.float32),
            pltpu.SemaphoreType.DMA((micro,)),
            pltpu.SemaphoreType.DMA((micro,)),
        ],
        compiler_params=pltpu.CompilerParams(
            collective_id=0, has_side_effects=True, vmem_limit_bytes=60 * 1024 * 1024
        ),
        name="chain",
    )(top, inputs, activated, preact, scores, unit, rstd, mask, w_first, w_second)


def add_into(target, left, right):
    step = 32

    def one(index, _):
        rows = pl.ds(pl.multiple_of(index * step, step), step)
        total = left[rows, :].astype(jnp.float32) + right[rows, :].astype(jnp.float32)
        target[rows, :] = total.astype(target.dtype)
        return 0

    lax.fori_loop(0, target.shape[0] // step, one, 0)


def scatter_kernel(line, part_a, part_b, out_a, out_b, *scratch):
    pairs = (
        (part_a, out_a) + scratch[0:4],
        (part_b, out_b) + scratch[4:8],
    )
    load_sem, pair_send, pair_recv, right_send, right_recv, left_send, left_recv = scratch[8:]
    rank = lax.axis_index("dp")
    spot, lane_of = rank // 2, rank % 2
    has_left, has_right = spot > 0, spot < line - 1
    partner = spot * 2 + 1 - lane_of
    right = jnp.minimum(spot + 1, line - 1) * 2 + lane_of
    left = jnp.maximum(spot - 1, 0) * 2 + lane_of

    barrier = pltpu.get_barrier_semaphore()
    pl.semaphore_signal(barrier, inc=1, device_id={"dp": partner}, device_id_type=MESH)

    @pl.when(has_left)
    def _():
        pl.semaphore_signal(barrier, inc=1, device_id={"dp": left}, device_id_type=MESH)

    @pl.when(has_right)
    def _():
        pl.semaphore_signal(barrier, inc=1, device_id={"dp": right}, device_id_type=MESH)

    pl.semaphore_wait(barrier, 1 + jnp.minimum(spot, 1) + jnp.minimum(line - 1 - spot, 1))

    def block_at(turn):
        near = jnp.minimum(spot, line - 1 - spot)
        ahead = line - 1 - 2 * near
        lone = jnp.where(spot <= line - 1 - spot, line - 1 - turn, turn)
        after = jnp.maximum(turn - ahead, 0)
        reach = near - after // 2
        both = jnp.where(after % 2 == 0, spot + reach, spot - reach)
        return jnp.where(turn < ahead, lone, both)

    def load_of(which, block):
        part, _, own, _, _, _ = pairs[which]
        return pltpu.make_async_copy(part.at[block, lane_of], own.at[block], load_sem.at[which, block])

    def pair_of(which, block):
        part, _, _, paired, _, _ = pairs[which]
        return pltpu.make_async_remote_copy(
            src_ref=part.at[block, 1 - lane_of], dst_ref=paired.at[block],
            send_sem=pair_send.at[which, block], recv_sem=pair_recv.at[which, block],
            device_id={"dp": partner}, device_id_type=MESH,
        )

    def flow_of(which, block, rightward, source):
        flow = pairs[which][4 if rightward else 5]
        sends, recvs = (right_send, right_recv) if rightward else (left_send, left_recv)
        return pltpu.make_async_remote_copy(
            src_ref=source.at[block], dst_ref=flow.at[block],
            send_sem=sends.at[which, block], recv_sem=recvs.at[which, block],
            device_id={"dp": right if rightward else left}, device_id_type=MESH,
        )

    def begin(turn, _):
        block = block_at(turn)
        for which in range(2):
            pair_of(which, block).start()
            load_of(which, block).start()
        return 0

    lax.fori_loop(0, line, begin, 0)

    def pass_on(turn, _):
        block = block_at(turn)
        for which in range(2):
            own, paired = pairs[which][2:4]
            load_of(which, block).wait()
            pair_of(which, block).wait_recv()
            add_into(own.at[block], own.at[block], paired.at[block])
            for rightward in (True, False):
                flow = pairs[which][4 if rightward else 5]
                fed = has_left if rightward else has_right
                wanted = block > spot if rightward else block < spot

                @pl.when(jnp.logical_and(wanted, fed))
                def _():
                    flow_of(which, block, rightward, flow).wait_recv()
                    add_into(flow.at[block], flow.at[block], own.at[block])
                    flow_of(which, block, rightward, flow).start()

                @pl.when(jnp.logical_and(wanted, jnp.logical_not(fed)))
                def _():
                    flow_of(which, block, rightward, own).start()
        return 0

    lax.fori_loop(0, line, pass_on, 0)

    for which in range(2):
        out, own = pairs[which][1:3]
        for rightward in (True, False):
            flow = pairs[which][4 if rightward else 5]

            @pl.when(has_left if rightward else has_right)
            def _():
                flow_of(which, spot, rightward, flow).wait_recv()

        @pl.when(jnp.logical_and(has_left, has_right))
        def _():
            add_into(out, own.at[spot], pairs[which][4].at[spot])
            add_into(out, out, pairs[which][5].at[spot])

        @pl.when(jnp.logical_and(has_left, jnp.logical_not(has_right)))
        def _():
            add_into(out, own.at[spot], pairs[which][4].at[spot])

        @pl.when(jnp.logical_and(has_right, jnp.logical_not(has_left)))
        def _():
            add_into(out, own.at[spot], pairs[which][5].at[spot])

    def finish(block, _):
        for which in range(2):
            pair_of(which, block).wait_send()
            for rightward in (True, False):

                @pl.when(block > spot if rightward else block < spot)
                def _():
                    flow_of(which, block, rightward, pairs[which][2]).wait_send()
        return 0

    lax.fori_loop(0, line, finish, 0)


def scatter_sums(part_a, part_b):
    devices = lax.axis_size("dp")
    line = devices // 2
    parts = [part.reshape(line, 2, part.shape[0] // devices, part.shape[1]) for part in (part_a, part_b)]
    scratch = []
    for part in parts:
        scratch += [pltpu.VMEM((line,) + part.shape[2:], part.dtype)] * 4
    scratch += [pltpu.SemaphoreType.DMA((2, line))] * 7
    return pl.pallas_call(
        functools.partial(scatter_kernel, line),
        out_shape=tuple(jax.ShapeDtypeStruct(part.shape[2:], jnp.float32) for part in parts),
        in_specs=[pl.BlockSpec(memory_space=pl.ANY)] * 2,
        out_specs=(VMEM,) * 2,
        scratch_shapes=scratch,
        compiler_params=pltpu.CompilerParams(
            collective_id=1, has_side_effects=True, vmem_limit_bytes=60 * 1024 * 1024
        ),
        name="scatter_sums",
    )(*parts)


def mask_of(segments):
    length = segments.shape[1]
    same = segments[:, :, None] == segments[:, None, :]
    positions = lax.broadcasted_iota(jnp.int32, (length, length), 0)
    columns = lax.broadcasted_iota(jnp.int32, (length, length), 1)
    counts = jnp.sum(same.astype(jnp.float32), axis=2, keepdims=True)
    allowed = jnp.logical_and(same, (columns <= positions)[None])
    return (allowed.astype(jnp.float32) / counts).reshape(-1, length)


def body(section_input, top_grad, w_in, w_out, segments):
    micro, length = segments.shape
    inputs = section_input[0]
    w_first = lax.all_gather(w_in[0], "dp", axis=0, tiled=True)
    w_mine, w_first = lax.optimization_barrier((w_out[0], w_first))
    w_second = lax.all_gather(w_mine, "dp", axis=0, tiled=True)
    mask = mask_of(segments)
    normed = norm_rows(inputs.astype(jnp.float32)).astype(jnp.bfloat16)
    preact = jnp.dot(normed, w_first, preferred_element_type=jnp.float32)
    activated = jax.nn.silu(preact).astype(jnp.bfloat16)
    scores, unit, rstd, gated = attend(activated, mask, micro, length)
    upstream, grad_preact, grads = chain(
        top_grad, inputs, activated, preact, scores, unit, rstd, mask, w_first, w_second, micro, length
    )
    part_out = contract_rows(gated, upstream).astype(jnp.bfloat16)
    part_in = contract_rows(normed, grad_preact).astype(jnp.bfloat16)
    grad_first, grad_out = scatter_sums(part_in, part_out)
    return (grads[None], grad_first[None], grad_out[None])


CORES = 2


class Place:
    def __init__(self):
        self.pipe, self.dp = lax.axis_index("pipe"), lax.axis_index("dp")
        self.x, self.core = self.pipe // CORES, self.pipe % CORES
        self.z, self.y = self.dp // CORES, self.dp % CORES

    def device(self, x=None, core=None, z=None, y=None, pipe=None):
        x = self.x if x is None else x
        core = self.core if core is None else core
        z = self.z if z is None else z
        y = self.y if y is None else y
        return {"pipe": x * CORES + core if pipe is None else pipe, "dp": z * CORES + y}


def signal(sem, device):
    pl.semaphore_signal(sem, inc=1, device_id=device, device_id_type=MESH)


def remote(src, dst, send, recv, device):
    return pltpu.make_async_remote_copy(
        src_ref=src, dst_ref=dst, send_sem=send, recv_sem=recv, device_id=device, device_id_type=MESH
    )


def either(local_if, local, far):
    pl.when(local_if)(local)
    pl.when(jnp.logical_not(local_if))(far)


def turned(index):
    return index % CORES * CORES + index // CORES


def layer_order(step, z, layers):
    return jnp.where(2 * z < layers, (z + step) % layers, (z + layers - step) % layers)


def work_kernel(
    micro, length, layers,
    input_ref, top_ref, w_in_ref, w_out_ref, home_mask_ref,
    out_first, out_second, out_grads,
    grads_ref, up_ref, gpre_ref, normed_ref, gated_ref,
    first, second, stage_first, stage_second, work_in, top, mask,
    unit_in, rstd_in, slope, act, weight, weight_slope, unit, rstd, mixed, landed, ggate, gnorm,
    swap_send, swap_recv, top_send, top_recv, pre_send, pre_recv, own_send, hop_send, to_core, to_x, to_y, came,
    chain_send, chain_recv, back_send, back_recv,
    *sums,
):
    me = Place()
    width = work_in.shape[1]
    tokens = micro * length
    section = me.z
    other_x, other_core, other_y = 1 - me.x, 1 - me.core, 1 - me.y
    at_home = me.pipe == me.z
    is_last, is_first = section == layers - 1, section == 0
    weights = (
        (w_in_ref, first, stage_first),
        (w_out_ref, second, stage_second),
    )
    sizes = [ref.shape[0] // 4 for ref, _, _ in weights]

    def quarter(which, block, half, core):
        size = sizes[which]
        start = pl.multiple_of(((block * 2 + half) * CORES + core) * size, size)
        return weights[which][1].at[pl.ds(start, size), :]

    def shard(which, half, core):
        size = sizes[which]
        start = pl.multiple_of((half * CORES + core) * size, size)
        return weights[which][0].at[pl.ds(start, size), :]

    def came_at(which, block, half, core):
        return came.at[which, (block * 2 + half) * CORES + core]

    barrier = pltpu.get_barrier_semaphore()
    def greet(index, _):
        pipe, layer = index // layers, index % layers

        @pl.when(jnp.logical_not(jnp.logical_and(pipe == me.pipe, layer == me.z)))
        def _():
            signal(barrier, {"pipe": pipe, "dp": layer * CORES + me.y})

        return 0

    lax.fori_loop(0, layers * layers, greet, 0)
    signal(barrier, me.device(y=other_y))
    pl.semaphore_wait(barrier, layers * layers)

    away = {"pipe": turned(me.z), "dp": me.pipe * CORES + me.y}
    back = {"pipe": me.z, "dp": turned(me.pipe) * CORES + me.y}
    stays = jnp.logical_and(at_home, turned(me.pipe) == me.pipe)
    swaps = ((input_ref, work_in), (home_mask_ref, mask))

    def swap_far(index):
        src, dst = swaps[index]
        return remote(src, dst, swap_send.at[index], swap_recv.at[index], away)

    def swap_near(index):
        src, dst = swaps[index]
        return pltpu.make_async_copy(src, dst, swap_recv.at[index])

    def swap_start():
        for index in range(2):
            either(stays, lambda: swap_near(index).start(), lambda: swap_far(index).start())

    def before(which, core):
        return remote(
            shard(which, other_x, core), weights[which][2].at[me.core],
            pre_send.at[which, core], pre_recv.at[which, me.core], me.device(x=other_x, core=core),
        )

    def own(which, core):
        return remote(
            shard(which, me.x, core), quarter(which, me.dp, me.x, core),
            own_send.at[which, core], came_at(which, me.dp, me.x, core), me.device(core=core, z=me.pipe),
        )

    def own_near(which, core):
        return pltpu.make_async_copy(
            shard(which, me.x, core), quarter(which, me.dp, me.x, core), came_at(which, me.dp, me.x, core)
        )

    def hop(which, source):
        return remote(
            weights[which][2].at[source], quarter(which, me.dp, me.x, me.core),
            hop_send.at[which, source], came_at(which, me.dp, me.x, me.core),
            me.device(z=other_x * CORES + source),
        )

    def hop_near(which, source):
        return pltpu.make_async_copy(
            weights[which][2].at[source], quarter(which, me.dp, me.x, me.core),
            came_at(which, me.dp, me.x, me.core),
        )

    def before_came(which, source):
        return remote(
            shard(which, other_x, me.core), weights[which][2].at[source],
            pre_send.at[which, source], pre_recv.at[which, source], me.device(x=other_x),
        )

    for which in range(2):
        for core in range(CORES):
            before(which, core).start()
        for core in range(CORES):
            near = jnp.logical_and(at_home, core == me.core)
            either(near, lambda: own_near(which, core).start(), lambda: own(which, core).start())

    for which in range(2):
        for source in range(CORES):
            before_came(which, source).wait_recv()
            either(
                other_x * CORES + source == me.z,
                lambda: hop_near(which, source).start(),
                lambda: hop(which, source).start(),
            )

    top_far = remote(top_ref, top, top_send, top_recv, me.device(z=layers - 1))
    top_near = pltpu.make_async_copy(top_ref, top, top_recv)
    has_top = me.z == turned(me.pipe)
    gives_top = jnp.logical_and(has_top, jnp.logical_not(is_last))
    keeps_top = jnp.logical_and(has_top, is_last)

    def top_start():
        pl.when(gives_top)(lambda: top_far.start())
        pl.when(keeps_top)(lambda: top_near.start())

    def send(which, block, half, core, sem, index, device):
        place = quarter(which, block, half, core)
        return remote(place, place, sem.at[which, index], came_at(which, block, half, core), device)

    def direct_block(step):
        return layer_order(step, me.z, layers) * CORES + me.y

    def core_copy(which, kind, step):
        block = direct_block(step)
        lane = kind // 2
        block = block if lane == 0 else block - me.y + other_y
        half = me.x if kind % 2 == 0 else other_x
        return send(which, block, half, me.core, to_core, kind * layers + step, me.device(core=other_core))

    def x_copy(which, step):
        return send(which, direct_block(step), me.x, me.core, to_x, step, me.device(x=other_x))

    def y_copy(which, kind, step):
        half = me.x if kind == 0 else other_x
        return send(which, direct_block(step), half, me.core, to_y, kind * layers + step, me.device(y=other_y))

    def arrived(which, block, half, core):
        place = quarter(which, block, half, core)
        return remote(
            place, place, to_core.at[which, 0], came_at(which, block, half, core), me.device(core=other_core)
        )

    def settled(which):
        for core in range(CORES):
            near = jnp.logical_and(at_home, core == me.core)
            pl.when(jnp.logical_not(near))(lambda: own(which, core).wait_send())
        for source in range(CORES):
            near = other_x * CORES + source == me.z
            pl.when(jnp.logical_not(near))(lambda: hop(which, source).wait_send())

    def direct_ready(which, step):
        block = direct_block(step)
        if step == 0:
            far = jnp.logical_and(me.x == me.z // CORES, me.core != me.z % CORES)
            place = quarter(which, block, me.x, me.core)
            either(
                jnp.logical_not(far),
                lambda: pltpu.make_async_copy(shard(which, 0, 0), place, came_at(which, block, me.x, me.core)).wait(),
                lambda: arrived(which, block, me.x, me.core).wait_recv(),
            )
        else:
            arrived(which, block, me.x, me.core).wait_recv()
        x_copy(which, step).start()
        y_copy(which, 0, step).start()
        core_copy(which, 0, step).start()

    def from_x(which, step):
        arrived(which, direct_block(step), other_x, me.core).wait_recv()
        y_copy(which, 1, step).start()
        core_copy(which, 1, step).start()

    def from_y(which, kind, step):
        block = direct_block(step) - me.y + other_y
        arrived(which, block, me.x if kind == 0 else other_x, me.core).wait_recv()
        core_copy(which, 2 + kind, step).start()

    def whole(which):
        def one(index, _):
            arrived(which, index // 2, index % 2, other_core).wait_recv()
            return 0

        lax.fori_loop(0, 2 * layers * CORES, one, 0)

    for step in range(layers + 1):
        if step == 3:
            for which in range(2):
                settled(which)
            swap_start()
            top_start()
        if step < layers:
            direct_ready(0, step)
        if step >= 1:
            from_x(0, step - 1)
            from_y(0, 0, step - 1)
        if step >= 2:
            from_y(0, 1, step - 2)
    for step in range(layers):
        direct_ready(1, step)
    for index in range(2):
        either(stays, lambda: swap_near(index).wait(), lambda: swap_far(index).wait_recv())
    norm_input(work_in, normed_ref, unit_in, rstd_in)
    from_y(0, 1, layers - 1)
    for step in range(layers):
        from_x(1, step)
    whole(0)
    tile = 2 * LANES

    def front(index, _):
        cols = at(index * tile, tile)
        value = dot_nn(normed_ref[...], first[:, cols])
        squash = jax.nn.sigmoid(value)
        act[:, cols] = (value * squash).astype(jnp.bfloat16)
        slope[:, cols] = squash * (1.0 + value * (1.0 - squash))
        return 0

    lax.fori_loop(0, slope.shape[1] // tile, front, 0)
    for step in range(layers):
        from_y(1, 0, step)
    attend_front(micro, length, act, mask, weight, weight_slope, unit, rstd, gated_ref, mixed)
    for step in range(layers):
        from_y(1, 1, step)
    whole(1)

    def copy_of(slot):
        return remote(
            grads_ref.at[pl.ds(slot * length, length), :], landed.at[slot], chain_send.at[slot], chain_recv.at[slot],
            me.device(z=jnp.maximum(me.z - 1, 0)),
        )

    def back_far(slot):
        rows = pl.ds(slot * length, length)
        return remote(grads_ref.at[rows, :], out_grads.at[rows, :], back_send.at[slot], back_recv.at[slot], back)

    def back_near(slot):
        rows = pl.ds(slot * length, length)
        return pltpu.make_async_copy(grads_ref.at[rows, :], out_grads.at[rows, :], back_recv.at[slot])

    def back_one(slot):
        either(stays, lambda: back_near(slot).start(), lambda: back_far(slot).start())

    def back_start():
        for slot in range(micro):
            back_one(slot)

    @pl.when(jnp.logical_and(is_last, jnp.logical_not(has_top)))
    def _():
        top_far.wait_recv()

    @pl.when(keeps_top)
    def _():
        top_near.wait()

    chain_steps(
        micro, length, is_first, is_last, copy_of, back_one,
        top, unit_in, rstd_in, act, slope, weight, weight_slope, unit, rstd, first, second,
        grads_ref, up_ref, gpre_ref, landed, ggate, gnorm,
    )

    for slot in range(micro):

        @pl.when(jnp.logical_not(is_first))
        def _():
            copy_of(slot).wait_send()

    for index in range(2):
        pl.when(jnp.logical_not(stays))(lambda: swap_far(index).wait_send())
    pl.when(gives_top)(lambda: top_far.wait_send())
    for which in range(2):
        for core in range(CORES):
            before(which, core).wait_send()

        def sent(step, _):
            x_copy(which, step).wait_send()
            for kind in range(2):
                y_copy(which, kind, step).wait_send()
            for kind in range(4):
                core_copy(which, kind, step).wait_send()
            return 0

        lax.fori_loop(0, layers, sent, 0)

    sum_weights(
        me, layers, normed_ref, gpre_ref, gated_ref, up_ref, out_first, out_second, first, second, *sums,
        lambda: pl.when(jnp.logical_not(is_first))(back_start),
    )
    for slot in range(micro):
        either(stays, lambda: back_near(slot).wait(), lambda: back_far(slot).wait())


def folded(value):
    total = value[:, :LANES]
    for start in range(LANES, value.shape[1], LANES):
        total = total + value[:, start : start + LANES]
    return total


def norm_input(work_in, normed_ref, unit_in, rstd_in):
    step = 64
    width = work_in.shape[1]

    def one(index, _):
        rows = pl.ds(pl.multiple_of(index * step, step), step)
        value = work_in[rows, :].astype(jnp.float32)
        center = value - jnp.mean(value, axis=-1, keepdims=True)
        rstd = lax.rsqrt(jnp.mean(center * center, axis=-1, keepdims=True) + EPSILON)
        unit = center * rstd
        unit_in[rows, :] = unit
        normed_ref[rows, :] = unit.astype(jnp.bfloat16)
        rstd_in[rows, :] = jnp.broadcast_to(rstd, (step, LANES))
        return 0

    lax.fori_loop(0, work_in.shape[0] // step, one, 0)


def attend_front(micro, length, act_ref, mask_ref, weight_ref, slope_ref, unit_ref, rstd_ref, gated_ref, mixed):
    lane = lax.broadcasted_iota(jnp.int32, (length, LANES), 1)

    def one(index, _):
        slot, group = index // GROUPS, index % GROUPS
        rows = at(slot * length, length)
        queries = act_ref[rows, at(2 * V_COLS + group * LANES, LANES)]
        keys = act_ref[rows, at(2 * V_COLS + Q_COLS + group * LANES, LANES)]
        mask = mask_ref[rows, :]
        for half in range(GROUP_V // LANES):
            cols = group * GROUP_V + half * LANES
            values = act_ref[rows, at(V_COLS + cols, LANES)]
            total = jnp.zeros((length, LANES), jnp.float32)
            for sub in range(V_HEADS):
                head = half * V_HEADS + sub
                score = dot_nt(only_head(queries, lane, QK_DIM, head), keys) * SCALE
                squash = jax.nn.sigmoid(score)
                place = at((index * QK_HEADS + head) * length, length)
                slope_ref[place, :] = squash * (1.0 + score * (1.0 - squash)) * (mask * SCALE)
                weight = (score * squash * mask).astype(jnp.bfloat16)
                weight_ref[place, :] = weight
                total += dot_nn(weight, only_head(values, lane, V_DIM, sub))
            mixed[rows, at(cols, LANES)] = total
        return 0

    lax.fori_loop(0, micro * GROUPS, one, 0)
    step = 64

    def finish(index, _):
        rows = pl.ds(pl.multiple_of(index * step, step), step)
        value = mixed[rows, :]
        center = value - jnp.mean(value, axis=-1, keepdims=True)
        rstd = lax.rsqrt(jnp.mean(center * center, axis=-1, keepdims=True) + EPSILON)
        unit = center * rstd
        unit_ref[rows, :] = unit
        rstd_ref[rows, :] = jnp.broadcast_to(rstd, (step, LANES))
        gated_ref[rows, :] = (unit * act_ref[rows, :V_COLS].astype(jnp.float32)).astype(jnp.bfloat16)
        return 0

    lax.fori_loop(0, micro * length // step, finish, 0)


def chain_steps(
    micro, length, is_first, is_last, copy_of, back_one,
    top_ref, unit_in, rstd_in, act_ref, slope_ref, weight_ref, weight_slope, unit_ref, rstd_ref, first_ref, second_ref,
    grads_ref, up_ref, gpre_ref, landed, ggate, gnorm,
):
    width = unit_in.shape[1]
    tile = 2 * LANES
    lane = lax.broadcasted_iota(jnp.int32, (length, LANES), 1)
    nothing = jnp.zeros((length, LANES), jnp.float32)

    def store_grad(rows, cols, size, value):
        rounded = value.astype(jnp.bfloat16).astype(jnp.float32)
        gpre_ref[rows, at(cols, size)] = (rounded * slope_ref[rows, at(cols, size)]).astype(jnp.bfloat16)

    for slot in range(micro):
        rows = pl.ds(slot * length, length)

        @pl.when(is_last)
        def _():
            up_ref[rows, :] = top_ref[rows, :]

        @pl.when(jnp.logical_not(is_last))
        def _():
            copy_of(slot).wait_recv()
            up_ref[rows, :] = landed[slot]

        def gate_tile(index, sums):
            cols = at(index * tile, tile)
            grad = dot_nt(up_ref[rows, :], second_ref[cols, :])
            unit = unit_ref[rows, cols]
            store_grad(rows, index * tile, tile, grad * unit)
            grad = grad * act_ref[rows, cols].astype(jnp.float32)
            ggate[:, cols] = grad
            return sums[0] + folded(grad), sums[1] + folded(grad * unit)

        sums = lax.fori_loop(0, V_COLS // tile, gate_tile, (nothing, nothing))
        mean_grad, mean_unit = [jnp.sum(part, axis=-1, keepdims=True) * (1.0 / V_COLS) for part in sums]
        rstd = rstd_ref[rows, :1]

        def one(group, _):
            queries = act_ref[rows, at(2 * V_COLS + group * LANES, LANES)]
            keys = act_ref[rows, at(2 * V_COLS + Q_COLS + group * LANES, LANES)]
            grad_q = jnp.zeros((length, LANES), jnp.float32)
            grad_k = jnp.zeros((length, LANES), jnp.float32)
            for half in range(GROUP_V // LANES):
                cols = group * GROUP_V + half * LANES
                values = act_ref[rows, at(V_COLS + cols, LANES)]
                spread = ggate[:, at(cols, LANES)] - mean_grad - unit_ref[rows, at(cols, LANES)] * mean_unit
                grad_mix = (rstd * spread).astype(jnp.bfloat16)
                grad_v = jnp.zeros((length, LANES), jnp.float32)
                for sub in range(V_HEADS):
                    head = half * V_HEADS + sub
                    mix_head = only_head(grad_mix, lane, V_DIM, sub)
                    place = at((slot * HEADS + group * QK_HEADS + head) * length, length)
                    grad_score = (dot_nt(mix_head, values) * weight_slope[place, :]).astype(jnp.bfloat16)
                    grad_v += contract_rows(weight_ref[place, :], mix_head)
                    grad_q += dot_nn(grad_score, only_head(keys, lane, QK_DIM, head))
                    grad_k += contract_rows(grad_score, only_head(queries, lane, QK_DIM, head))
                store_grad(rows, V_COLS + cols, LANES, grad_v)
            store_grad(rows, 2 * V_COLS + group * LANES, LANES, grad_q)
            store_grad(rows, 2 * V_COLS + Q_COLS + group * LANES, LANES, grad_k)
            return 0

        lax.fori_loop(0, GROUPS, one, 0)

        def norm_tile(index, sums):
            cols = at(index * tile, tile)
            grad = dot_nt(gpre_ref[rows, :], first_ref[cols, :])
            gnorm[:, cols] = grad
            return sums[0] + folded(grad), sums[1] + folded(grad * unit_in[rows, cols])

        sums = lax.fori_loop(0, width // tile, norm_tile, (nothing, nothing))
        mean_grad, mean_unit = [jnp.sum(part, axis=-1, keepdims=True) * (1.0 / width) for part in sums]
        rstd = rstd_in[rows, :1]

        def pass_tile(index, _):
            cols = at(index * tile, tile)
            through = rstd * (gnorm[:, cols] - mean_grad - unit_in[rows, cols] * mean_unit)
            grads_ref[rows, cols] = (up_ref[rows, cols].astype(jnp.float32) + through).astype(jnp.bfloat16)
            return 0

        lax.fori_loop(0, width // tile, pass_tile, 0)

        @pl.when(jnp.logical_not(is_first))
        def _():
            copy_of(slot).start()

        back_one(slot)


ANY = pl.BlockSpec(memory_space=pl.ANY)
LIMIT = 60 * 1024 * 1024


def work(inputs, top_grad, w_in, w_out, mask, micro, length):
    tokens, width = inputs.shape
    layers, blocks = lax.axis_size("pipe"), lax.axis_size("dp")
    columns = w_in.shape[1]
    quarters = [w.shape[0] // 4 for w in (w_in, w_out)]
    dma = pltpu.SemaphoreType.DMA
    return pl.pallas_call(
        functools.partial(work_kernel, micro, length, layers),
        out_shape=tuple(jax.ShapeDtypeStruct(a.shape, a.dtype) for a in (w_in, w_out, inputs)),
        in_specs=[ANY] * 5,
        out_specs=(ANY,) * 3,
        scratch_shapes=[
            pltpu.VMEM((tokens, width), jnp.bfloat16),
            pltpu.VMEM((tokens, width), jnp.bfloat16),
            pltpu.VMEM((tokens, columns), jnp.bfloat16),
            pltpu.VMEM((tokens, width), jnp.bfloat16),
            pltpu.VMEM((tokens, V_COLS), jnp.bfloat16),
            pltpu.VMEM((blocks * w_in.shape[0], columns), jnp.bfloat16),
            pltpu.VMEM((blocks * w_out.shape[0], width), jnp.bfloat16),
            pltpu.VMEM((CORES, quarters[0], columns), jnp.bfloat16),
            pltpu.VMEM((CORES, quarters[1], width), jnp.bfloat16),
            pltpu.VMEM((tokens, width), jnp.bfloat16),
            pltpu.VMEM((tokens, width), jnp.bfloat16),
            pltpu.VMEM((tokens, length), jnp.float32),
            pltpu.VMEM((tokens, width), jnp.float32),
            pltpu.VMEM((tokens, LANES), jnp.float32),
            pltpu.VMEM((tokens, columns), jnp.float32),
            pltpu.VMEM((tokens, columns), jnp.bfloat16),
            pltpu.VMEM((micro * HEADS * length, length), jnp.bfloat16),
            pltpu.VMEM((micro * HEADS * length, length), jnp.float32),
            pltpu.VMEM((tokens, V_COLS), jnp.float32),
            pltpu.VMEM((tokens, LANES), jnp.float32),
            pltpu.VMEM((tokens, V_COLS), jnp.float32),
            pltpu.VMEM((micro, length, width), jnp.bfloat16),
            pltpu.VMEM((length, V_COLS), jnp.float32),
            pltpu.VMEM((length, width), jnp.float32),
            dma((2,)), dma((2,)), dma, dma,
            dma((2, CORES)), dma((2, CORES)), dma((2, CORES)), dma((2, CORES)),
            dma((2, 4 * layers)), dma((2, layers)), dma((2, 2 * layers)), dma((2, 4 * blocks)),
            dma((micro,)), dma((micro,)), dma((micro,)), dma((micro,)),
        ]
        + [
            pltpu.VMEM((count, size, cols), jnp.bfloat16)
            for count in (2 * blocks, 2 * layers, layers)
            for size, cols in zip(quarters, (columns, width))
        ]
        + [dma((2, count)) for count in (2 * blocks, 2 * layers, layers, layers) for _ in range(2)],
        compiler_params=pltpu.CompilerParams(collective_id=2, has_side_effects=True, vmem_limit_bytes=LIMIT),
        name="work",
    )(inputs, top_grad, w_in, w_out, mask)


def add_rows(target, other):
    step = 16

    def one(index, _):
        rows = pl.ds(pl.multiple_of(index * step, step), step)
        total = target[rows, :].astype(jnp.float32) + other[rows, :].astype(jnp.float32)
        target[rows, :] = total.astype(target.dtype)
        return 0

    lax.fori_loop(0, target.shape[0] // step, one, 0)


def sum_weights(
    me, layers, normed_ref, gpre_ref, gated_ref, up_ref, out_first, out_second, first, second,
    core_first, core_second, early_first, early_second, late_first, late_second,
    core_send, core_recv, y_send, y_recv, x_send, x_recv, home_send, home_recv,
    between,
):
    other_x, other_core, other_y = 1 - me.x, 1 - me.core, 1 - me.y
    at_home = me.pipe == me.z
    sets = (
        (normed_ref, gpre_ref, out_first, first, core_first, early_first, late_first),
        (gated_ref, up_ref, out_second, second, core_second, early_second, late_second),
    )
    sizes = [s[2].shape[0] // 4 for s in sets]

    def quarter(which, block, half, core):
        size = sizes[which]
        start = pl.multiple_of(((block * 2 + half) * CORES + core) * size, size)
        return sets[which][3].at[pl.ds(start, size), :]

    def core_copy(which, block, half, mine):
        core = me.core if mine else other_core
        index = block * 2 + half
        return remote(
            quarter(which, block, half, core), sets[which][4].at[index],
            core_send.at[which, index], core_recv.at[which, index], me.device(core=other_core),
        )

    along_y = me.core == 0
    early_to = {
        "pipe": jnp.where(along_y, me.x, other_x) * CORES + me.core,
        "dp": me.z * CORES + jnp.where(along_y, other_y, me.y),
    }
    late_to = {
        "pipe": jnp.where(along_y, other_x, me.x) * CORES + me.core,
        "dp": me.z * CORES + jnp.where(along_y, me.y, other_y),
    }

    def near_unit(row, index, far):
        lane_of = jnp.where(along_y, other_y if far else me.y, index)
        half = jnp.where(along_y, index, other_x if far else me.x)
        return row * CORES + lane_of, half

    def early_copy(which, row, index):
        block, half = near_unit(row, index, True)
        slot = row * 2 + index
        return remote(
            quarter(which, block, half, me.core), sets[which][5].at[slot],
            y_send.at[which, slot], y_recv.at[which, slot], early_to,
        )

    def late_copy(which, row):
        block, half = near_unit(row, jnp.where(along_y, other_x, other_y), False)
        return remote(
            quarter(which, block, half, me.core), sets[which][6].at[row],
            x_send.at[which, row], x_recv.at[which, row], late_to,
        )

    def home_rows(which, half, core):
        size = sizes[which]
        return sets[which][2].at[pl.ds(pl.multiple_of((half * CORES + core) * size, size), size), :]

    def home_copy(which, row):
        return remote(
            quarter(which, row * CORES + me.y, me.x, me.core), home_rows(which, me.x, me.core),
            home_send.at[which, row], home_recv.at[which, me.x * CORES + me.core],
            {"pipe": me.z, "dp": row * CORES + me.y},
        )

    def home_near(which):
        return pltpu.make_async_copy(
            quarter(which, me.dp, me.x, me.core), home_rows(which, me.x, me.core),
            home_recv.at[which, me.x * CORES + me.core],
        )

    def row_at(step):
        return layer_order(layers - 1 - step, me.z, layers)

    def product(row):
        for which in (1, 0):
            left, right, _, whole = sets[which][:4]
            size = 8 * sizes[which]
            tile = 2 * LANES
            place = pl.ds(pl.multiple_of(row * size, size), size)

            def one(index, _):
                cols = at(index * tile, tile)
                whole[place, cols] = contract_rows(left[:, place], right[:, cols]).astype(whole.dtype)
                return 0

            lax.fori_loop(0, right.shape[1] // tile, one, 0)
            for lane_of in range(CORES):
                for half in range(2):
                    core_copy(which, row * CORES + lane_of, half, False).start()

    def fold_core(row, far):
        for which in (1, 0):

            def one(index, _):
                block, half = near_unit(row, index, far)
                core_copy(which, block, half, True).wait_recv()
                add_rows(quarter(which, block, half, me.core), sets[which][4].at[block * 2 + half])
                return 0

            lax.fori_loop(0, 2, one, 0)

    def start_early(row):
        for which in (1, 0):
            for index in range(2):
                early_copy(which, row, index).start()

    def fold_early(row):
        for which in (1, 0):

            def one(turn, _):
                mine = jnp.where(along_y, me.x, me.y)
                index = jnp.where(turn == 0, 1 - mine, mine)
                block, half = near_unit(row, index, False)
                early_copy(which, row, index).wait_recv()
                add_rows(quarter(which, block, half, me.core), sets[which][5].at[row * 2 + index])
                pl.when(turn == 0)(lambda: late_copy(which, row).start())
                return 0

            lax.fori_loop(0, 2, one, 0)

    def fold_late(row):
        for which in (1, 0):
            late_copy(which, row).wait_recv()
            add_rows(quarter(which, row * CORES + me.y, me.x, me.core), sets[which][6].at[row])
            near = jnp.logical_and(at_home, row == me.z)
            either(near, lambda: home_near(which).start(), lambda: home_copy(which, row).start())

    steps = [row_at(step) for step in range(layers)]
    ahead = 2
    for step in range(layers + 1):
        if step < layers:
            product(steps[step])
        if step >= 1:
            fold_core(steps[step - 1], True)
            if step <= ahead:
                start_early(steps[step - 1])
            fold_core(steps[step - 1], False)
    for step in range(layers + 1):
        if step < layers:
            if step + ahead < layers:
                for which in (1, 0):
                    early_copy(which, steps[step], 0).wait_send()
                    early_copy(which, steps[step], 1).wait_send()
                start_early(steps[step + ahead])
            fold_early(steps[step])
        if step >= 1:
            fold_late(steps[step - 1])
    for which in range(2):
        for pipe in range(layers):
            place = home_rows(which, pipe // CORES, pipe % CORES)
            near = jnp.logical_and(at_home, pipe == me.pipe)
            either(
                near,
                lambda: home_near(which).wait(),
                lambda: remote(
                    place, place, home_send.at[which, 0], home_recv.at[which, pipe], me.device(core=other_core)
                ).wait_recv(),
            )

        def sent(row, _):
            for half in range(2):
                for lane_of in range(2):
                    core_copy(which, row * CORES + lane_of, half, False).wait_send()
            near = jnp.logical_and(at_home, row == me.z)
            pl.when(jnp.logical_not(near))(lambda: home_copy(which, row).wait_send())
            return 0

        lax.fori_loop(0, layers, sent, 0)
        for step in range(layers):
            if step + ahead >= layers:
                early_copy(which, steps[step], 0).wait_send()
                early_copy(which, steps[step], 1).wait_send()
            late_copy(which, steps[step]).wait_send()


def layered_body(section_input, top_grad, w_in, w_out, segments):
    micro, length = segments.shape
    mask = mask_of(segments)
    grad_first, grad_out, grads = work(section_input[0], top_grad, w_in[0], w_out[0], mask, micro, length)
    return (grads[None], grad_first.astype(jnp.float32)[None], grad_out.astype(jnp.float32)[None])


def solution(mesh):
    layered = mesh.shape["pipe"] == CORES * 2 and mesh.shape["dp"] == CORES * mesh.shape["pipe"]
    return jax.shard_map(
        layered_body if layered else body,
        mesh=mesh,
        in_specs=(
            P("pipe", "dp", None),
            P("dp", None),
            P("pipe", "dp", None),
            P("pipe", "dp", None),
            P("dp", None),
        ),
        out_specs=(P("pipe", "dp", None), P("pipe", "dp", None), P("pipe", "dp", None)),
        check_vma=False,
    )
```

```python
import functools

import jax
import jax.numpy as jnp
from jax import lax
from jax.experimental import pallas as pl
from jax.experimental.pallas import tpu as pltpu
from jax.sharding import PartitionSpec as P

HEADS = 16
QK_DIM = 32
V_DIM = 64
LANES = 128

EPSILON = 1e-05
MESH = pl.DeviceIdType.MESH
VMEM = pl.BlockSpec(memory_space=pltpu.VMEM)

QK_HEADS = LANES // QK_DIM
V_HEADS = LANES // V_DIM
GROUPS = HEADS // QK_HEADS
V_COLS = HEADS * V_DIM
Q_COLS = HEADS * QK_DIM
GROUP_V = QK_HEADS * V_DIM
SCALE = QK_DIM ** (-0.5)


def norm_rows(values):
    center = values - jnp.mean(values, axis=-1, keepdims=True)
    return center * lax.rsqrt(jnp.mean(center * center, axis=-1, keepdims=True) + EPSILON)


def silu_slope(preact):
    squash = jax.nn.sigmoid(preact)
    return squash * (1.0 + preact * (1.0 - squash))


def dot_nt(left, right):
    return lax.dot_general(
        left, right, (((1,), (1,)), ((), ())), preferred_element_type=jnp.float32
    )


def dot_nn(left, right):
    return lax.dot_general(
        left, right, (((1,), (0,)), ((), ())), preferred_element_type=jnp.float32
    )


def contract_rows(left, right):
    return lax.dot_general(
        left, right, (((0,), (0,)), ((), ())), preferred_element_type=jnp.float32
    )


def only_head(block, lane, width, index):
    keep = jnp.logical_and(lane >= index * width, lane < (index + 1) * width)
    return jnp.where(keep, block, jnp.zeros_like(block))


def at(start, size):
    return pl.ds(pl.multiple_of(start, LANES), size)


def attend_kernel(micro, length, act_ref, mask_ref, score_ref, unit_ref, rstd_ref, gated_ref, mixed):
    lane = lax.broadcasted_iota(jnp.int32, (length, LANES), 1)

    def one(index, _):
        slot, group = index // GROUPS, index % GROUPS
        rows = at(slot * length, length)
        queries = act_ref[rows, at(2 * V_COLS + group * LANES, LANES)]
        keys = act_ref[rows, at(2 * V_COLS + Q_COLS + group * LANES, LANES)]
        mask = mask_ref[rows, :]
        for half in range(GROUP_V // LANES):
            cols = group * GROUP_V + half * LANES
            values = act_ref[rows, at(V_COLS + cols, LANES)]
            total = jnp.zeros((length, LANES), jnp.float32)
            for sub in range(V_HEADS):
                head = half * V_HEADS + sub
                score = dot_nt(only_head(queries, lane, QK_DIM, head), keys) * SCALE
                score_ref[at((index * QK_HEADS + head) * length, length), :] = score
                weight = (jax.nn.silu(score) * mask).astype(jnp.bfloat16)
                total += dot_nn(weight, only_head(values, lane, V_DIM, sub))
            mixed[rows, at(cols, LANES)] = total
        return 0

    lax.fori_loop(0, micro * GROUPS, one, 0)

    def finish(slot, _):
        rows = at(slot * length, length)
        value = mixed[rows, :]
        center = value - jnp.mean(value, axis=-1, keepdims=True)
        rstd = lax.rsqrt(jnp.mean(center * center, axis=-1, keepdims=True) + EPSILON)
        unit = center * rstd
        unit_ref[rows, :] = unit
        rstd_ref[rows, :] = jnp.broadcast_to(rstd, (length, LANES))
        gated_ref[rows, :] = (unit * act_ref[rows, :V_COLS].astype(jnp.float32)).astype(jnp.bfloat16)
        return 0

    lax.fori_loop(0, micro, finish, 0)


def attend(activated, mask, micro, length):
    tokens = micro * length
    return pl.pallas_call(
        functools.partial(attend_kernel, micro, length),
        out_shape=(
            jax.ShapeDtypeStruct((micro * HEADS * length, length), jnp.float32),
            jax.ShapeDtypeStruct((tokens, V_COLS), jnp.float32),
            jax.ShapeDtypeStruct((tokens, LANES), jnp.float32),
            jax.ShapeDtypeStruct((tokens, V_COLS), jnp.bfloat16),
        ),
        in_specs=[VMEM] * 2,
        out_specs=(VMEM,) * 4,
        scratch_shapes=[pltpu.VMEM((tokens, V_COLS), jnp.float32)],
        name="attend",
    )(activated, mask)


def chain_kernel(
    micro, length, sections,
    top_ref, input_ref, act_ref, pre_ref, score_ref, unit_ref, rstd_ref, mask_ref, first_ref, second_ref,
    up_ref, gpre_ref, gin_ref,
    landed, leaving, ggate, dmix, gnorm, send_sem, recv_sem,
):
    section = lax.axis_index("pipe")
    width = input_ref.shape[1]
    tile = 2 * LANES
    lane = lax.broadcasted_iota(jnp.int32, (length, LANES), 1)
    is_last = section == sections - 1
    is_first = section == 0

    barrier = pltpu.get_barrier_semaphore()

    @pl.when(jnp.logical_not(is_last))
    def _():
        pl.semaphore_signal(
            barrier, inc=1, device_id={"pipe": jnp.minimum(section + 1, sections - 1)}, device_id_type=MESH
        )

    @pl.when(jnp.logical_not(is_first))
    def _():
        pl.semaphore_wait(barrier, 1)

    def copy_of(slot):
        return pltpu.make_async_remote_copy(
            src_ref=leaving.at[slot],
            dst_ref=landed.at[slot],
            send_sem=send_sem.at[slot],
            recv_sem=recv_sem.at[slot],
            device_id={"pipe": jnp.maximum(section - 1, 0)},
            device_id_type=MESH,
        )

    def store_grad(rows, cols, size, value):
        rounded = value.astype(jnp.bfloat16).astype(jnp.float32)
        gpre_ref[rows, at(cols, size)] = (
            rounded * silu_slope(pre_ref[rows, at(cols, size)])
        ).astype(jnp.bfloat16)

    for slot in range(micro):
        rows = pl.ds(slot * length, length)

        @pl.when(is_last)
        def _():
            up_ref[rows, :] = top_ref[rows, :]

        @pl.when(jnp.logical_not(is_last))
        def _():
            copy_of(slot).wait_recv()
            up_ref[rows, :] = landed[slot]

        def gate_tile(index, _):
            ggate[:, at(index * tile, tile)] = dot_nt(up_ref[rows, :], second_ref[at(index * tile, tile), :])
            return 0

        lax.fori_loop(0, V_COLS // tile, gate_tile, 0)
        gating = act_ref[rows, :V_COLS].astype(jnp.float32)
        unit = unit_ref[rows, :]
        grad = ggate[...]
        store_grad(rows, 0, V_COLS, grad * unit)
        grad = grad * gating
        mean_grad = jnp.mean(grad, axis=-1, keepdims=True)
        mean_unit = jnp.mean(grad * unit, axis=-1, keepdims=True)
        dmix[...] = (rstd_ref[rows, :1] * (grad - mean_grad - unit * mean_unit)).astype(jnp.bfloat16)

        def one(group, _):
            queries = act_ref[rows, at(2 * V_COLS + group * LANES, LANES)]
            keys = act_ref[rows, at(2 * V_COLS + Q_COLS + group * LANES, LANES)]
            mask = mask_ref[rows, :]
            grad_q = jnp.zeros((length, LANES), jnp.float32)
            grad_k = jnp.zeros((length, LANES), jnp.float32)
            for half in range(GROUP_V // LANES):
                cols = group * GROUP_V + half * LANES
                values = act_ref[rows, at(V_COLS + cols, LANES)]
                grad_mix = dmix[:, at(cols, LANES)]
                grad_v = jnp.zeros((length, LANES), jnp.float32)
                for sub in range(V_HEADS):
                    head = half * V_HEADS + sub
                    mix_head = only_head(grad_mix, lane, V_DIM, sub)
                    place = (slot * HEADS + group * QK_HEADS + head) * length
                    score = score_ref[at(place, length), :]
                    squash = jax.nn.sigmoid(score)
                    weight = (score * squash * mask).astype(jnp.bfloat16)
                    slope = squash * (1.0 + score * (1.0 - squash)) * mask * SCALE
                    grad_score = (dot_nt(mix_head, values) * slope).astype(jnp.bfloat16)
                    grad_v += contract_rows(weight, mix_head)
                    grad_q += dot_nn(grad_score, only_head(keys, lane, QK_DIM, head))
                    grad_k += contract_rows(grad_score, only_head(queries, lane, QK_DIM, head))
                store_grad(rows, V_COLS + cols, LANES, grad_v)
            store_grad(rows, 2 * V_COLS + group * LANES, LANES, grad_q)
            store_grad(rows, 2 * V_COLS + Q_COLS + group * LANES, LANES, grad_k)
            return 0

        lax.fori_loop(0, GROUPS, one, 0)

        def norm_tile(index, _):
            gnorm[:, at(index * tile, tile)] = dot_nt(gpre_ref[rows, :], first_ref[at(index * tile, tile), :])
            return 0

        lax.fori_loop(0, width // tile, norm_tile, 0)
        value = input_ref[rows, :].astype(jnp.float32)
        center = value - jnp.mean(value, axis=-1, keepdims=True)
        rstd = lax.rsqrt(jnp.mean(center * center, axis=-1, keepdims=True) + EPSILON)
        unit = center * rstd
        grad = gnorm[...]
        mean_grad = jnp.mean(grad, axis=-1, keepdims=True)
        mean_unit = jnp.mean(grad * unit, axis=-1, keepdims=True)
        through = rstd * (grad - mean_grad - unit * mean_unit)
        result = (up_ref[rows, :].astype(jnp.float32) + through).astype(jnp.bfloat16)
        leaving[slot] = result
        gin_ref[rows, :] = result

        @pl.when(jnp.logical_not(is_first))
        def _():
            copy_of(slot).start()

    for slot in range(micro):

        @pl.when(jnp.logical_not(is_first))
        def _():
            copy_of(slot).wait_send()


def chain(top, inputs, activated, preact, scores, unit, rstd, mask, w_first, w_second, micro, length):
    tokens, width = inputs.shape
    return pl.pallas_call(
        functools.partial(chain_kernel, micro, length, lax.axis_size("pipe")),
        out_shape=(
            jax.ShapeDtypeStruct((tokens, width), jnp.bfloat16),
            jax.ShapeDtypeStruct(preact.shape, jnp.bfloat16),
            jax.ShapeDtypeStruct((tokens, width), jnp.bfloat16),
        ),
        in_specs=[VMEM] * 10,
        out_specs=(VMEM,) * 3,
        scratch_shapes=[
            pltpu.VMEM((micro, length, width), jnp.bfloat16),
            pltpu.VMEM((micro, length, width), jnp.bfloat16),
            pltpu.VMEM((length, V_COLS), jnp.float32),
            pltpu.VMEM((length, V_COLS), jnp.bfloat16),
            pltpu.VMEM((length, width), jnp.float32),
            pltpu.SemaphoreType.DMA((micro,)),
            pltpu.SemaphoreType.DMA((micro,)),
        ],
        compiler_params=pltpu.CompilerParams(
            collective_id=0, has_side_effects=True, vmem_limit_bytes=60 * 1024 * 1024
        ),
        name="chain",
    )(top, inputs, activated, preact, scores, unit, rstd, mask, w_first, w_second)


def add_into(target, left, right):
    step = 32

    def one(index, _):
        rows = pl.ds(pl.multiple_of(index * step, step), step)
        total = left[rows, :].astype(jnp.float32) + right[rows, :].astype(jnp.float32)
        target[rows, :] = total.astype(target.dtype)
        return 0

    lax.fori_loop(0, target.shape[0] // step, one, 0)


def scatter_kernel(line, part_a, part_b, out_a, out_b, *scratch):
    pairs = (
        (part_a, out_a) + scratch[0:4],
        (part_b, out_b) + scratch[4:8],
    )
    load_sem, pair_send, pair_recv, right_send, right_recv, left_send, left_recv = scratch[8:]
    rank = lax.axis_index("dp")
    spot, lane_of = rank // 2, rank % 2
    has_left, has_right = spot > 0, spot < line - 1
    partner = spot * 2 + 1 - lane_of
    right = jnp.minimum(spot + 1, line - 1) * 2 + lane_of
    left = jnp.maximum(spot - 1, 0) * 2 + lane_of

    barrier = pltpu.get_barrier_semaphore()
    pl.semaphore_signal(barrier, inc=1, device_id={"dp": partner}, device_id_type=MESH)

    @pl.when(has_left)
    def _():
        pl.semaphore_signal(barrier, inc=1, device_id={"dp": left}, device_id_type=MESH)

    @pl.when(has_right)
    def _():
        pl.semaphore_signal(barrier, inc=1, device_id={"dp": right}, device_id_type=MESH)

    pl.semaphore_wait(barrier, 1 + jnp.minimum(spot, 1) + jnp.minimum(line - 1 - spot, 1))

    def block_at(turn):
        near = jnp.minimum(spot, line - 1 - spot)
        ahead = line - 1 - 2 * near
        lone = jnp.where(spot <= line - 1 - spot, line - 1 - turn, turn)
        after = jnp.maximum(turn - ahead, 0)
        reach = near - after // 2
        both = jnp.where(after % 2 == 0, spot + reach, spot - reach)
        return jnp.where(turn < ahead, lone, both)

    def load_of(which, block):
        part, _, own, _, _, _ = pairs[which]
        return pltpu.make_async_copy(part.at[block, lane_of], own.at[block], load_sem.at[which, block])

    def pair_of(which, block):
        part, _, _, paired, _, _ = pairs[which]
        return pltpu.make_async_remote_copy(
            src_ref=part.at[block, 1 - lane_of], dst_ref=paired.at[block],
            send_sem=pair_send.at[which, block], recv_sem=pair_recv.at[which, block],
            device_id={"dp": partner}, device_id_type=MESH,
        )

    def flow_of(which, block, rightward, source):
        flow = pairs[which][4 if rightward else 5]
        sends, recvs = (right_send, right_recv) if rightward else (left_send, left_recv)
        return pltpu.make_async_remote_copy(
            src_ref=source.at[block], dst_ref=flow.at[block],
            send_sem=sends.at[which, block], recv_sem=recvs.at[which, block],
            device_id={"dp": right if rightward else left}, device_id_type=MESH,
        )

    def begin(turn, _):
        block = block_at(turn)
        for which in range(2):
            pair_of(which, block).start()
            load_of(which, block).start()
        return 0

    lax.fori_loop(0, line, begin, 0)

    def pass_on(turn, _):
        block = block_at(turn)
        for which in range(2):
            own, paired = pairs[which][2:4]
            load_of(which, block).wait()
            pair_of(which, block).wait_recv()
            add_into(own.at[block], own.at[block], paired.at[block])
            for rightward in (True, False):
                flow = pairs[which][4 if rightward else 5]
                fed = has_left if rightward else has_right
                wanted = block > spot if rightward else block < spot

                @pl.when(jnp.logical_and(wanted, fed))
                def _():
                    flow_of(which, block, rightward, flow).wait_recv()
                    add_into(flow.at[block], flow.at[block], own.at[block])
                    flow_of(which, block, rightward, flow).start()

                @pl.when(jnp.logical_and(wanted, jnp.logical_not(fed)))
                def _():
                    flow_of(which, block, rightward, own).start()
        return 0

    lax.fori_loop(0, line, pass_on, 0)

    for which in range(2):
        out, own = pairs[which][1:3]
        for rightward in (True, False):
            flow = pairs[which][4 if rightward else 5]

            @pl.when(has_left if rightward else has_right)
            def _():
                flow_of(which, spot, rightward, flow).wait_recv()

        @pl.when(jnp.logical_and(has_left, has_right))
        def _():
            add_into(out, own.at[spot], pairs[which][4].at[spot])
            add_into(out, out, pairs[which][5].at[spot])

        @pl.when(jnp.logical_and(has_left, jnp.logical_not(has_right)))
        def _():
            add_into(out, own.at[spot], pairs[which][4].at[spot])

        @pl.when(jnp.logical_and(has_right, jnp.logical_not(has_left)))
        def _():
            add_into(out, own.at[spot], pairs[which][5].at[spot])

    def finish(block, _):
        for which in range(2):
            pair_of(which, block).wait_send()
            for rightward in (True, False):

                @pl.when(block > spot if rightward else block < spot)
                def _():
                    flow_of(which, block, rightward, pairs[which][2]).wait_send()
        return 0

    lax.fori_loop(0, line, finish, 0)


def scatter_sums(part_a, part_b):
    devices = lax.axis_size("dp")
    line = devices // 2
    parts = [part.reshape(line, 2, part.shape[0] // devices, part.shape[1]) for part in (part_a, part_b)]
    scratch = []
    for part in parts:
        scratch += [pltpu.VMEM((line,) + part.shape[2:], part.dtype)] * 4
    scratch += [pltpu.SemaphoreType.DMA((2, line))] * 7
    return pl.pallas_call(
        functools.partial(scatter_kernel, line),
        out_shape=tuple(jax.ShapeDtypeStruct(part.shape[2:], jnp.float32) for part in parts),
        in_specs=[pl.BlockSpec(memory_space=pl.ANY)] * 2,
        out_specs=(VMEM,) * 2,
        scratch_shapes=scratch,
        compiler_params=pltpu.CompilerParams(
            collective_id=1, has_side_effects=True, vmem_limit_bytes=60 * 1024 * 1024
        ),
        name="scatter_sums",
    )(*parts)


def mask_of(segments):
    length = segments.shape[1]
    same = segments[:, :, None] == segments[:, None, :]
    positions = lax.broadcasted_iota(jnp.int32, (length, length), 0)
    columns = lax.broadcasted_iota(jnp.int32, (length, length), 1)
    counts = jnp.sum(same.astype(jnp.float32), axis=2, keepdims=True)
    allowed = jnp.logical_and(same, (columns <= positions)[None])
    return (allowed.astype(jnp.float32) / counts).reshape(-1, length)


def body(section_input, top_grad, w_in, w_out, segments):
    micro, length = segments.shape
    inputs = section_input[0]
    w_first = lax.all_gather(w_in[0], "dp", axis=0, tiled=True)
    w_mine, w_first = lax.optimization_barrier((w_out[0], w_first))
    w_second = lax.all_gather(w_mine, "dp", axis=0, tiled=True)
    mask = mask_of(segments)
    normed = norm_rows(inputs.astype(jnp.float32)).astype(jnp.bfloat16)
    preact = jnp.dot(normed, w_first, preferred_element_type=jnp.float32)
    activated = jax.nn.silu(preact).astype(jnp.bfloat16)
    scores, unit, rstd, gated = attend(activated, mask, micro, length)
    upstream, grad_preact, grads = chain(
        top_grad, inputs, activated, preact, scores, unit, rstd, mask, w_first, w_second, micro, length
    )
    part_out = contract_rows(gated, upstream).astype(jnp.bfloat16)
    part_in = contract_rows(normed, grad_preact).astype(jnp.bfloat16)
    grad_first, grad_out = scatter_sums(part_in, part_out)
    return (grads[None], grad_first[None], grad_out[None])


CORES = 2


class Place:
    def __init__(self):
        self.pipe, self.dp = lax.axis_index("pipe"), lax.axis_index("dp")
        self.x, self.core = self.pipe // CORES, self.pipe % CORES
        self.z, self.y = self.dp // CORES, self.dp % CORES

    def device(self, x=None, core=None, z=None, y=None, pipe=None):
        x = self.x if x is None else x
        core = self.core if core is None else core
        z = self.z if z is None else z
        y = self.y if y is None else y
        return {"pipe": x * CORES + core if pipe is None else pipe, "dp": z * CORES + y}


def signal(sem, device):
    pl.semaphore_signal(sem, inc=1, device_id=device, device_id_type=MESH)


def remote(src, dst, send, recv, device):
    return pltpu.make_async_remote_copy(
        src_ref=src, dst_ref=dst, send_sem=send, recv_sem=recv, device_id=device, device_id_type=MESH
    )


def either(local_if, local, far):
    pl.when(local_if)(local)
    pl.when(jnp.logical_not(local_if))(far)


def turned(index):
    return index % CORES * CORES + index // CORES


def layer_order(step, z, layers):
    return jnp.where(2 * z < layers, (z + step) % layers, (z + layers - step) % layers)


def work_kernel(
    micro, length, layers,
    input_ref, top_ref, w_in_ref, w_out_ref, home_mask_ref,
    out_first, out_second, out_grads,
    grads_ref, up_ref, gpre_ref, normed_ref, gated_ref,
    first, second, stage_first, stage_second, work_in, top, mask,
    unit_in, rstd_in, slope, act, weight, weight_slope, unit, rstd, mixed, landed, ggate, gnorm,
    swap_send, swap_recv, top_send, top_recv, pre_send, pre_recv, own_send, hop_send, to_core, to_x, to_y, came,
    chain_send, chain_recv, back_send, back_recv,
    *sums,
):
    me = Place()
    width = work_in.shape[1]
    tokens = micro * length
    section = me.z
    other_x, other_core, other_y = 1 - me.x, 1 - me.core, 1 - me.y
    at_home = me.pipe == me.z
    is_last, is_first = section == layers - 1, section == 0
    weights = (
        (w_in_ref, first, stage_first),
        (w_out_ref, second, stage_second),
    )
    sizes = [ref.shape[0] // 4 for ref, _, _ in weights]

    def quarter(which, block, half, core):
        size = sizes[which]
        start = pl.multiple_of(((block * 2 + half) * CORES + core) * size, size)
        return weights[which][1].at[pl.ds(start, size), :]

    def shard(which, half, core):
        size = sizes[which]
        start = pl.multiple_of((half * CORES + core) * size, size)
        return weights[which][0].at[pl.ds(start, size), :]

    def came_at(which, block, half, core):
        return came.at[which, (block * 2 + half) * CORES + core]

    barrier = pltpu.get_barrier_semaphore()
    def greet(index, _):
        pipe, layer = index // layers, index % layers

        @pl.when(jnp.logical_not(jnp.logical_and(pipe == me.pipe, layer == me.z)))
        def _():
            signal(barrier, {"pipe": pipe, "dp": layer * CORES + me.y})

        return 0

    lax.fori_loop(0, layers * layers, greet, 0)
    signal(barrier, me.device(y=other_y))
    pl.semaphore_wait(barrier, layers * layers)

    away = {"pipe": turned(me.z), "dp": me.pipe * CORES + me.y}
    back = {"pipe": me.z, "dp": turned(me.pipe) * CORES + me.y}
    stays = jnp.logical_and(at_home, turned(me.pipe) == me.pipe)
    swaps = ((input_ref, work_in), (home_mask_ref, mask))

    def swap_far(index):
        src, dst = swaps[index]
        return remote(src, dst, swap_send.at[index], swap_recv.at[index], away)

    def swap_near(index):
        src, dst = swaps[index]
        return pltpu.make_async_copy(src, dst, swap_recv.at[index])

    def swap_start():
        for index in range(2):
            either(stays, lambda: swap_near(index).start(), lambda: swap_far(index).start())

    def before(which, core):
        return remote(
            shard(which, other_x, core), weights[which][2].at[me.core],
            pre_send.at[which, core], pre_recv.at[which, me.core], me.device(x=other_x, core=core),
        )

    def own(which, core):
        return remote(
            shard(which, me.x, core), quarter(which, me.dp, me.x, core),
            own_send.at[which, core], came_at(which, me.dp, me.x, core), me.device(core=core, z=me.pipe),
        )

    def own_near(which, core):
        return pltpu.make_async_copy(
            shard(which, me.x, core), quarter(which, me.dp, me.x, core), came_at(which, me.dp, me.x, core)
        )

    def hop(which, source):
        return remote(
            weights[which][2].at[source], quarter(which, me.dp, me.x, me.core),
            hop_send.at[which, source], came_at(which, me.dp, me.x, me.core),
            me.device(z=other_x * CORES + source),
        )

    def hop_near(which, source):
        return pltpu.make_async_copy(
            weights[which][2].at[source], quarter(which, me.dp, me.x, me.core),
            came_at(which, me.dp, me.x, me.core),
        )

    def before_came(which, source):
        return remote(
            shard(which, other_x, me.core), weights[which][2].at[source],
            pre_send.at[which, source], pre_recv.at[which, source], me.device(x=other_x),
        )

    for which in range(2):
        for core in range(CORES):
            before(which, core).start()
        for core in range(CORES):
            near = jnp.logical_and(at_home, core == me.core)
            either(near, lambda: own_near(which, core).start(), lambda: own(which, core).start())

    for which in range(2):
        for source in range(CORES):
            before_came(which, source).wait_recv()
            either(
                other_x * CORES + source == me.z,
                lambda: hop_near(which, source).start(),
                lambda: hop(which, source).start(),
            )

    top_far = remote(top_ref, top, top_send, top_recv, me.device(z=layers - 1))
    top_near = pltpu.make_async_copy(top_ref, top, top_recv)
    has_top = me.z == turned(me.pipe)
    gives_top = jnp.logical_and(has_top, jnp.logical_not(is_last))
    keeps_top = jnp.logical_and(has_top, is_last)

    def top_start():
        pl.when(gives_top)(lambda: top_far.start())
        pl.when(keeps_top)(lambda: top_near.start())

    def send(which, block, half, core, sem, index, device):
        place = quarter(which, block, half, core)
        return remote(place, place, sem.at[which, index], came_at(which, block, half, core), device)

    def direct_block(step):
        return layer_order(step, me.z, layers) * CORES + me.y

    def core_copy(which, kind, step):
        block = direct_block(step)
        lane = kind // 2
        block = block if lane == 0 else block - me.y + other_y
        half = me.x if kind % 2 == 0 else other_x
        return send(which, block, half, me.core, to_core, kind * layers + step, me.device(core=other_core))

    def x_copy(which, step):
        return send(which, direct_block(step), me.x, me.core, to_x, step, me.device(x=other_x))

    def y_copy(which, kind, step):
        half = me.x if kind == 0 else other_x
        return send(which, direct_block(step), half, me.core, to_y, kind * layers + step, me.device(y=other_y))

    def arrived(which, block, half, core):
        place = quarter(which, block, half, core)
        return remote(
            place, place, to_core.at[which, 0], came_at(which, block, half, core), me.device(core=other_core)
        )

    def settled(which):
        for core in range(CORES):
            near = jnp.logical_and(at_home, core == me.core)
            pl.when(jnp.logical_not(near))(lambda: own(which, core).wait_send())
        for source in range(CORES):
            near = other_x * CORES + source == me.z
            pl.when(jnp.logical_not(near))(lambda: hop(which, source).wait_send())

    def direct_ready(which, step):
        block = direct_block(step)
        if step == 0:
            far = jnp.logical_and(me.x == me.z // CORES, me.core != me.z % CORES)
            place = quarter(which, block, me.x, me.core)
            either(
                jnp.logical_not(far),
                lambda: pltpu.make_async_copy(shard(which, 0, 0), place, came_at(which, block, me.x, me.core)).wait(),
                lambda: arrived(which, block, me.x, me.core).wait_recv(),
            )
        else:
            arrived(which, block, me.x, me.core).wait_recv()
        x_copy(which, step).start()
        y_copy(which, 0, step).start()
        core_copy(which, 0, step).start()

    def from_x(which, step):
        arrived(which, direct_block(step), other_x, me.core).wait_recv()
        y_copy(which, 1, step).start()
        core_copy(which, 1, step).start()

    def from_y(which, kind, step):
        block = direct_block(step) - me.y + other_y
        arrived(which, block, me.x if kind == 0 else other_x, me.core).wait_recv()
        core_copy(which, 2 + kind, step).start()

    def whole(which):
        def one(index, _):
            arrived(which, index // 2, index % 2, other_core).wait_recv()
            return 0

        lax.fori_loop(0, 2 * layers * CORES, one, 0)

    for step in range(layers + 1):
        if step == 3:
            for which in range(2):
                settled(which)
            swap_start()
        if step < layers:
            direct_ready(0, step)
        if step >= 1:
            from_x(0, step - 1)
            from_y(0, 0, step - 1)
        if step >= 2:
            from_y(0, 1, step - 2)
    top_start()
    for step in range(layers):
        direct_ready(1, step)
    for index in range(2):
        either(stays, lambda: swap_near(index).wait(), lambda: swap_far(index).wait_recv())
    norm_input(work_in, normed_ref, unit_in, rstd_in)
    from_y(0, 1, layers - 1)
    for step in range(layers):
        from_x(1, step)
    whole(0)
    tile = 2 * LANES

    def front(index, _):
        cols = at(index * tile, tile)
        value = dot_nn(normed_ref[...], first[:, cols])
        squash = jax.nn.sigmoid(value)
        act[:, cols] = (value * squash).astype(jnp.bfloat16)
        slope[:, cols] = squash * (1.0 + value * (1.0 - squash))
        return 0

    lax.fori_loop(0, slope.shape[1] // tile, front, 0)
    for step in range(layers):
        from_y(1, 0, step)
    attend_front(micro, length, act, mask, weight, weight_slope, unit, rstd, gated_ref, mixed)
    for step in range(layers):
        from_y(1, 1, step)
    whole(1)

    def copy_of(slot):
        return remote(
            grads_ref.at[pl.ds(slot * length, length), :], landed.at[slot], chain_send.at[slot], chain_recv.at[slot],
            me.device(z=jnp.maximum(me.z - 1, 0)),
        )

    def back_far(slot):
        rows = pl.ds(slot * length, length)
        return remote(grads_ref.at[rows, :], out_grads.at[rows, :], back_send.at[slot], back_recv.at[slot], back)

    def back_near(slot):
        rows = pl.ds(slot * length, length)
        return pltpu.make_async_copy(grads_ref.at[rows, :], out_grads.at[rows, :], back_recv.at[slot])

    def back_one(slot):
        either(stays, lambda: back_near(slot).start(), lambda: back_far(slot).start())

    def back_start():
        for slot in range(micro):
            back_one(slot)

    @pl.when(jnp.logical_and(is_last, jnp.logical_not(has_top)))
    def _():
        top_far.wait_recv()

    @pl.when(keeps_top)
    def _():
        top_near.wait()

    chain_steps(
        micro, length, is_first, is_last, copy_of, back_one,
        top, unit_in, rstd_in, act, slope, weight, weight_slope, unit, rstd, first, second,
        grads_ref, up_ref, gpre_ref, landed, ggate, gnorm,
    )

    for slot in range(micro):

        @pl.when(jnp.logical_not(is_first))
        def _():
            copy_of(slot).wait_send()

    for index in range(2):
        pl.when(jnp.logical_not(stays))(lambda: swap_far(index).wait_send())
    pl.when(gives_top)(lambda: top_far.wait_send())
    for which in range(2):
        for core in range(CORES):
            before(which, core).wait_send()

        def sent(step, _):
            x_copy(which, step).wait_send()
            for kind in range(2):
                y_copy(which, kind, step).wait_send()
            for kind in range(4):
                core_copy(which, kind, step).wait_send()
            return 0

        lax.fori_loop(0, layers, sent, 0)

    sum_weights(
        me, layers, normed_ref, gpre_ref, gated_ref, up_ref, out_first, out_second, first, second, *sums,
        lambda: pl.when(jnp.logical_not(is_first))(back_start),
    )
    for slot in range(micro):
        either(stays, lambda: back_near(slot).wait(), lambda: back_far(slot).wait())


def folded(value):
    total = value[:, :LANES]
    for start in range(LANES, value.shape[1], LANES):
        total = total + value[:, start : start + LANES]
    return total


def norm_input(work_in, normed_ref, unit_in, rstd_in):
    step = 64
    width = work_in.shape[1]

    def one(index, _):
        rows = pl.ds(pl.multiple_of(index * step, step), step)
        value = work_in[rows, :].astype(jnp.float32)
        center = value - jnp.mean(value, axis=-1, keepdims=True)
        rstd = lax.rsqrt(jnp.mean(center * center, axis=-1, keepdims=True) + EPSILON)
        unit = center * rstd
        unit_in[rows, :] = unit
        normed_ref[rows, :] = unit.astype(jnp.bfloat16)
        rstd_in[rows, :] = jnp.broadcast_to(rstd, (step, LANES))
        return 0

    lax.fori_loop(0, work_in.shape[0] // step, one, 0)


def attend_front(micro, length, act_ref, mask_ref, weight_ref, slope_ref, unit_ref, rstd_ref, gated_ref, mixed):
    lane = lax.broadcasted_iota(jnp.int32, (length, LANES), 1)

    def one(index, _):
        slot, group = index // GROUPS, index % GROUPS
        rows = at(slot * length, length)
        queries = act_ref[rows, at(2 * V_COLS + group * LANES, LANES)]
        keys = act_ref[rows, at(2 * V_COLS + Q_COLS + group * LANES, LANES)]
        mask = mask_ref[rows, :]
        for half in range(GROUP_V // LANES):
            cols = group * GROUP_V + half * LANES
            values = act_ref[rows, at(V_COLS + cols, LANES)]
            total = jnp.zeros((length, LANES), jnp.float32)
            for sub in range(V_HEADS):
                head = half * V_HEADS + sub
                score = dot_nt(only_head(queries, lane, QK_DIM, head), keys) * SCALE
                squash = jax.nn.sigmoid(score)
                place = at((index * QK_HEADS + head) * length, length)
                slope_ref[place, :] = squash * (1.0 + score * (1.0 - squash)) * (mask * SCALE)
                weight = (score * squash * mask).astype(jnp.bfloat16)
                weight_ref[place, :] = weight
                total += dot_nn(weight, only_head(values, lane, V_DIM, sub))
            mixed[rows, at(cols, LANES)] = total
        return 0

    lax.fori_loop(0, micro * GROUPS, one, 0)
    step = 64

    def finish(index, _):
        rows = pl.ds(pl.multiple_of(index * step, step), step)
        value = mixed[rows, :]
        center = value - jnp.mean(value, axis=-1, keepdims=True)
        rstd = lax.rsqrt(jnp.mean(center * center, axis=-1, keepdims=True) + EPSILON)
        unit = center * rstd
        unit_ref[rows, :] = unit
        rstd_ref[rows, :] = jnp.broadcast_to(rstd, (step, LANES))
        gated_ref[rows, :] = (unit * act_ref[rows, :V_COLS].astype(jnp.float32)).astype(jnp.bfloat16)
        return 0

    lax.fori_loop(0, micro * length // step, finish, 0)


def chain_steps(
    micro, length, is_first, is_last, copy_of, back_one,
    top_ref, unit_in, rstd_in, act_ref, slope_ref, weight_ref, weight_slope, unit_ref, rstd_ref, first_ref, second_ref,
    grads_ref, up_ref, gpre_ref, landed, ggate, gnorm,
):
    width = unit_in.shape[1]
    tile = 2 * LANES
    lane = lax.broadcasted_iota(jnp.int32, (length, LANES), 1)
    nothing = jnp.zeros((length, LANES), jnp.float32)

    def store_grad(rows, cols, size, value):
        rounded = value.astype(jnp.bfloat16).astype(jnp.float32)
        gpre_ref[rows, at(cols, size)] = (rounded * slope_ref[rows, at(cols, size)]).astype(jnp.bfloat16)

    for slot in range(micro):
        rows = pl.ds(slot * length, length)

        @pl.when(is_last)
        def _():
            up_ref[rows, :] = top_ref[rows, :]

        @pl.when(jnp.logical_not(is_last))
        def _():
            copy_of(slot).wait_recv()
            up_ref[rows, :] = landed[slot]

        def gate_tile(index, sums):
            cols = at(index * tile, tile)
            grad = dot_nt(up_ref[rows, :], second_ref[cols, :])
            unit = unit_ref[rows, cols]
            store_grad(rows, index * tile, tile, grad * unit)
            grad = grad * act_ref[rows, cols].astype(jnp.float32)
            ggate[:, cols] = grad
            return sums[0] + folded(grad), sums[1] + folded(grad * unit)

        sums = lax.fori_loop(0, V_COLS // tile, gate_tile, (nothing, nothing))
        mean_grad, mean_unit = [jnp.sum(part, axis=-1, keepdims=True) * (1.0 / V_COLS) for part in sums]
        rstd = rstd_ref[rows, :1]

        def one(group, _):
            queries = act_ref[rows, at(2 * V_COLS + group * LANES, LANES)]
            keys = act_ref[rows, at(2 * V_COLS + Q_COLS + group * LANES, LANES)]
            grad_q = jnp.zeros((length, LANES), jnp.float32)
            grad_k = jnp.zeros((length, LANES), jnp.float32)
            for half in range(GROUP_V // LANES):
                cols = group * GROUP_V + half * LANES
                values = act_ref[rows, at(V_COLS + cols, LANES)]
                spread = ggate[:, at(cols, LANES)] - mean_grad - unit_ref[rows, at(cols, LANES)] * mean_unit
                grad_mix = (rstd * spread).astype(jnp.bfloat16)
                grad_v = jnp.zeros((length, LANES), jnp.float32)
                for sub in range(V_HEADS):
                    head = half * V_HEADS + sub
                    mix_head = only_head(grad_mix, lane, V_DIM, sub)
                    place = at((slot * HEADS + group * QK_HEADS + head) * length, length)
                    grad_score = (dot_nt(mix_head, values) * weight_slope[place, :]).astype(jnp.bfloat16)
                    grad_v += contract_rows(weight_ref[place, :], mix_head)
                    grad_q += dot_nn(grad_score, only_head(keys, lane, QK_DIM, head))
                    grad_k += contract_rows(grad_score, only_head(queries, lane, QK_DIM, head))
                store_grad(rows, V_COLS + cols, LANES, grad_v)
            store_grad(rows, 2 * V_COLS + group * LANES, LANES, grad_q)
            store_grad(rows, 2 * V_COLS + Q_COLS + group * LANES, LANES, grad_k)
            return 0

        lax.fori_loop(0, GROUPS, one, 0)

        def norm_tile(index, sums):
            cols = at(index * tile, tile)
            grad = dot_nt(gpre_ref[rows, :], first_ref[cols, :])
            gnorm[:, cols] = grad
            return sums[0] + folded(grad), sums[1] + folded(grad * unit_in[rows, cols])

        sums = lax.fori_loop(0, width // tile, norm_tile, (nothing, nothing))
        mean_grad, mean_unit = [jnp.sum(part, axis=-1, keepdims=True) * (1.0 / width) for part in sums]
        rstd = rstd_in[rows, :1]

        def pass_tile(index, _):
            cols = at(index * tile, tile)
            through = rstd * (gnorm[:, cols] - mean_grad - unit_in[rows, cols] * mean_unit)
            grads_ref[rows, cols] = (up_ref[rows, cols].astype(jnp.float32) + through).astype(jnp.bfloat16)
            return 0

        lax.fori_loop(0, width // tile, pass_tile, 0)

        @pl.when(jnp.logical_not(is_first))
        def _():
            copy_of(slot).start()

        back_one(slot)


ANY = pl.BlockSpec(memory_space=pl.ANY)
LIMIT = 60 * 1024 * 1024


def work(inputs, top_grad, w_in, w_out, mask, micro, length):
    tokens, width = inputs.shape
    layers, blocks = lax.axis_size("pipe"), lax.axis_size("dp")
    columns = w_in.shape[1]
    quarters = [w.shape[0] // 4 for w in (w_in, w_out)]
    dma = pltpu.SemaphoreType.DMA
    return pl.pallas_call(
        functools.partial(work_kernel, micro, length, layers),
        out_shape=tuple(jax.ShapeDtypeStruct(a.shape, a.dtype) for a in (w_in, w_out, inputs)),
        in_specs=[ANY] * 5,
        out_specs=(ANY,) * 3,
        scratch_shapes=[
            pltpu.VMEM((tokens, width), jnp.bfloat16),
            pltpu.VMEM((tokens, width), jnp.bfloat16),
            pltpu.VMEM((tokens, columns), jnp.bfloat16),
            pltpu.VMEM((tokens, width), jnp.bfloat16),
            pltpu.VMEM((tokens, V_COLS), jnp.bfloat16),
            pltpu.VMEM((blocks * w_in.shape[0], columns), jnp.bfloat16),
            pltpu.VMEM((blocks * w_out.shape[0], width), jnp.bfloat16),
            pltpu.VMEM((CORES, quarters[0], columns), jnp.bfloat16),
            pltpu.VMEM((CORES, quarters[1], width), jnp.bfloat16),
            pltpu.VMEM((tokens, width), jnp.bfloat16),
            pltpu.VMEM((tokens, width), jnp.bfloat16),
            pltpu.VMEM((tokens, length), jnp.float32),
            pltpu.VMEM((tokens, width), jnp.float32),
            pltpu.VMEM((tokens, LANES), jnp.float32),
            pltpu.VMEM((tokens, columns), jnp.float32),
            pltpu.VMEM((tokens, columns), jnp.bfloat16),
            pltpu.VMEM((micro * HEADS * length, length), jnp.bfloat16),
            pltpu.VMEM((micro * HEADS * length, length), jnp.float32),
            pltpu.VMEM((tokens, V_COLS), jnp.float32),
            pltpu.VMEM((tokens, LANES), jnp.float32),
            pltpu.VMEM((tokens, V_COLS), jnp.float32),
            pltpu.VMEM((micro, length, width), jnp.bfloat16),
            pltpu.VMEM((length, V_COLS), jnp.float32),
            pltpu.VMEM((length, width), jnp.float32),
            dma((2,)), dma((2,)), dma, dma,
            dma((2, CORES)), dma((2, CORES)), dma((2, CORES)), dma((2, CORES)),
            dma((2, 4 * layers)), dma((2, layers)), dma((2, 2 * layers)), dma((2, 4 * blocks)),
            dma((micro,)), dma((micro,)), dma((micro,)), dma((micro,)),
        ]
        + [
            pltpu.VMEM((count, size, cols), jnp.bfloat16)
            for count in (2 * blocks, 2 * layers, layers)
            for size, cols in zip(quarters, (columns, width))
        ]
        + [dma((2, count)) for count in (2 * blocks, 2 * layers, layers, layers) for _ in range(2)],
        compiler_params=pltpu.CompilerParams(collective_id=2, has_side_effects=True, vmem_limit_bytes=LIMIT),
        name="work",
    )(inputs, top_grad, w_in, w_out, mask)


def add_rows(target, other):
    step = 16

    def one(index, _):
        rows = pl.ds(pl.multiple_of(index * step, step), step)
        total = target[rows, :].astype(jnp.float32) + other[rows, :].astype(jnp.float32)
        target[rows, :] = total.astype(target.dtype)
        return 0

    lax.fori_loop(0, target.shape[0] // step, one, 0)


def sum_weights(
    me, layers, normed_ref, gpre_ref, gated_ref, up_ref, out_first, out_second, first, second,
    core_first, core_second, early_first, early_second, late_first, late_second,
    core_send, core_recv, y_send, y_recv, x_send, x_recv, home_send, home_recv,
    between,
):
    other_x, other_core, other_y = 1 - me.x, 1 - me.core, 1 - me.y
    at_home = me.pipe == me.z
    sets = (
        (normed_ref, gpre_ref, out_first, first, core_first, early_first, late_first),
        (gated_ref, up_ref, out_second, second, core_second, early_second, late_second),
    )
    sizes = [s[2].shape[0] // 4 for s in sets]

    def quarter(which, block, half, core):
        size = sizes[which]
        start = pl.multiple_of(((block * 2 + half) * CORES + core) * size, size)
        return sets[which][3].at[pl.ds(start, size), :]

    def core_copy(which, block, half, mine):
        core = me.core if mine else other_core
        index = block * 2 + half
        return remote(
            quarter(which, block, half, core), sets[which][4].at[index],
            core_send.at[which, index], core_recv.at[which, index], me.device(core=other_core),
        )

    along_y = me.core == 0
    early_to = {
        "pipe": jnp.where(along_y, me.x, other_x) * CORES + me.core,
        "dp": me.z * CORES + jnp.where(along_y, other_y, me.y),
    }
    late_to = {
        "pipe": jnp.where(along_y, other_x, me.x) * CORES + me.core,
        "dp": me.z * CORES + jnp.where(along_y, me.y, other_y),
    }

    def near_unit(row, index, far):
        lane_of = jnp.where(along_y, other_y if far else me.y, index)
        half = jnp.where(along_y, index, other_x if far else me.x)
        return row * CORES + lane_of, half

    def early_copy(which, row, index):
        block, half = near_unit(row, index, True)
        slot = row * 2 + index
        return remote(
            quarter(which, block, half, me.core), sets[which][5].at[slot],
            y_send.at[which, slot], y_recv.at[which, slot], early_to,
        )

    def late_copy(which, row):
        block, half = near_unit(row, jnp.where(along_y, other_x, other_y), False)
        return remote(
            quarter(which, block, half, me.core), sets[which][6].at[row],
            x_send.at[which, row], x_recv.at[which, row], late_to,
        )

    def home_rows(which, half, core):
        size = sizes[which]
        return sets[which][2].at[pl.ds(pl.multiple_of((half * CORES + core) * size, size), size), :]

    def home_copy(which, row):
        return remote(
            quarter(which, row * CORES + me.y, me.x, me.core), home_rows(which, me.x, me.core),
            home_send.at[which, row], home_recv.at[which, me.x * CORES + me.core],
            {"pipe": me.z, "dp": row * CORES + me.y},
        )

    def home_near(which):
        return pltpu.make_async_copy(
            quarter(which, me.dp, me.x, me.core), home_rows(which, me.x, me.core),
            home_recv.at[which, me.x * CORES + me.core],
        )

    def row_at(step):
        return layer_order(layers - 1 - step, me.z, layers)

    def product(row):
        for which in (1, 0):
            left, right, _, whole = sets[which][:4]
            size = 8 * sizes[which]
            tile = 2 * LANES
            place = pl.ds(pl.multiple_of(row * size, size), size)

            def one(index, _):
                cols = at(index * tile, tile)
                whole[place, cols] = contract_rows(left[:, place], right[:, cols]).astype(whole.dtype)
                return 0

            lax.fori_loop(0, right.shape[1] // tile, one, 0)
            for lane_of in range(CORES):
                for half in range(2):
                    core_copy(which, row * CORES + lane_of, half, False).start()

    def fold_core(row, far):
        for which in (1, 0):

            def one(index, _):
                block, half = near_unit(row, index, far)
                core_copy(which, block, half, True).wait_recv()
                add_rows(quarter(which, block, half, me.core), sets[which][4].at[block * 2 + half])
                return 0

            lax.fori_loop(0, 2, one, 0)

    def start_early(row):
        for which in (1, 0):
            for index in range(2):
                early_copy(which, row, index).start()

    def fold_early(row):
        for which in (1, 0):

            def one(turn, _):
                mine = jnp.where(along_y, me.x, me.y)
                index = jnp.where(turn == 0, 1 - mine, mine)
                block, half = near_unit(row, index, False)
                early_copy(which, row, index).wait_recv()
                add_rows(quarter(which, block, half, me.core), sets[which][5].at[row * 2 + index])
                pl.when(turn == 0)(lambda: late_copy(which, row).start())
                return 0

            lax.fori_loop(0, 2, one, 0)

    def fold_late(row):
        for which in (1, 0):
            late_copy(which, row).wait_recv()
            add_rows(quarter(which, row * CORES + me.y, me.x, me.core), sets[which][6].at[row])
            near = jnp.logical_and(at_home, row == me.z)
            either(near, lambda: home_near(which).start(), lambda: home_copy(which, row).start())

    steps = [row_at(step) for step in range(layers)]
    ahead = 2
    for step in range(layers + 1):
        if step < layers:
            product(steps[step])
        if step >= 1:
            fold_core(steps[step - 1], True)
            if step <= ahead:
                start_early(steps[step - 1])
            fold_core(steps[step - 1], False)
    for step in range(layers + 1):
        if step < layers:
            if step + ahead < layers:
                for which in (1, 0):
                    early_copy(which, steps[step], 0).wait_send()
                    early_copy(which, steps[step], 1).wait_send()
                start_early(steps[step + ahead])
            fold_early(steps[step])
        if step >= 1:
            fold_late(steps[step - 1])
    for which in range(2):
        for pipe in range(layers):
            place = home_rows(which, pipe // CORES, pipe % CORES)
            near = jnp.logical_and(at_home, pipe == me.pipe)
            either(
                near,
                lambda: home_near(which).wait(),
                lambda: remote(
                    place, place, home_send.at[which, 0], home_recv.at[which, pipe], me.device(core=other_core)
                ).wait_recv(),
            )

        def sent(row, _):
            for half in range(2):
                for lane_of in range(2):
                    core_copy(which, row * CORES + lane_of, half, False).wait_send()
            near = jnp.logical_and(at_home, row == me.z)
            pl.when(jnp.logical_not(near))(lambda: home_copy(which, row).wait_send())
            return 0

        lax.fori_loop(0, layers, sent, 0)
        for step in range(layers):
            if step + ahead >= layers:
                early_copy(which, steps[step], 0).wait_send()
                early_copy(which, steps[step], 1).wait_send()
            late_copy(which, steps[step]).wait_send()


def layered_body(section_input, top_grad, w_in, w_out, segments):
    micro, length = segments.shape
    mask = mask_of(segments)
    grad_first, grad_out, grads = work(section_input[0], top_grad, w_in[0], w_out[0], mask, micro, length)
    return (grads[None], grad_first.astype(jnp.float32)[None], grad_out.astype(jnp.float32)[None])


def solution(mesh):
    layered = mesh.shape["pipe"] == CORES * 2 and mesh.shape["dp"] == CORES * mesh.shape["pipe"]
    return jax.shard_map(
        layered_body if layered else body,
        mesh=mesh,
        in_specs=(
            P("pipe", "dp", None),
            P("dp", None),
            P("pipe", "dp", None),
            P("pipe", "dp", None),
            P("dp", None),
        ),
        out_specs=(P("pipe", "dp", None), P("pipe", "dp", None), P("pipe", "dp", None)),
        check_vma=False,
    )
```
